128 devices in a mesh: patch: 16 (over y, z), col: 8 (over x, core).
Axes of the slice: x: 4, y: 4, z: 4, core: 2. Of those that a mesh axis runs over, the one named last changes fastest.
Arguments:
- contributions: float32 [8192, 128, 128], P(('patch', 'col')), may hold values from -0.21875 to 0.21875
- targets: int32 [8192, 2], P(('patch', 'col')), may hold values from 0 to 127, as said below
- counts: int32 [128], P(('patch', 'col')), may hold values from 48 to 64, as said below
- pivot: int32 [128], replicated, may hold values from 0 to 127, as said below
- fill_draw: int32 [128, 128], replicated, may hold values 0 or 1
- regular: float32 [16384], P('patch'), may hold values from 1.5 to 3
Outputs:
- factor_panels: float32 [16384, 1024], P('patch')
- schur: float32 [16, 8, 16384, 128], P(None, 'col', 'patch')
The draws below stay inside these ranges and needn't reach their ends.
Inputs may be any that keep to these rules, and one draw needn't show every extreme that they name: `targets`: under pivot, each contribution's pair lands at position (r, c) with r >= c after ordering; its owner is device (r // 8) * 8 + c % 8 of patch+col. Every slot of one device, live or not, has a different owner, so a device sends at most one block to each owner; one owner receives a block from every device. `pivot`: A permutation: each position once. `counts`: some device has all its slots live.
All inputs are finite; a program needn't handle non-finite values.
Results may differ from the reference program's by a relative error of at most 0.0001.
Values sent between devices are 32-bit elements; how exact they have to be, the bound alone decides.
A program may use at most 256 MiB of HBM per device.

```python
import math
import jax
import jax.numpy as jnp
from jax import lax

B = 128
K = 8
RB_DEV = 8
NB = 128
E_DEV = 64
N_PATCH = 16
N_COL = 8


def route_tables(key):
    ndevice = N_PATCH * N_COL
    order = jax.random.permutation(jax.random.fold_in(key, 11), NB).astype(jnp.int32)
    inverse = jnp.zeros((NB,), jnp.int32).at[order].set(jnp.arange(NB, dtype=jnp.int32))
    owners = jnp.arange(ndevice, dtype=jnp.int32)
    owner_patch = owners // N_COL
    owner_col = owners % N_COL
    owner_rows = owner_patch[:, None] * RB_DEV + jnp.arange(RB_DEV, dtype=jnp.int32)[None, :]
    row_spans = jnp.where(owner_rows >= owner_col[:, None], (owner_rows - owner_col[:, None]) // N_COL + 1, 0)
    lower_count = jnp.sum(row_spans, 1).astype(jnp.int32)
    spread = NB * (NB + 1) * 64 // ndevice
    first_hot = N_PATCH // 2 * N_COL
    hot = first_hot + jax.random.randint(jax.random.fold_in(key, 12), (), 0, ndevice - first_hot)
    popular = lower_count * 64
    popular = jnp.where(owners == hot, 64 * NB * RB_DEV + 2 * spread, popular)
    noise = jax.random.randint(jax.random.fold_in(key, 14), (ndevice, ndevice), 0, spread)
    score = (popular[None, :] + noise) * ndevice + owners[None, :]
    ignored, dest = lax.top_k(score, E_DEV)
    dest_patch = dest // N_COL
    dest_col = dest % N_COL
    low_row = jnp.where(dest_patch == 0, dest_col, 0)
    row_local = jax.random.randint(jax.random.fold_in(key, 15), dest.shape, low_row, RB_DEV)
    grow = dest_patch * RB_DEV + row_local
    span = (grow - dest_col) // N_COL + 1
    gcol = dest_col + N_COL * jax.random.randint(jax.random.fold_in(key, 16), dest.shape, 0, span)
    swapped = jax.random.randint(jax.random.fold_in(key, 17), dest.shape, 0, 2)
    first = jnp.where(swapped == 1, gcol, grow)
    second = jnp.where(swapped == 1, grow, gcol)
    pairs = jnp.stack([inverse[first], inverse[second]], -1).reshape(ndevice * E_DEV, 2)
    return (order, pairs.astype(jnp.int32))


def draw_pivot(key, part):
    order, pairs = route_tables(key)
    return order


def draw_targets(key, part):
    order, pairs = route_tables(key)
    return pairs


def draw_counts(key, part):
    ndevice = N_PATCH * N_COL
    hot = jax.random.randint(jax.random.fold_in(key, 21), (), 0, ndevice)
    base = jax.random.randint(jax.random.fold_in(key, 22), (ndevice,), 3 * E_DEV // 4, E_DEV + 1)
    return jnp.where(jnp.arange(ndevice) == hot, E_DEV, base).astype(jnp.int32)


def place_ends(values, rng, smallest, top_value):
    extent = values.shape
    index_at = [jax.random.randint(jax.random.fold_in(rng, axis), (), 0, extent[axis]) for axis in range(len(extent))]
    values = values.at[tuple(index_at)].set(smallest)
    longest = extent.index(max(extent))
    index_at[longest] = (index_at[longest] + 1) % extent[longest]
    return values.at[tuple(index_at)].set(top_value)


def shard_levels(stream_key, shape, cuts, least, largest):
    loudness = 1.0
    for position, shards_of in cuts:
        heights = jax.random.uniform(jax.random.fold_in(jax.random.fold_in(stream_key, 6), position), (shards_of,), jnp.float32, least / len(cuts), largest / len(cuts))
        loudness = loudness * jnp.repeat(jnp.exp(heights), shape[position] // shards_of).reshape((-1,) + (1,) * (len(shape) - 1 - position))
    return loudness


def bell_draw(own_key, dims, scale, reach, pieces=(), kind=jnp.bfloat16):
    factor_of = shard_levels(own_key, dims, pieces, -0.22, 0.18) if pieces else 1.0
    entries = jax.random.normal(own_key, dims, jnp.float32) * scale * factor_of
    return jnp.minimum(jnp.maximum(entries, -reach), reach).astype(kind)


def setup_inputs(seed: int = 0) -> dict:
    keys = jax.random.split(jax.random.key(seed), 7)
    return {
        "contributions": bell_draw(keys[0], (N_PATCH * N_COL * E_DEV, B, B), (0.45 / (K * B) ** 0.5), 0.21875, ((0, 128),), jnp.float32),
        "targets": draw_targets(jax.random.fold_in(keys[6], 71), 0),
        "counts": draw_counts(jax.random.fold_in(keys[6], 71), 0),
        "pivot": draw_pivot(jax.random.fold_in(keys[6], 71), 0),
        "fill_draw": place_ends((jax.random.randint(keys[4], (NB, NB), 0, 2) < 1).astype(jnp.int32), jax.random.fold_in(keys[4], 1), 0, 1),
        "regular": jnp.clip(jnp.exp(math.log(3.0) - 0.6931472 * jax.random.uniform(keys[5], (NB * B,), jnp.float32) ** shard_levels(keys[5], (NB * B,), ((0, 16),), -0.2, 0.2)), 1.5, 3.0),
    }


HIGH = lax.Precision.HIGHEST

def reference(contributions, targets, counts, pivot, fill_draw, regular):
    width = contributions.shape[1]
    nblock = pivot.shape[0]
    slots = contributions.shape[0]
    slot_index = jnp.arange(slots, dtype=jnp.int32)
    device_of = slot_index // E_DEV
    live = slot_index % E_DEV < counts[device_of]
    pos_first = pivot[targets[:, 0]]
    pos_second = pivot[targets[:, 1]]
    upper_pos = jnp.maximum(pos_first, pos_second)
    lower_pos = jnp.minimum(pos_first, pos_second)
    placed = jnp.where((pos_first < pos_second)[:, None, None], jnp.swapaxes(contributions, 1, 2), contributions)
    placed = jnp.where(live[:, None, None], placed, jnp.zeros_like(placed))
    matrix = jnp.zeros((nblock, nblock, width, width), jnp.float32).at[upper_pos, lower_pos].add(placed)
    index = jnp.arange(nblock, dtype=jnp.int32)
    blocks = matrix[index, index]
    shift = jnp.eye(width, dtype=jnp.float32)[None] * regular.reshape(nblock, 1, width)
    blocks = 0.5 * (blocks + jnp.swapaxes(blocks, 1, 2)) + shift
    matrix = matrix.at[index, index].set(blocks)
    drawn = fill_draw.astype(jnp.float32)
    pattern = jnp.maximum(jnp.maximum(drawn, drawn.T), jnp.eye(nblock, dtype=jnp.float32))
    factor = []
    for kblock in range(K):
        column = matrix[:, kblock]
        for earlier in range(kblock):
            term = jnp.einsum('iab,cb->iac', factor[earlier], factor[earlier][kblock], precision=HIGH)
            column = column - pattern[:, kblock][:, None, None] * term
        chol = jnp.linalg.cholesky(column[kblock])
        stacked = column.transpose(2, 0, 1).reshape(width, nblock * width)
        solved = lax.linalg.triangular_solve(chol, stacked, left_side=True, lower=True)
        rows_l = solved.reshape(width, nblock, width).transpose(1, 2, 0)
        rows_l = jnp.where((index > kblock)[:, None, None], rows_l, jnp.where((index == kblock)[:, None, None], chol[None], jnp.zeros_like(rows_l)))
        factor.append(rows_l)
    stack = jnp.stack(factor, 1)
    update = jnp.einsum('ipab,jpcb->ijac', stack, stack, precision=HIGH)
    keep = (index[:, None] >= index[None, :]) & (index >= K)[None, :]
    schur_full = jnp.where(keep[:, :, None, None], matrix - pattern[:, :, None, None] * update, 0.0)
    colslots = nblock // N_COL
    schur = schur_full.reshape(nblock, colslots, N_COL, width, width).transpose(1, 2, 0, 3, 4)
    schur = schur.reshape(colslots, N_COL, nblock * width, width)
    factor_panels = stack.transpose(0, 2, 1, 3).reshape(nblock * width, K * width)
    return (factor_panels, schur)
```

```python
import functools

import jax
import jax.numpy as jnp
from jax import lax
from jax.experimental import pallas as pl
from jax.experimental.pallas import tpu as pltpu
from jax.sharding import PartitionSpec as P

K = 8
HIGH = lax.Precision.HIGHEST
F32 = jnp.float32
BF16 = jnp.bfloat16
VMEM_BYTES = 60 * 1024 * 1024
SMEM = pl.BlockSpec(memory_space=pltpu.SMEM)
WHOLE = pl.BlockSpec(memory_space=pltpu.VMEM)
NT = (((1,), (1,)), ((), ()))
TN = (((0,), (0,)), ((), ()))


def params(**more):
    return pltpu.CompilerParams(vmem_limit_bytes=VMEM_BYTES, **more)


def dot_nt(a, b):
    return lax.dot_general(a, b, NT, precision=HIGH, preferred_element_type=F32)


def eye_mask(n):
    return lax.broadcasted_iota(jnp.int32, (n, n), 0) == lax.broadcasted_iota(jnp.int32, (n, n), 1)


def pack_kernel(per, meta, x_ref, o_ref):
    first = pl.program_id(0) * per
    width = x_ref.shape[2]

    def step(t, carry):
        slot = meta[0, first + t]
        turned = meta[1, first + t]

        @pl.when((slot >= 0) & (turned == 0))
        def _():
            o_ref[t, 0:width, :] = x_ref[slot]

        @pl.when((slot >= 0) & (turned == 1))
        def _():
            o_ref[t, 0:width, :] = x_ref[slot].T

        o_ref[t, width:, :] = jnp.full((8, width), meta[2, first + t].astype(F32), F32)
        return carry

    lax.fori_loop(0, per, step, 0)


def pack(meta, contributions, ndevice, per=16):
    slots, width, _ = contributions.shape
    return pl.pallas_call(
        functools.partial(pack_kernel, per),
        grid=(ndevice // per,),
        in_specs=[SMEM, pl.BlockSpec((slots, width, width), lambda g: (0, 0, 0), pipeline_mode=pl.Buffered(1))],
        out_specs=pl.BlockSpec((per, width + 8, width), lambda g: (g, 0, 0)),
        out_shape=jax.ShapeDtypeStruct((ndevice, width + 8, width), F32),
        compiler_params=params(),
        name="pack",
    )(meta, contributions)


def place_kernel(per, last, codes, diag, x_ref, reg_ref, o_ref):
    g = pl.program_id(0)
    width = x_ref.shape[2]

    @pl.when(g == 0)
    def _():
        def clear(q, carry):
            o_ref[q] = jnp.zeros((width, width), F32)
            return carry

        lax.fori_loop(0, o_ref.shape[0], clear, 0)

    def step(t, carry):
        code = codes[g * per + t]

        @pl.when(code >= 0)
        def _():
            o_ref[code] += x_ref[t, 0:width, :]

        return carry

    lax.fori_loop(0, per, step, 0)

    @pl.when(g == last)
    def _():
        block = o_ref[diag[0]]
        o_ref[diag[0]] = 0.5 * (block + block.T) + jnp.where(eye_mask(width), reg_ref[...], 0.0)


def place(codes, diag, got, reg, per=16):
    ndevice, high, width = got.shape
    places = 128
    return pl.pallas_call(
        functools.partial(place_kernel, per, ndevice // per - 1),
        grid=(ndevice // per,),
        in_specs=[SMEM, SMEM, pl.BlockSpec((per, high, width), lambda g: (g, 0, 0)), pl.BlockSpec((1, width), lambda g: (0, 0))],
        out_specs=pl.BlockSpec((places, width, width), lambda g: (0, 0, 0), pipeline_mode=pl.Buffered(1)),
        out_shape=jax.ShapeDtypeStruct((places, width, width), F32),
        compiler_params=params(),
        name="place",
    )(codes, diag, got, reg)


def split3(a):
    one = a.astype(BF16).astype(F32)
    rest = a - one
    two = rest.astype(BF16).astype(F32)
    return one, two, rest - two


def chol_inverse(w_ref, lt_ref):
    width = w_ref.shape[0]
    sub = lax.broadcasted_iota(jnp.int32, (8, width), 0)
    lane = lax.broadcasted_iota(jnp.int32, (8, width), 1)
    for base in range(0, width, 8):
        both = w_ref[base : base + 8, :]
        rows = both[:, :width]
        unit = both[:, width:]
        cols = [jnp.broadcast_to(rows[:, base + j : base + j + 1], (8, width)) for j in range(8)]
        scale = jnp.zeros((8, width), F32)
        for j in range(8):
            root = lax.rsqrt(cols[j][j : j + 1, :])
            lower = cols[j] * root
            for i in range(j + 1, 8):
                cols[i] = cols[i] - lower * lower[i : i + 1, :]
            below = jnp.where(sub > j, lower, 0.0)
            rows = rows - below * (rows[j : j + 1, :] * root)
            unit = unit - below * (unit[j : j + 1, :] * root)
            scale = jnp.where(sub == j, root, scale)
        upper = jnp.where(lane >= sub + base, rows * scale, 0.0)
        unit = unit * scale
        lt_ref[base : base + 8, :] = upper
        w_ref[base : base + 8, width:] = unit
        if base + 8 < width:
            u1, u2, u3 = split3(upper)
            v1, v2, v3 = split3(unit)
            left = jnp.concatenate([u1, u1, u2, u2, u1, u3], 0).astype(BF16)
            w1, w2, w3 = (jnp.concatenate([a, b], 1) for a, b in ((u1, v1), (u2, v2), (u3, v3)))
            right = jnp.concatenate([w1, w2, w1, w2, w3, w1], 0).astype(BF16)
            change = lax.dot_general(left, right, TN, preferred_element_type=F32)
            w_ref[base + 8 :, :] -= change[base + 8 :, :]


def head_kernel(fill, head_ref, lh_ref, li_ref, w_ref, lt_ref):
    width = head_ref.shape[1]
    eye = jnp.where(eye_mask(width), 1.0, 0.0).astype(F32)
    n = 0
    for c in range(K):
        for r in range(K):
            at = slice(r * width, (r + 1) * width)
            if r < c:
                lh_ref[c, at, :] = jnp.zeros((width, width), F32)
                continue
            block = head_ref[n]
            n += 1
            lh_ref[c, at, :] = 0.5 * (block + block.T) if r == c else block

    def step(k, carry):
        w_ref[:, :width] = lh_ref[k, pl.ds(pl.multiple_of(k * width, width), width), :]
        w_ref[:, width:] = eye
        chol_inverse(w_ref, lt_ref)
        li_ref[k] = w_ref[:, width:]
        lh_ref[k, pl.ds(pl.multiple_of(k * width, width), width), :] = lt_ref[...].T
        for s in range(K - 1):

            @pl.when(k == s)
            def _(s=s):
                below = slice((s + 1) * width, K * width)
                solved = dot_nt(lh_ref[s, below, :], li_ref[s])
                lh_ref[s, below, :] = solved
                for j in range(s + 1, K):
                    part = solved[(j - s - 1) * width :]
                    change = dot_nt(part, part[:width])
                    for i in range(j, K):
                        at = slice(i * width, (i + 1) * width)
                        lh_ref[j, at, :] -= fill[i, j] * change[(i - j) * width : (i - j + 1) * width]

        return carry

    lax.fori_loop(0, K, step, 0)


def factor_head(fill, head):
    width = head.shape[1]
    return pl.pallas_call(
        head_kernel,
        in_specs=[SMEM, WHOLE],
        out_specs=[WHOLE, WHOLE],
        out_shape=[
            jax.ShapeDtypeStruct((K, K * width, width), F32),
            jax.ShapeDtypeStruct((K, width, width), F32),
        ],
        scratch_shapes=[pltpu.VMEM((width, 2 * width), F32), pltpu.VMEM((width, width), F32)],
        compiler_params=params(),
        name="factor_head",
    )(fill, head)


def solve_kernel(fill, which, a_ref, lh_ref, li_ref, o_ref):
    width = a_ref.shape[1]
    row = which[0]
    work = [a_ref[k] for k in range(K)]
    for k in range(K):
        solved = dot_nt(work[k], li_ref[k])
        own = lh_ref[k, k * width : (k + 1) * width, :]
        solved = jnp.where(row > k, solved, jnp.where(row == k, own, 0.0))
        o_ref[:, k * width : (k + 1) * width] = solved
        if k + 1 < K:
            change = dot_nt(solved, lh_ref[k, (k + 1) * width :, :])
            for j in range(k + 1, K):
                work[j] = work[j] - fill[0, j] * change[:, (j - k - 1) * width : (j - k) * width]


def solve(fill, which, arow, lh, li):
    width = arow.shape[1]
    return pl.pallas_call(
        solve_kernel,
        in_specs=[SMEM, SMEM, WHOLE, WHOLE, WHOLE],
        out_specs=WHOLE,
        out_shape=jax.ShapeDtypeStruct((width, K * width), F32),
        compiler_params=params(),
        name="solve",
    )(fill, which, arow, lh, li)


def schur_kernel(pair, fill, keep, a_ref, rows_ref, cols_ref, o_ref, hi_ref, lo_ref):
    g = pl.program_id(0)
    width = a_ref.shape[2]
    nrow = a_ref.shape[1] // width

    @pl.when(g == 0)
    def _():
        def split(r, carry):
            at = pl.ds(pl.multiple_of(r * width, width), width)
            rows = rows_ref[at, :]
            hi = rows.astype(BF16)
            hi_ref[at, :] = hi
            lo_ref[at, :] = (rows - hi.astype(F32)).astype(BF16)
            return carry

        lax.fori_loop(0, nrow, split, 0)

    cols = cols_ref[...].reshape(pair * width, cols_ref.shape[2])
    col_hi = cols.astype(BF16)
    col_lo = (cols - col_hi.astype(F32)).astype(BF16)

    def step(r, carry):
        at = pl.ds(pl.multiple_of(r * width, width), width)
        some = keep[r, g * pair]
        for q in range(1, pair):
            some = some + keep[r, g * pair + q]

        @pl.when(some > 0)
        def _():
            hi = hi_ref[at, :]
            product = lax.dot_general(hi, col_hi, NT, preferred_element_type=F32)
            product += lax.dot_general(hi, col_lo, NT, preferred_element_type=F32)
            product += lax.dot_general(lo_ref[at, :], col_hi, NT, preferred_element_type=F32)
            for q in range(pair):
                value = a_ref[q, at, :] - fill[r, g * pair + q] * product[:, q * width : (q + 1) * width]
                o_ref[q, at, :] = jnp.where(keep[r, g * pair + q] > 0, value, 0.0)

        @pl.when(some == 0)
        def _():
            for q in range(pair):
                o_ref[q, at, :] = jnp.zeros((width, width), F32)

        return carry

    lax.fori_loop(0, nrow, step, 0)


def trailing(fill, keep, matrix, rows_l, cols_l, pair=2):
    colslots, tall, width = matrix.shape
    depth = rows_l.shape[1]
    return pl.pallas_call(
        functools.partial(schur_kernel, pair),
        grid=(colslots // pair,),
        in_specs=[
            SMEM,
            SMEM,
            pl.BlockSpec((pair, tall, width), lambda g: (g, 0, 0)),
            pl.BlockSpec((tall, depth), lambda g: (0, 0), pipeline_mode=pl.Buffered(1)),
            pl.BlockSpec((pair, width, depth), lambda g: (g, 0, 0)),
        ],
        out_specs=pl.BlockSpec((pair, tall, width), lambda g: (g, 0, 0)),
        out_shape=jax.ShapeDtypeStruct((colslots, tall, width), F32),
        scratch_shapes=[pltpu.VMEM((tall, depth), BF16), pltpu.VMEM((tall, depth), BF16)],
        compiler_params=params(),
        name="trailing",
    )(fill, keep, matrix, rows_l, cols_l)


def route(targets, counts, pivot, rowblk, ncol, ndevice):
    slots = targets.shape[0]
    pos_first = pivot[targets[:, 0]]
    pos_second = pivot[targets[:, 1]]
    upper_pos = jnp.maximum(pos_first, pos_second)
    lower_pos = jnp.minimum(pos_first, pos_second)
    number = jnp.arange(slots, dtype=jnp.int32)
    live = number < counts[0]
    owner = upper_pos // rowblk * ncol + lower_pos % ncol
    select = (owner[:, None] == jnp.arange(ndevice, dtype=jnp.int32)[None, :]) & live[:, None]
    turned = (pos_first < pos_second).astype(jnp.int32)
    code = lower_pos // ncol * rowblk + upper_pos % rowblk
    table = jnp.stack([number, turned, code], 0)
    return jnp.max(jnp.where(select[None], table[:, :, None], -1), 1)


def body(contributions, targets, counts, pivot, fill_draw, regular):
    width = contributions.shape[1]
    npatch = lax.axis_size("patch")
    ncol = lax.axis_size("col")
    ndevice = npatch * ncol
    nblock = pivot.shape[0]
    rowblk = regular.shape[0] // width
    colslots = nblock // ncol
    patch_id = lax.axis_index("patch")
    col_id = lax.axis_index("col")

    meta = route(targets, counts, pivot, rowblk, ncol, ndevice)
    outgoing = pack(meta, contributions, ndevice)

    reg = lax.dynamic_slice_in_dim(regular, col_id * width, width, 0)
    codes = meta[2, :K]
    mine = jnp.where(patch_id == 0, jnp.eye(width, dtype=F32) * reg[None, :], 0.0)
    parts = []
    for c in range(K):
        for r in range(c, K):
            part = jnp.where(codes[c] == r, outgoing[c, :width], 0.0)
            if r == c:
                part = part + jnp.where(col_id == c, mine, 0.0)
            parts.append(part)
    head = lax.psum(jnp.stack(parts, 0), ("patch", "col"))

    got = lax.all_to_all(outgoing, ("patch", "col"), split_axis=0, concat_axis=0, tiled=True)

    drawn = fill_draw.astype(F32)
    pattern = jnp.maximum(jnp.maximum(drawn, drawn.T), jnp.eye(nblock, dtype=F32))
    lh, li = factor_head(pattern[:K, :K], head)

    diag = (patch_id * rowblk + col_id).astype(jnp.int32)[None]
    matrix = place(got[:, width, 0].astype(jnp.int32), diag, got, reg[None, :])

    arow = lax.all_to_all(matrix[:rowblk], "col", split_axis=0, concat_axis=0, tiled=True)
    row = patch_id * rowblk + col_id
    row_fill = lax.dynamic_slice(pattern, (row, 0), (1, K))
    lrow = solve(row_fill, row.astype(jnp.int32)[None], arow, lh, li)
    rows_l = lax.all_gather(lrow, "col", axis=0, tiled=True)
    cols_l = lax.all_gather(lrow, "patch", axis=0, tiled=False)

    grow = patch_id * rowblk + jnp.arange(rowblk, dtype=jnp.int32)
    gcol = jnp.arange(colslots, dtype=jnp.int32) * ncol + col_id
    keep = ((grow[:, None] >= gcol[None, :]) & (gcol >= K)[None, :]).astype(jnp.int32)
    band = lax.dynamic_slice_in_dim(pattern, patch_id * rowblk, rowblk, 0).reshape(rowblk, colslots, ncol)
    local_fill = lax.dynamic_index_in_dim(band, col_id, 2, keepdims=False)
    schur = trailing(local_fill, keep, matrix.reshape(colslots, rowblk * width, width), rows_l, cols_l)
    return (rows_l, schur.reshape(colslots, 1, rowblk * width, width))


def solution(mesh):
    in_specs = (
        P(("patch", "col"), None, None),
        P(("patch", "col"), None),
        P(("patch", "col")),
        P(),
        P(),
        P("patch"),
    )
    out_specs = (P("patch", None), P(None, "col", "patch", None))
    return jax.shard_map(body, mesh=mesh, in_specs=in_specs, out_specs=out_specs, check_vma=False)
```

```python
import functools

import jax
import jax.numpy as jnp
from jax import lax
from jax.experimental import pallas as pl
from jax.experimental.pallas import tpu as pltpu
from jax.sharding import PartitionSpec as P

K = 8
HIGH = lax.Precision.HIGHEST
F32 = jnp.float32
BF16 = jnp.bfloat16
VMEM_BYTES = 60 * 1024 * 1024
SMEM = pl.BlockSpec(memory_space=pltpu.SMEM)
WHOLE = pl.BlockSpec(memory_space=pltpu.VMEM)
NT = (((1,), (1,)), ((), ()))
TN = (((0,), (0,)), ((), ()))


def params(**more):
    return pltpu.CompilerParams(vmem_limit_bytes=VMEM_BYTES, **more)


def dot_nt(a, b):
    return lax.dot_general(a, b, NT, precision=HIGH, preferred_element_type=F32)


def eye_mask(n):
    return lax.broadcasted_iota(jnp.int32, (n, n), 0) == lax.broadcasted_iota(jnp.int32, (n, n), 1)


def pack_kernel(per, meta, x_ref, o_ref):
    first = pl.program_id(0) * per
    width = x_ref.shape[2]

    def step(t, carry):
        slot = meta[0, first + t]
        turned = meta[1, first + t]

        @pl.when((slot >= 0) & (turned == 0))
        def _():
            o_ref[t, 0:width, :] = x_ref[slot]

        @pl.when((slot >= 0) & (turned == 1))
        def _():
            o_ref[t, 0:width, :] = x_ref[slot].T

        o_ref[t, width:, :] = jnp.full((8, width), meta[2, first + t].astype(F32), F32)
        return carry

    lax.fori_loop(0, per, step, 0)


def pack(meta, contributions, ndevice, per=16):
    slots, width, _ = contributions.shape
    return pl.pallas_call(
        functools.partial(pack_kernel, per),
        grid=(ndevice // per,),
        in_specs=[SMEM, pl.BlockSpec((slots, width, width), lambda g: (0, 0, 0), pipeline_mode=pl.Buffered(1))],
        out_specs=pl.BlockSpec((per, width + 8, width), lambda g: (g, 0, 0)),
        out_shape=jax.ShapeDtypeStruct((ndevice, width + 8, width), F32),
        compiler_params=params(),
        name="pack",
    )(meta, contributions)


def place_kernel(per, last, codes, diag, x_ref, reg_ref, o_ref):
    g = pl.program_id(0)
    width = x_ref.shape[2]

    @pl.when(g == 0)
    def _():
        def clear(q, carry):
            o_ref[q] = jnp.zeros((width, width), F32)
            return carry

        lax.fori_loop(0, o_ref.shape[0], clear, 0)

    def step(t, carry):
        code = codes[g * per + t]

        @pl.when(code >= 0)
        def _():
            o_ref[code] += x_ref[t, 0:width, :]

        return carry

    lax.fori_loop(0, per, step, 0)

    @pl.when(g == last)
    def _():
        block = o_ref[diag[0]]
        o_ref[diag[0]] = 0.5 * (block + block.T) + jnp.where(eye_mask(width), reg_ref[...], 0.0)


def place(codes, diag, got, reg, per=16):
    ndevice, high, width = got.shape
    places = 128
    return pl.pallas_call(
        functools.partial(place_kernel, per, ndevice // per - 1),
        grid=(ndevice // per,),
        in_specs=[SMEM, SMEM, pl.BlockSpec((per, high, width), lambda g: (g, 0, 0)), pl.BlockSpec((1, width), lambda g: (0, 0))],
        out_specs=pl.BlockSpec((places, width, width), lambda g: (0, 0, 0), pipeline_mode=pl.Buffered(1)),
        out_shape=jax.ShapeDtypeStruct((places, width, width), F32),
        compiler_params=params(),
        name="place",
    )(codes, diag, got, reg)


def split3(a):
    one = a.astype(BF16).astype(F32)
    rest = a - one
    two = rest.astype(BF16).astype(F32)
    return one, two, rest - two


def chol_inverse(w_ref, lt_ref):
    width = w_ref.shape[0]
    sub = lax.broadcasted_iota(jnp.int32, (8, width), 0)
    lane = lax.broadcasted_iota(jnp.int32, (8, width), 1)
    for base in range(0, width, 8):
        both = w_ref[base : base + 8, :]
        rows = both[:, :width]
        unit = both[:, width:]
        cols = [jnp.broadcast_to(rows[:, base + j : base + j + 1], (8, width)) for j in range(8)]
        scale = jnp.zeros((8, width), F32)
        for j in range(8):
            root = lax.rsqrt(cols[j][j : j + 1, :])
            lower = cols[j] * root
            for i in range(j + 1, 8):
                cols[i] = cols[i] - lower * lower[i : i + 1, :]
            below = jnp.where(sub > j, lower, 0.0)
            rows = rows - below * (rows[j : j + 1, :] * root)
            unit = unit - below * (unit[j : j + 1, :] * root)
            scale = jnp.where(sub == j, root, scale)
        upper = jnp.where(lane >= sub + base, rows * scale, 0.0)
        unit = unit * scale
        lt_ref[base : base + 8, :] = upper
        w_ref[base : base + 8, width:] = unit
        if base + 8 < width:
            u1, u2, u3 = split3(upper)
            v1, v2, v3 = split3(unit)
            left = jnp.concatenate([u1, u1, u2, u2, u1, u3], 0).astype(BF16)
            w1, w2, w3 = (jnp.concatenate([a, b], 1) for a, b in ((u1, v1), (u2, v2), (u3, v3)))
            right = jnp.concatenate([w1, w2, w1, w2, w3, w1], 0).astype(BF16)
            change = lax.dot_general(left, right, TN, preferred_element_type=F32)
            w_ref[base + 8 :, :] -= change[base + 8 :, :]


def head_kernel(fill, head_ref, lh_ref, li_ref, w_ref, lt_ref):
    width = head_ref.shape[2]
    eye = jnp.where(eye_mask(width), 1.0, 0.0).astype(F32)
    for c in range(K):
        for r in range(K):
            at = slice(r * width, (r + 1) * width)
            if r < c:
                lh_ref[c, at, :] = jnp.zeros((width, width), F32)
                continue
            block = head_ref[c, r]
            lh_ref[c, at, :] = 0.5 * (block + block.T) if r == c else block

    def step(k, carry):
        w_ref[:, :width] = lh_ref[k, pl.ds(pl.multiple_of(k * width, width), width), :]
        w_ref[:, width:] = eye
        chol_inverse(w_ref, lt_ref)
        li_ref[k] = w_ref[:, width:]
        lh_ref[k, pl.ds(pl.multiple_of(k * width, width), width), :] = lt_ref[...].T
        for s in range(K - 1):

            @pl.when(k == s)
            def _(s=s):
                below = slice((s + 1) * width, K * width)
                solved = dot_nt(lh_ref[s, below, :], li_ref[s])
                lh_ref[s, below, :] = solved
                for j in range(s + 1, K):
                    part = solved[(j - s - 1) * width :]
                    change = dot_nt(part, part[:width])
                    for i in range(j, K):
                        at = slice(i * width, (i + 1) * width)
                        lh_ref[j, at, :] -= fill[i, j] * change[(i - j) * width : (i - j + 1) * width]

        return carry

    lax.fori_loop(0, K, step, 0)


def factor_head(fill, head):
    width = head.shape[2]
    return pl.pallas_call(
        head_kernel,
        in_specs=[SMEM, WHOLE],
        out_specs=[WHOLE, WHOLE],
        out_shape=[
            jax.ShapeDtypeStruct((K, K * width, width), F32),
            jax.ShapeDtypeStruct((K, width, width), F32),
        ],
        scratch_shapes=[pltpu.VMEM((width, 2 * width), F32), pltpu.VMEM((width, width), F32)],
        compiler_params=params(),
        cost_estimate=pl.CostEstimate(flops=60_000_000_000, bytes_accessed=16_000_000, transcendentals=0),
        name="factor_head",
    )(fill, head)


def solve_kernel(fill, which, a_ref, lh_ref, li_ref, o_ref):
    width = a_ref.shape[1]
    row = which[0]
    work = [a_ref[k] for k in range(K)]
    for k in range(K):
        solved = dot_nt(work[k], li_ref[k])
        own = lh_ref[k, k * width : (k + 1) * width, :]
        solved = jnp.where(row > k, solved, jnp.where(row == k, own, 0.0))
        o_ref[:, k * width : (k + 1) * width] = solved
        if k + 1 < K:
            change = dot_nt(solved, lh_ref[k, (k + 1) * width :, :])
            for j in range(k + 1, K):
                work[j] = work[j] - fill[0, j] * change[:, (j - k - 1) * width : (j - k) * width]


def solve(fill, which, arow, lh, li):
    width = arow.shape[1]
    return pl.pallas_call(
        solve_kernel,
        in_specs=[SMEM, SMEM, WHOLE, WHOLE, WHOLE],
        out_specs=WHOLE,
        out_shape=jax.ShapeDtypeStruct((width, K * width), F32),
        compiler_params=params(),
        name="solve",
    )(fill, which, arow, lh, li)


def schur_kernel(pair, chunk, fill, keep, a_ref, rows_ref, cols_ref, o_ref, panels_ref, hi_ref, lo_ref, sem):
    g = pl.program_id(0)
    width = a_ref.shape[2]
    nrow = a_ref.shape[1] // width

    @pl.when(g == 0)
    def _():
        pltpu.make_async_copy(rows_ref, panels_ref, sem).start()

        def split(r, carry):
            at = pl.ds(pl.multiple_of(r * width, width), width)
            rows = rows_ref[at, :]
            hi = rows.astype(BF16)
            hi_ref[at, :] = hi
            lo_ref[at, :] = (rows - hi.astype(F32)).astype(BF16)
            return carry

        lax.fori_loop(0, nrow, split, 0)

    cols = cols_ref[...].reshape(pair * width, cols_ref.shape[2])
    col_hi = cols.astype(BF16)
    col_lo = (cols - col_hi.astype(F32)).astype(BF16)

    some = keep[nrow - 1, g * pair]
    for q in range(1, pair):
        some = some + keep[nrow - 1, g * pair + q]

    @pl.when(some > 0)
    def _():
        def step(m, carry):
            at = pl.ds(pl.multiple_of(m * chunk * width, chunk * width), chunk * width)
            hi = hi_ref[at, :]
            product = lax.dot_general(hi, col_hi, NT, preferred_element_type=F32)
            product += lax.dot_general(hi, col_lo, NT, preferred_element_type=F32)
            product += lax.dot_general(lo_ref[at, :], col_hi, NT, preferred_element_type=F32)
            for i in range(chunk):
                r = m * chunk + i
                here = pl.ds(pl.multiple_of(r * width, width), width)
                for q in range(pair):
                    part = product[i * width : (i + 1) * width, q * width : (q + 1) * width]
                    value = a_ref[q, here, :] - fill[r, g * pair + q] * part
                    o_ref[q, here, :] = jnp.where(keep[r, g * pair + q] > 0, value, 0.0)
            return carry

        lax.fori_loop(0, nrow // chunk, step, 0)

    @pl.when(some == 0)
    def _():
        o_ref[...] = jnp.zeros(o_ref.shape, F32)

    @pl.when(g == pl.num_programs(0) - 1)
    def _():
        pltpu.make_async_copy(rows_ref, panels_ref, sem).wait()


def trailing(fill, keep, matrix, rows_l, cols_l, pair=2, chunk=4):
    colslots, tall, width = matrix.shape
    depth = rows_l.shape[1]
    return pl.pallas_call(
        functools.partial(schur_kernel, pair, chunk),
        grid=(colslots // pair,),
        in_specs=[
            SMEM,
            SMEM,
            pl.BlockSpec((pair, tall, width), lambda g: (g, 0, 0)),
            pl.BlockSpec((tall, depth), lambda g: (0, 0), pipeline_mode=pl.Buffered(1)),
            pl.BlockSpec((pair, width, depth), lambda g: (g, 0, 0)),
        ],
        out_specs=[pl.BlockSpec((pair, tall, width), lambda g: (g, 0, 0)), pl.BlockSpec(memory_space=pl.ANY)],
        out_shape=[
            jax.ShapeDtypeStruct((colslots, tall, width), F32),
            jax.ShapeDtypeStruct((tall, depth), F32),
        ],
        scratch_shapes=[pltpu.VMEM((tall, depth), BF16), pltpu.VMEM((tall, depth), BF16), pltpu.SemaphoreType.DMA],
        compiler_params=params(),
        name="trailing",
    )(fill, keep, matrix, rows_l, cols_l)


RING = 4


def turn(value, by, size=RING):
    return lax.rem(value + (by + size), size)


class Sends:
    def __init__(self, ssem, rsem):
        self.ssem, self.rsem, self.all = ssem, rsem, []

    def start(self, src, dst, patch, col):
        n = len(self.all)
        copy = pltpu.make_async_remote_copy(
            src_ref=src,
            dst_ref=dst,
            send_sem=self.ssem.at[n],
            recv_sem=self.rsem.at[n],
            device_id={"patch": patch, "col": col},
            device_id_type=pl.DeviceIdType.MESH,
        )
        copy.start()
        self.all.append(copy)
        return copy

    def finish(self):
        for copy in self.all:
            copy.wait_send()


def meet(peers):
    barrier = pltpu.get_barrier_semaphore()
    for patch, col in peers:
        pl.semaphore_signal(
            barrier, inc=1, device_id={"patch": patch, "col": col}, device_id_type=pl.DeviceIdType.MESH
        )
    pl.semaphore_wait(barrier, len(peers))


def col_ring(sends, src, items_ref, patch, col):
    x, core = col // 2, lax.rem(col, 2)
    there = [turn(x, by) * 2 + core for by in range(RING)]
    other = x * 2 + (1 - core)
    half = items_ref.shape[1] // 2
    up = sends.start(src, items_ref.at[col], patch, there[1])
    down = sends.start(src, items_ref.at[col], patch, there[3])
    side = [sends.start(src, items_ref.at[col], patch, other)]
    yield
    up.wait_recv()
    from_down = items_ref.at[there[3]]
    onward = [sends.start(from_down.at[pl.ds(0, half)], from_down.at[pl.ds(0, half)], patch, there[1])]
    side.append(sends.start(from_down, from_down, patch, other))
    down.wait_recv()
    from_up = items_ref.at[there[1]]
    onward.append(sends.start(from_up.at[pl.ds(half, half)], from_up.at[pl.ds(half, half)], patch, there[3]))
    side.append(sends.start(from_up, from_up, patch, other))
    yield
    for copy in onward:
        copy.wait_recv()
    far = items_ref.at[there[2]]
    side.append(sends.start(far, far, patch, other))
    yield
    for copy in side:
        copy.wait_recv()
    yield


def patch_ring(sends, src, items_ref, patch, col, swap):
    y, z = patch // RING, lax.rem(patch, RING)

    def at(first, second):
        i, j = (first, second) if swap else (second, first)
        return turn(y, i) * RING + turn(z, j)

    size = items_ref.shape[1] // 2
    start = size if swap else 0
    whole = pl.ds(start, size)
    parts = (pl.ds(start, size // 2), pl.ds(start + size // 2, size // 2))

    def relay(item, rows, target):
        return sends.start(items_ref.at[item, rows], items_ref.at[item, rows], target, col)

    mine = src.at[whole]
    up = sends.start(mine, items_ref.at[patch, whole], at(1, 0), col)
    down = sends.start(mine, items_ref.at[patch, whole], at(3, 0), col)
    yield
    across = {0: [sends.start(mine, items_ref.at[patch, whole], at(0, by), col) for by in (1, 3)]}
    yield
    up.wait_recv()
    onward = [relay(at(3, 0), parts[0], at(1, 0))]
    across[3] = [relay(at(3, 0), whole, at(0, by)) for by in (1, 3)]
    yield
    down.wait_recv()
    onward.append(relay(at(1, 0), parts[1], at(3, 0)))
    across[1] = [relay(at(1, 0), whole, at(0, by)) for by in (1, 3)]
    yield
    for copy in onward:
        copy.wait_recv()
    across[2] = [relay(at(2, 0), whole, at(0, by)) for by in (1, 3)]
    last = []
    for i in (0, 3, 1, 2):
        yield
        across[i][0].wait_recv()
        last.append(relay(at(i, 3), parts[0], at(0, 1)))
        across[i][1].wait_recv()
        last.append(relay(at(i, 1), parts[1], at(0, 3)))
    yield
    for copy in last:
        copy.wait_recv()
    yield


def interleave(*steps):
    running = list(steps)
    while running:
        running = [one for one in running if next(one, "end") != "end"]


def spread_kernel(own_ref, rows_ref, cols_ref, ssem, rsem, lsem):
    patch, col = lax.axis_index("patch"), lax.axis_index("col")
    y, z, x, core = patch // RING, lax.rem(patch, RING), col // 2, lax.rem(col, 2)
    meet(
        [(turn(y, by) * RING + z, col) for by in (1, 3)]
        + [(y * RING + turn(z, by), col) for by in (1, 3)]
        + [(patch, turn(x, by) * 2 + core) for by in (1, 3)]
        + [(patch, x * 2 + 1 - core)]
    )
    local = [
        pltpu.make_async_copy(own_ref, rows_ref.at[col], lsem.at[0]),
        pltpu.make_async_copy(own_ref, cols_ref.at[patch], lsem.at[1]),
    ]
    sends = Sends(ssem, rsem)
    for copy in local:
        copy.start()
    interleave(
        patch_ring(sends, own_ref, cols_ref, patch, col, False),
        patch_ring(sends, own_ref, cols_ref, patch, col, True),
        col_ring(sends, own_ref, rows_ref, patch, col),
    )
    sends.finish()
    for copy in local:
        copy.wait()


def spread(own, npatch, ncol):
    tall, wide = own.shape
    copies = 48
    return pl.pallas_call(
        spread_kernel,
        in_specs=[WHOLE],
        out_specs=[pl.BlockSpec(memory_space=pl.ANY)] * 2,
        out_shape=[
            jax.ShapeDtypeStruct((ncol, tall, wide), F32),
            jax.ShapeDtypeStruct((npatch, tall, wide), F32),
        ],
        scratch_shapes=[
            pltpu.SemaphoreType.DMA((copies,)),
            pltpu.SemaphoreType.DMA((copies,)),
            pltpu.SemaphoreType.DMA((2,)),
        ],
        compiler_params=params(collective_id=1, has_side_effects=True),
        name="spread",
    )(own)


def gather_head_kernel(npatch, x_ref, reg_ref, head_ref, got_ref, dense_ref, part_ref, piece_ref, ssem, rsem, lsem):
    patch, col = lax.axis_index("patch"), lax.axis_index("col")
    width = x_ref.shape[2]
    meet(
        [(turn(patch, by, npatch), col) for by in range(1, npatch)]
        + [(patch, turn(col, by, K)) for by in range(1, K)]
    )
    sends = Sends(ssem, rsem)
    local = pltpu.make_async_copy(x_ref.at[col], got_ref.at[col], lsem.at[0])
    local.start()
    first = [
        sends.start(x_ref.at[turn(col, by, K)], got_ref.at[col], patch, turn(col, by, K)) for by in range(1, K)
    ]
    local.wait()
    for copy in first:
        copy.wait_recv()
    reg = jnp.broadcast_to(reg_ref[...], (8, width))
    sub = lax.broadcasted_iota(jnp.int32, (8, width), 0)
    lane = lax.broadcasted_iota(jnp.int32, (8, width), 1)
    codes = [got_ref[c, width:, :] for c in range(K)]
    for r in range(K):
        hits = [code == r for code in codes]
        shift = jnp.where((patch == 0) & (col == r), reg, 0.0)
        for q in range(npatch):
            total = jnp.where(lane == sub + q * 8, shift, 0.0)
            for c in range(K):
                total = total + jnp.where(hits[c], got_ref[c, q * 8 : (q + 1) * 8, :], 0.0)
            dense_ref[q, r] = total
    second = [
        sends.start(dense_ref.at[turn(patch, by, npatch)], part_ref.at[by - 1], turn(patch, by, npatch), col)
        for by in range(1, npatch)
    ]
    total = dense_ref[patch]
    for by, copy in enumerate(second):
        copy.wait_recv()
        total = total + part_ref[by]
    piece_ref[...] = total
    here = pl.ds(pl.multiple_of(patch * 8, 8), 8)
    local = pltpu.make_async_copy(piece_ref, head_ref.at[col, :, here, :], lsem.at[1])
    local.start()
    third = [
        sends.start(piece_ref, head_ref.at[col, :, here, :], turn(patch, by, npatch), col) for by in range(1, npatch)
    ]
    local.wait()
    for copy in third:
        copy.wait_recv()
    interleave(col_ring(sends, head_ref.at[col], head_ref, patch, col))
    sends.finish()


def gather_head(outgoing, reg, npatch):
    _, high, width = outgoing.shape
    copies = (K - 1) + 2 * (npatch - 1) + 8
    rows = width // npatch
    return pl.pallas_call(
        functools.partial(gather_head_kernel, npatch),
        grid=(1,),
        in_specs=[pl.BlockSpec((K, high, width), lambda g: (0, 0, 0)), pl.BlockSpec((1, width), lambda g: (0, 0))],
        out_specs=WHOLE,
        out_shape=jax.ShapeDtypeStruct((K, K, width, width), F32),
        scratch_shapes=[
            pltpu.VMEM((K, high, width), F32),
            pltpu.VMEM((npatch, K, rows, width), F32),
            pltpu.VMEM((npatch - 1, K, rows, width), F32),
            pltpu.VMEM((K, rows, width), F32),
            pltpu.SemaphoreType.DMA((copies,)),
            pltpu.SemaphoreType.DMA((copies,)),
            pltpu.SemaphoreType.DMA((2,)),
        ],
        compiler_params=params(collective_id=0, has_side_effects=True),
        name="gather_head",
    )(outgoing, reg)


def route(targets, counts, pivot, rowblk, ncol, ndevice):
    slots = targets.shape[0]
    pos_first = pivot[targets[:, 0]]
    pos_second = pivot[targets[:, 1]]
    upper_pos = jnp.maximum(pos_first, pos_second)
    lower_pos = jnp.minimum(pos_first, pos_second)
    number = jnp.arange(slots, dtype=jnp.int32)
    live = number < counts[0]
    owner = upper_pos // rowblk * ncol + lower_pos % ncol
    select = (owner[:, None] == jnp.arange(ndevice, dtype=jnp.int32)[None, :]) & live[:, None]
    turned = (pos_first < pos_second).astype(jnp.int32)
    code = lower_pos // ncol * rowblk + upper_pos % rowblk
    table = jnp.stack([number, turned, code], 0)
    return jnp.max(jnp.where(select[None], table[:, :, None], -1), 1)


def body(contributions, targets, counts, pivot, fill_draw, regular):
    width = contributions.shape[1]
    npatch = lax.axis_size("patch")
    ncol = lax.axis_size("col")
    ndevice = npatch * ncol
    nblock = pivot.shape[0]
    rowblk = regular.shape[0] // width
    colslots = nblock // ncol
    patch_id = lax.axis_index("patch")
    col_id = lax.axis_index("col")

    meta = route(targets, counts, pivot, rowblk, ncol, ndevice)
    outgoing = pack(meta, contributions, ndevice)

    reg = lax.dynamic_slice_in_dim(regular, col_id * width, width, 0)
    head = gather_head(outgoing, reg[None, :], npatch)
    outgoing, head = lax.optimization_barrier((outgoing, head))

    got = lax.all_to_all(outgoing, ("patch", "col"), split_axis=0, concat_axis=0, tiled=True)

    drawn = fill_draw.astype(F32)
    pattern = jnp.maximum(jnp.maximum(drawn, drawn.T), jnp.eye(nblock, dtype=F32))
    lh, li = factor_head(pattern[:K, :K], head)

    diag = (patch_id * rowblk + col_id).astype(jnp.int32)[None]
    matrix = place(got[:, width, 0].astype(jnp.int32), diag, got, reg[None, :])

    arow = lax.all_to_all(matrix[:rowblk], "col", split_axis=0, concat_axis=0, tiled=True)
    row = patch_id * rowblk + col_id
    row_fill = lax.dynamic_slice(pattern, (row, 0), (1, K))
    lrow = solve(row_fill, row.astype(jnp.int32)[None], arow, lh, li)
    rows_l, cols_l = spread(lrow, npatch, ncol)
    rows_l = rows_l.reshape(rowblk * width, K * width)

    grow = patch_id * rowblk + jnp.arange(rowblk, dtype=jnp.int32)
    gcol = jnp.arange(colslots, dtype=jnp.int32) * ncol + col_id
    keep = ((grow[:, None] >= gcol[None, :]) & (gcol >= K)[None, :]).astype(jnp.int32)
    band = lax.dynamic_slice_in_dim(pattern, patch_id * rowblk, rowblk, 0).reshape(rowblk, colslots, ncol)
    local_fill = lax.dynamic_index_in_dim(band, col_id, 2, keepdims=False)
    schur, panels = trailing(local_fill, keep, matrix.reshape(colslots, rowblk * width, width), rows_l, cols_l)
    return (panels, schur.reshape(colslots, 1, rowblk * width, width))


def solution(mesh):
    in_specs = (
        P(("patch", "col"), None, None),
        P(("patch", "col"), None),
        P(("patch", "col")),
        P(),
        P(),
        P("patch"),
    )
    out_specs = (P("patch", None), P(None, "col", "patch", None))
    return jax.shard_map(body, mesh=mesh, in_specs=in_specs, out_specs=out_specs, check_vma=False)
```

```python
import functools
import itertools
import random

import jax
import jax.numpy as jnp
from jax import lax
from jax.experimental import pallas as pl
from jax.experimental.pallas import tpu as pltpu
from jax.sharding import PartitionSpec as P

K = 8
HIGH = lax.Precision.HIGHEST
F32 = jnp.float32
BF16 = jnp.bfloat16
VMEM_BYTES = 60 * 1024 * 1024
SMEM = pl.BlockSpec(memory_space=pltpu.SMEM)
WHOLE = pl.BlockSpec(memory_space=pltpu.VMEM)
NT = (((1,), (1,)), ((), ()))
TN = (((0,), (0,)), ((), ()))


def params(**more):
    return pltpu.CompilerParams(vmem_limit_bytes=VMEM_BYTES, **more)


def dot_nt(a, b):
    return lax.dot_general(a, b, NT, precision=HIGH, preferred_element_type=F32)


def eye_mask(n):
    return lax.broadcasted_iota(jnp.int32, (n, n), 0) == lax.broadcasted_iota(jnp.int32, (n, n), 1)


def place_kernel(per, last, codes, diag, x_ref, reg_ref, o_ref):
    g = pl.program_id(0)
    width = x_ref.shape[2]

    @pl.when(g == 0)
    def _():
        def clear(q, carry):
            o_ref[q] = jnp.zeros((width, width), F32)
            return carry

        lax.fori_loop(0, o_ref.shape[0], clear, 0)

    def step(t, carry):
        code = codes[g * per + t]

        @pl.when(code >= 0)
        def _():
            o_ref[code] += x_ref[t]

        return carry

    lax.fori_loop(0, per, step, 0)

    @pl.when(g == last)
    def _():
        block = o_ref[diag[0]]
        o_ref[diag[0]] = 0.5 * (block + block.T) + jnp.where(eye_mask(width), reg_ref[...], 0.0)


def place(codes, diag, got, reg, per=16):
    ndevice, _, width = got.shape
    places = 128
    return pl.pallas_call(
        functools.partial(place_kernel, per, ndevice // per - 1),
        grid=(ndevice // per,),
        in_specs=[SMEM, SMEM, pl.BlockSpec((per, width, width), lambda g: (g, 0, 0)), pl.BlockSpec((1, width), lambda g: (0, 0))],
        out_specs=pl.BlockSpec((places, width, width), lambda g: (0, 0, 0), pipeline_mode=pl.Buffered(1)),
        out_shape=jax.ShapeDtypeStruct((places, width, width), F32),
        compiler_params=params(),
        name="place",
    )(codes, diag, got, reg)


def split3(a):
    one = a.astype(BF16).astype(F32)
    rest = a - one
    two = rest.astype(BF16).astype(F32)
    return one, two, rest - two


def chol_inverse(w_ref, lt_ref):
    width = w_ref.shape[0]
    sub = lax.broadcasted_iota(jnp.int32, (8, width), 0)
    lane = lax.broadcasted_iota(jnp.int32, (8, width), 1)
    for base in range(0, width, 8):
        both = w_ref[base : base + 8, :]
        rows = both[:, :width]
        unit = both[:, width:]
        cols = [jnp.broadcast_to(rows[:, base + j : base + j + 1], (8, width)) for j in range(8)]
        scale = jnp.zeros((8, width), F32)
        for j in range(8):
            root = lax.rsqrt(cols[j][j : j + 1, :])
            lower = cols[j] * root
            for i in range(j + 1, 8):
                cols[i] = cols[i] - lower * lower[i : i + 1, :]
            below = jnp.where(sub > j, lower, 0.0)
            rows = rows - below * (rows[j : j + 1, :] * root)
            unit = unit - below * (unit[j : j + 1, :] * root)
            scale = jnp.where(sub == j, root, scale)
        upper = jnp.where(lane >= sub + base, rows * scale, 0.0)
        unit = unit * scale
        lt_ref[base : base + 8, :] = upper
        w_ref[base : base + 8, width:] = unit
        if base + 8 < width:
            u1, u2, u3 = split3(upper)
            v1, v2, v3 = split3(unit)
            left = jnp.concatenate([u1, u1, u2, u2, u1, u3], 0).astype(BF16)
            w1, w2, w3 = (jnp.concatenate([a, b], 1) for a, b in ((u1, v1), (u2, v2), (u3, v3)))
            right = jnp.concatenate([w1, w2, w1, w2, w3, w1], 0).astype(BF16)
            change = lax.dot_general(left, right, TN, preferred_element_type=F32)
            w_ref[base + 8 :, :] -= change[base + 8 :, :]


def factor_head(fill, head_ref, lh_ref, li_ref, w_ref, lt_ref):
    width = head_ref.shape[2]
    eye = jnp.where(eye_mask(width), 1.0, 0.0).astype(F32)
    for c in range(K):
        for r in range(K):
            at = slice(r * width, (r + 1) * width)
            if r < c:
                lh_ref[c, at, :] = jnp.zeros((width, width), F32)
                continue
            block = head_ref[c, r]
            lh_ref[c, at, :] = 0.5 * (block + block.T) if r == c else block

    def step(k, carry):
        w_ref[:, :width] = lh_ref[k, pl.ds(pl.multiple_of(k * width, width), width), :]
        w_ref[:, width:] = eye
        chol_inverse(w_ref, lt_ref)
        li_ref[k] = w_ref[:, width:]
        lh_ref[k, pl.ds(pl.multiple_of(k * width, width), width), :] = lt_ref[...].T
        for s in range(K - 1):

            @pl.when(k == s)
            def _(s=s):
                below = slice((s + 1) * width, K * width)
                solved = dot_nt(lh_ref[s, below, :], li_ref[s])
                lh_ref[s, below, :] = solved
                for j in range(s + 1, K):
                    part = solved[(j - s - 1) * width :]
                    change = dot_nt(part, part[:width])
                    for i in range(j, K):
                        at = slice(i * width, (i + 1) * width)
                        lh_ref[j, at, :] -= fill[i, j] * change[(i - j) * width : (i - j + 1) * width]

        return carry

    lax.fori_loop(0, K, step, 0)


def solve_kernel(fill, which, a_ref, lh_ref, li_ref, o_ref):
    width = a_ref.shape[1]
    row = which[0]
    work = [a_ref[k] for k in range(K)]
    for k in range(K):
        solved = dot_nt(work[k], li_ref[k])
        own = lh_ref[k, k * width : (k + 1) * width, :]
        solved = jnp.where(row > k, solved, jnp.where(row == k, own, 0.0))
        o_ref[:, k * width : (k + 1) * width] = solved
        if k + 1 < K:
            change = dot_nt(solved, lh_ref[k, (k + 1) * width :, :])
            for j in range(k + 1, K):
                work[j] = work[j] - fill[0, j] * change[:, (j - k - 1) * width : (j - k) * width]


def solve(fill, which, arow, lh, li):
    width = arow.shape[1]
    return pl.pallas_call(
        solve_kernel,
        in_specs=[SMEM, SMEM, WHOLE, WHOLE, WHOLE],
        out_specs=WHOLE,
        out_shape=jax.ShapeDtypeStruct((width, K * width), F32),
        compiler_params=params(),
        name="solve",
    )(fill, which, arow, lh, li)


def schur_kernel(pair, chunk, fill, keep, a_ref, rows_ref, cols_ref, o_ref, panels_ref, hi_ref, lo_ref, sem):
    g = pl.program_id(0)
    width = a_ref.shape[2]
    nrow = a_ref.shape[1] // width

    @pl.when(g == 0)
    def _():
        pltpu.make_async_copy(rows_ref, panels_ref, sem).start()

        def split(r, carry):
            at = pl.ds(pl.multiple_of(r * width, width), width)
            rows = rows_ref[at, :]
            hi = rows.astype(BF16)
            hi_ref[at, :] = hi
            lo_ref[at, :] = (rows - hi.astype(F32)).astype(BF16)
            return carry

        lax.fori_loop(0, nrow, split, 0)

    cols = cols_ref[...].reshape(pair * width, cols_ref.shape[2])
    col_hi = cols.astype(BF16)
    col_lo = (cols - col_hi.astype(F32)).astype(BF16)

    some = keep[nrow - 1, g * pair]
    for q in range(1, pair):
        some = some + keep[nrow - 1, g * pair + q]

    @pl.when(some > 0)
    def _():
        def step(m, carry):
            at = pl.ds(pl.multiple_of(m * chunk * width, chunk * width), chunk * width)
            hi = hi_ref[at, :]
            product = lax.dot_general(hi, col_hi, NT, preferred_element_type=F32)
            product += lax.dot_general(hi, col_lo, NT, preferred_element_type=F32)
            product += lax.dot_general(lo_ref[at, :], col_hi, NT, preferred_element_type=F32)
            for i in range(chunk):
                r = m * chunk + i
                here = pl.ds(pl.multiple_of(r * width, width), width)
                for q in range(pair):
                    part = product[i * width : (i + 1) * width, q * width : (q + 1) * width]
                    value = a_ref[q, here, :] - fill[r, g * pair + q] * part
                    o_ref[q, here, :] = jnp.where(keep[r, g * pair + q] > 0, value, 0.0)
            return carry

        lax.fori_loop(0, nrow // chunk, step, 0)

    @pl.when(some == 0)
    def _():
        o_ref[...] = jnp.zeros(o_ref.shape, F32)

    @pl.when(g == pl.num_programs(0) - 1)
    def _():
        pltpu.make_async_copy(rows_ref, panels_ref, sem).wait()


def trailing(fill, keep, matrix, rows_l, cols_l, pair=2, chunk=4):
    colslots, tall, width = matrix.shape
    depth = rows_l.shape[1]
    return pl.pallas_call(
        functools.partial(schur_kernel, pair, chunk),
        grid=(colslots // pair,),
        in_specs=[
            SMEM,
            SMEM,
            pl.BlockSpec((pair, tall, width), lambda g: (g, 0, 0)),
            pl.BlockSpec((tall, depth), lambda g: (0, 0), pipeline_mode=pl.Buffered(1)),
            pl.BlockSpec((pair, width, depth), lambda g: (g, 0, 0)),
        ],
        out_specs=[pl.BlockSpec((pair, tall, width), lambda g: (g, 0, 0)), pl.BlockSpec(memory_space=pl.ANY)],
        out_shape=[
            jax.ShapeDtypeStruct((colslots, tall, width), F32),
            jax.ShapeDtypeStruct((tall, depth), F32),
        ],
        scratch_shapes=[pltpu.VMEM((tall, depth), BF16), pltpu.VMEM((tall, depth), BF16), pltpu.SemaphoreType.DMA],
        compiler_params=params(),
        name="trailing",
    )(fill, keep, matrix, rows_l, cols_l)


RING = 4


def turn(value, by, size=RING):
    return lax.rem(value + (by + size), size)


class Sends:
    def __init__(self, ssem, rsem):
        self.ssem, self.rsem, self.all = ssem, rsem, []

    def start(self, src, dst, patch, col):
        n = len(self.all)
        copy = pltpu.make_async_remote_copy(
            src_ref=src,
            dst_ref=dst,
            send_sem=self.ssem.at[n],
            recv_sem=self.rsem.at[n],
            device_id={"patch": patch, "col": col},
            device_id_type=pl.DeviceIdType.MESH,
        )
        copy.start()
        self.all.append(copy)
        return copy

    def finish(self):
        for copy in self.all:
            copy.wait_send()


def meet(peers):
    barrier = pltpu.get_barrier_semaphore()
    for patch, col in peers:
        pl.semaphore_signal(
            barrier, inc=1, device_id={"patch": patch, "col": col}, device_id_type=pl.DeviceIdType.MESH
        )
    pl.semaphore_wait(barrier, len(peers))


def col_ring(sends, src, items_ref, patch, col):
    x, core = col // 2, lax.rem(col, 2)
    there = [turn(x, by) * 2 + core for by in range(RING)]
    other = x * 2 + (1 - core)
    half = items_ref.shape[1] // 2
    up = sends.start(src, items_ref.at[col], patch, there[1])
    down = sends.start(src, items_ref.at[col], patch, there[3])
    side = [sends.start(src, items_ref.at[col], patch, other)]
    yield
    up.wait_recv()
    from_down = items_ref.at[there[3]]
    onward = [sends.start(from_down.at[pl.ds(0, half)], from_down.at[pl.ds(0, half)], patch, there[1])]
    side.append(sends.start(from_down, from_down, patch, other))
    down.wait_recv()
    from_up = items_ref.at[there[1]]
    onward.append(sends.start(from_up.at[pl.ds(half, half)], from_up.at[pl.ds(half, half)], patch, there[3]))
    side.append(sends.start(from_up, from_up, patch, other))
    yield
    for copy in onward:
        copy.wait_recv()
    far = items_ref.at[there[2]]
    side.append(sends.start(far, far, patch, other))
    yield
    for copy in side:
        copy.wait_recv()
    yield


def patch_ring(sends, src, items_ref, patch, col, swap):
    y, z = patch // RING, lax.rem(patch, RING)

    def at(first, second):
        i, j = (first, second) if swap else (second, first)
        return turn(y, i) * RING + turn(z, j)

    size = items_ref.shape[1] // 2
    start = size if swap else 0
    whole = pl.ds(start, size)
    parts = (pl.ds(start, size // 2), pl.ds(start + size // 2, size // 2))

    def relay(item, rows, target):
        return sends.start(items_ref.at[item, rows], items_ref.at[item, rows], target, col)

    mine = src.at[whole]
    up = sends.start(mine, items_ref.at[patch, whole], at(1, 0), col)
    down = sends.start(mine, items_ref.at[patch, whole], at(3, 0), col)
    yield
    across = {0: [sends.start(mine, items_ref.at[patch, whole], at(0, by), col) for by in (1, 3)]}
    yield
    up.wait_recv()
    onward = [relay(at(3, 0), parts[0], at(1, 0))]
    across[3] = [relay(at(3, 0), whole, at(0, by)) for by in (1, 3)]
    yield
    down.wait_recv()
    onward.append(relay(at(1, 0), parts[1], at(3, 0)))
    across[1] = [relay(at(1, 0), whole, at(0, by)) for by in (1, 3)]
    yield
    for copy in onward:
        copy.wait_recv()
    across[2] = [relay(at(2, 0), whole, at(0, by)) for by in (1, 3)]
    last = []
    for i in (0, 3, 1, 2):
        yield
        across[i][0].wait_recv()
        last.append(relay(at(i, 3), parts[0], at(0, 1)))
        across[i][1].wait_recv()
        last.append(relay(at(i, 1), parts[1], at(0, 3)))
    yield
    for copy in last:
        copy.wait_recv()
    yield


def interleave(*steps):
    running = list(steps)
    while running:
        running = [one for one in running if next(one, "end") != "end"]


def spread_kernel(own_ref, rows_ref, cols_ref, ssem, rsem, lsem):
    patch, col = lax.axis_index("patch"), lax.axis_index("col")
    y, z, x, core = patch // RING, lax.rem(patch, RING), col // 2, lax.rem(col, 2)
    meet(
        [(turn(y, by) * RING + z, col) for by in (1, 3)]
        + [(y * RING + turn(z, by), col) for by in (1, 3)]
        + [(patch, turn(x, by) * 2 + core) for by in (1, 3)]
        + [(patch, x * 2 + 1 - core)]
    )
    local = [
        pltpu.make_async_copy(own_ref, rows_ref.at[col], lsem.at[0]),
        pltpu.make_async_copy(own_ref, cols_ref.at[patch], lsem.at[1]),
    ]
    sends = Sends(ssem, rsem)
    for copy in local:
        copy.start()
    interleave(
        patch_ring(sends, own_ref, cols_ref, patch, col, False),
        patch_ring(sends, own_ref, cols_ref, patch, col, True),
        col_ring(sends, own_ref, rows_ref, patch, col),
    )
    sends.finish()
    for copy in local:
        copy.wait()


def spread(own, npatch, ncol):
    tall, wide = own.shape
    copies = 48
    return pl.pallas_call(
        spread_kernel,
        in_specs=[WHOLE],
        out_specs=[pl.BlockSpec(memory_space=pl.ANY)] * 2,
        out_shape=[
            jax.ShapeDtypeStruct((ncol, tall, wide), F32),
            jax.ShapeDtypeStruct((npatch, tall, wide), F32),
        ],
        scratch_shapes=[
            pltpu.SemaphoreType.DMA((copies,)),
            pltpu.SemaphoreType.DMA((copies,)),
            pltpu.SemaphoreType.DMA((2,)),
        ],
        compiler_params=params(collective_id=1, has_side_effects=True),
        name="spread",
    )(own)


def offsets():
    left = [o for o in itertools.product(range(RING), range(RING), range(RING), range(2)) if any(o)]
    random.Random(3).shuffle(left)

    def links(o):
        return [float(v in (2, want)) for v in o[:3] for want in (1, 3)]

    load, order = [0.0] * 6, []
    while left:
        best = min(left, key=lambda o: max(map(sum, zip(load, links(o)))) - min(map(sum, zip(load, links(o)))))
        left.remove(best)
        order.append(best)
        load = [sum(pair) for pair in zip(load, links(best))]
    return order


batches = (12, 12, 12, 12, 6, 0)


def exchange_kernel(
    npatch,
    meta,
    fill,
    x_ref,
    code_ref,
    reg_ref,
    all_ref,
    codes_ref,
    lh_ref,
    li_ref,
    out_ref,
    mine_ref,
    tile_ref,
    row_ref,
    dense_ref,
    part_ref,
    piece_ref,
    head_ref,
    w_ref,
    lt_ref,
    ssem,
    rsem,
    bulk,
    lsem,
):
    patch, col = lax.axis_index("patch"), lax.axis_index("col")
    y, z, x, core = patch // RING, lax.rem(patch, RING), col // 2, lax.rem(col, 2)
    me = patch * K + col
    width = x_ref.shape[2]
    ndevice = npatch * K

    sign = 1 + 2 * core
    peers = []
    for dy, dz, dx, dc in offsets():
        to_patch = lax.rem(y + dy * sign, RING) * RING + lax.rem(z + dz * sign, RING)
        to_col = lax.rem(x + dx * sign, RING) * 2 + lax.rem(core + dc, 2)
        peers.append((to_patch, to_col))
    barrier = pltpu.get_barrier_semaphore()
    for to_patch, to_col in peers:
        pl.semaphore_signal(
            barrier, inc=1, device_id={"patch": to_patch, "col": to_col}, device_id_type=pl.DeviceIdType.MESH
        )

    def pack(d, carry):
        block = x_ref[jnp.maximum(meta[0, d], 0)]
        out_ref[d] = jnp.where(meta[1, d] > 0, block.T, block)
        return carry

    lax.fori_loop(0, K, pack, 0)
    row_ref[...] = jnp.broadcast_to(code_ref[...], (8, width))
    pl.semaphore_wait(barrier, len(peers))

    sends = Sends(ssem, rsem)

    def flow(count):
        for to_patch, to_col in peers[flow.done : flow.done + count]:
            pltpu.make_async_remote_copy(
                src_ref=out_ref.at[to_patch * K + to_col],
                dst_ref=all_ref.at[me],
                send_sem=bulk.at[0],
                recv_sem=bulk.at[1],
                device_id={"patch": to_patch, "col": to_col},
                device_id_type=pl.DeviceIdType.MESH,
            ).start()
        flow.done += count

    flow.done = 0

    local = [
        pltpu.make_async_copy(out_ref.at[col], mine_ref.at[col], lsem.at[0]),
        pltpu.make_async_copy(row_ref, tile_ref.at[col], lsem.at[1]),
    ]
    for copy in local:
        copy.start()
    first = []
    for by in range(1, K):
        to = turn(col, by, K)
        first.append(sends.start(row_ref, tile_ref.at[col], patch, to))
        first.append(sends.start(out_ref.at[to], mine_ref.at[col], patch, to))
    lax.fori_loop(K, ndevice, pack, 0)
    own = pltpu.make_async_copy(out_ref.at[me], all_ref.at[me], lsem.at[2])
    own.start()
    flow(4)
    for copy in local:
        copy.wait()
    for copy in first:
        copy.wait_recv()
    reg = jnp.broadcast_to(reg_ref[...], (8, width))
    sub = lax.broadcasted_iota(jnp.int32, (8, width), 0)
    lane = lax.broadcasted_iota(jnp.int32, (8, width), 1)
    codes = []
    tile = jnp.zeros((8, width), F32)
    for c in range(K):
        row = tile_ref[c]
        tile = jnp.where(sub == c, row, tile)
        codes.append(jnp.broadcast_to(jnp.sum(jnp.where(lane == col, row, 0.0), 1, keepdims=True), (8, width)))
    for r in range(K):
        hits = [code == r for code in codes]
        shift = jnp.where((patch == 0) & (col == r), reg, 0.0)
        for q in range(npatch):
            total = jnp.where(lane == sub + q * 8, shift, 0.0)
            for c in range(K):
                total = total + jnp.where(hits[c], mine_ref[c, q * 8 : (q + 1) * 8, :], 0.0)
            dense_ref[q, r] = total
    here = pl.ds(pl.multiple_of(patch * 8, 8), 8)
    codes_ref[here, :] = tile
    second = []
    tables = []
    for by in range(1, npatch):
        to = turn(patch, by, npatch)
        second.append(sends.start(dense_ref.at[to], part_ref.at[by - 1], to, col))
    for by in range(1, npatch):
        tables.append(sends.start(codes_ref.at[here, :], codes_ref.at[here, :], turn(patch, by, npatch), col))
    flow(batches[0])
    total = dense_ref[patch]
    for by, copy in enumerate(second):
        copy.wait_recv()
        total = total + part_ref[by]
    piece_ref[...] = total
    local = pltpu.make_async_copy(piece_ref, head_ref.at[col, :, here, :], lsem.at[0])
    local.start()
    third = [
        sends.start(piece_ref, head_ref.at[col, :, here, :], turn(patch, by, npatch), col) for by in range(1, npatch)
    ]
    flow(batches[1])
    local.wait()
    for copy in third:
        copy.wait_recv()
    for count, _ in zip(batches[2:], col_ring(sends, head_ref.at[col], head_ref, patch, col)):
        flow(count)
    flow(len(peers) - flow.done)

    factor_head(fill, head_ref, lh_ref, li_ref, w_ref, lt_ref)

    sends.finish()
    for copy in tables:
        copy.wait_recv()
    own.wait()
    every = pl.ds(0, ndevice - 1)
    whole = pltpu.make_async_remote_copy(
        src_ref=out_ref.at[every],
        dst_ref=all_ref.at[every],
        send_sem=bulk.at[0],
        recv_sem=bulk.at[1],
        device_id={"patch": peers[0][0], "col": peers[0][1]},
        device_id_type=pl.DeviceIdType.MESH,
    )
    whole.wait_send()
    whole.wait_recv()


def exchange(meta, fill, contributions, reg, npatch):
    slots, width, _ = contributions.shape
    ndevice = npatch * K
    copies = 2 * (K - 1) + 3 * (npatch - 1) + 8
    rows = width // npatch
    block = (width, width)
    return pl.pallas_call(
        functools.partial(exchange_kernel, npatch),
        in_specs=[SMEM, SMEM, WHOLE, WHOLE, WHOLE],
        out_specs=[pl.BlockSpec(memory_space=pl.ANY), WHOLE, WHOLE, WHOLE],
        out_shape=[
            jax.ShapeDtypeStruct((ndevice,) + block, F32),
            jax.ShapeDtypeStruct((ndevice, ndevice), F32),
            jax.ShapeDtypeStruct((K, K * width, width), F32),
            jax.ShapeDtypeStruct((K,) + block, F32),
        ],
        scratch_shapes=[
            pltpu.VMEM((ndevice,) + block, F32),
            pltpu.VMEM((K,) + block, F32),
            pltpu.VMEM((K, 8, width), F32),
            pltpu.VMEM((8, width), F32),
            pltpu.VMEM((npatch, K, rows, width), F32),
            pltpu.VMEM((npatch - 1, K, rows, width), F32),
            pltpu.VMEM((K, rows, width), F32),
            pltpu.VMEM((K, K) + block, F32),
            pltpu.VMEM((width, 2 * width), F32),
            pltpu.VMEM(block, F32),
            pltpu.SemaphoreType.DMA((copies,)),
            pltpu.SemaphoreType.DMA((copies,)),
            pltpu.SemaphoreType.DMA((2,)),
            pltpu.SemaphoreType.DMA((3,)),
        ],
        compiler_params=params(collective_id=0, has_side_effects=True),
        name="exchange",
    )(meta[:2], fill, contributions, meta[2:].astype(F32), reg)


def route(targets, counts, pivot, rowblk, ncol, ndevice):
    slots = targets.shape[0]
    pos_first = pivot[targets[:, 0]]
    pos_second = pivot[targets[:, 1]]
    upper_pos = jnp.maximum(pos_first, pos_second)
    lower_pos = jnp.minimum(pos_first, pos_second)
    number = jnp.arange(slots, dtype=jnp.int32)
    live = number < counts[0]
    owner = upper_pos // rowblk * ncol + lower_pos % ncol
    select = (owner[:, None] == jnp.arange(ndevice, dtype=jnp.int32)[None, :]) & live[:, None]
    turned = (pos_first < pos_second).astype(jnp.int32)
    code = lower_pos // ncol * rowblk + upper_pos % rowblk
    table = jnp.stack([number, turned, code], 0)
    return jnp.max(jnp.where(select[None], table[:, :, None], -1), 1)


def body(contributions, targets, counts, pivot, fill_draw, regular):
    width = contributions.shape[1]
    npatch = lax.axis_size("patch")
    ncol = lax.axis_size("col")
    ndevice = npatch * ncol
    nblock = pivot.shape[0]
    rowblk = regular.shape[0] // width
    colslots = nblock // ncol
    patch_id = lax.axis_index("patch")
    col_id = lax.axis_index("col")

    meta = route(targets, counts, pivot, rowblk, ncol, ndevice)
    reg = lax.dynamic_slice_in_dim(regular, col_id * width, width, 0)[None, :]
    drawn = fill_draw.astype(F32)
    pattern = jnp.maximum(jnp.maximum(drawn, drawn.T), jnp.eye(nblock, dtype=F32))
    got, table, lh, li = exchange(meta, pattern[:K, :K], contributions, reg, npatch)

    diag = (patch_id * rowblk + col_id).astype(jnp.int32)[None]
    codes = lax.dynamic_slice_in_dim(table, diag[0], 1, 1)[:, 0].astype(jnp.int32)
    matrix = place(codes, diag, got, reg)

    arow = lax.all_to_all(matrix[:rowblk], "col", split_axis=0, concat_axis=0, tiled=True)
    row = patch_id * rowblk + col_id
    row_fill = lax.dynamic_slice(pattern, (row, 0), (1, K))
    lrow = solve(row_fill, row.astype(jnp.int32)[None], arow, lh, li)
    rows_l, cols_l = spread(lrow, npatch, ncol)
    rows_l = rows_l.reshape(rowblk * width, K * width)

    grow = patch_id * rowblk + jnp.arange(rowblk, dtype=jnp.int32)
    gcol = jnp.arange(colslots, dtype=jnp.int32) * ncol + col_id
    keep = ((grow[:, None] >= gcol[None, :]) & (gcol >= K)[None, :]).astype(jnp.int32)
    band = lax.dynamic_slice_in_dim(pattern, patch_id * rowblk, rowblk, 0).reshape(rowblk, colslots, ncol)
    local_fill = lax.dynamic_index_in_dim(band, col_id, 2, keepdims=False)
    schur, panels = trailing(local_fill, keep, matrix.reshape(colslots, rowblk * width, width), rows_l, cols_l)
    return (panels, schur.reshape(colslots, 1, rowblk * width, width))


def solution(mesh):
    in_specs = (
        P(("patch", "col"), None, None),
        P(("patch", "col"), None),
        P(("patch", "col")),
        P(),
        P(),
        P("patch"),
    )
    out_specs = (P("patch", None), P(None, "col", "patch", None))
    return jax.shard_map(body, mesh=mesh, in_specs=in_specs, out_specs=out_specs, check_vma=False)
```

```python
import functools
import itertools
import random

import jax
import jax.numpy as jnp
from jax import lax
from jax.experimental import pallas as pl
from jax.experimental.pallas import tpu as pltpu
from jax.sharding import PartitionSpec as P

K = 8
HIGH = lax.Precision.HIGHEST
F32 = jnp.float32
BF16 = jnp.bfloat16
VMEM_BYTES = 60 * 1024 * 1024
SMEM = pl.BlockSpec(memory_space=pltpu.SMEM)
WHOLE = pl.BlockSpec(memory_space=pltpu.VMEM)
NT = (((1,), (1,)), ((), ()))
TN = (((0,), (0,)), ((), ()))


def params(**more):
    return pltpu.CompilerParams(vmem_limit_bytes=VMEM_BYTES, **more)


def dot_nt(a, b):
    return lax.dot_general(a, b, NT, precision=HIGH, preferred_element_type=F32)


def eye_mask(n):
    return lax.broadcasted_iota(jnp.int32, (n, n), 0) == lax.broadcasted_iota(jnp.int32, (n, n), 1)


def place_kernel(per, last, codes, diag, x_ref, reg_ref, o_ref):
    g = pl.program_id(0)
    width = x_ref.shape[2]

    @pl.when(g == 0)
    def _():
        def clear(q, carry):
            o_ref[q] = jnp.zeros((width, width), F32)
            return carry

        lax.fori_loop(0, o_ref.shape[0], clear, 0)

    def step(t, carry):
        code = codes[g * per + t]

        @pl.when(code >= 0)
        def _():
            o_ref[code] += x_ref[t]

        return carry

    lax.fori_loop(0, per, step, 0)

    @pl.when(g == last)
    def _():
        block = o_ref[diag[0]]
        o_ref[diag[0]] = 0.5 * (block + block.T) + jnp.where(eye_mask(width), reg_ref[...], 0.0)


def place(codes, diag, got, reg, per=16):
    ndevice, _, width = got.shape
    places = 128
    return pl.pallas_call(
        functools.partial(place_kernel, per, ndevice // per - 1),
        grid=(ndevice // per,),
        in_specs=[SMEM, SMEM, pl.BlockSpec((per, width, width), lambda g: (g, 0, 0)), pl.BlockSpec((1, width), lambda g: (0, 0))],
        out_specs=pl.BlockSpec((places, width, width), lambda g: (0, 0, 0), pipeline_mode=pl.Buffered(1)),
        out_shape=jax.ShapeDtypeStruct((places, width, width), F32),
        compiler_params=params(),
        name="place",
    )(codes, diag, got, reg)


def split3(a):
    one = a.astype(BF16).astype(F32)
    rest = a - one
    two = rest.astype(BF16).astype(F32)
    return one, two, rest - two


def chol_inverse(w_ref, lt_ref):
    width = w_ref.shape[0]
    sub = lax.broadcasted_iota(jnp.int32, (8, width), 0)
    lane = lax.broadcasted_iota(jnp.int32, (8, width), 1)
    for base in range(0, width, 8):
        both = w_ref[base : base + 8, :]
        rows = both[:, :width]
        unit = both[:, width:]
        cols = [jnp.broadcast_to(rows[:, base + j : base + j + 1], (8, width)) for j in range(8)]
        scale = jnp.zeros((8, width), F32)
        for j in range(8):
            root = lax.rsqrt(cols[j][j : j + 1, :])
            lower = cols[j] * root
            for i in range(j + 1, 8):
                cols[i] = cols[i] - lower * lower[i : i + 1, :]
            below = jnp.where(sub > j, lower, 0.0)
            rows = rows - below * (rows[j : j + 1, :] * root)
            unit = unit - below * (unit[j : j + 1, :] * root)
            scale = jnp.where(sub == j, root, scale)
        upper = jnp.where(lane >= sub + base, rows * scale, 0.0)
        unit = unit * scale
        lt_ref[base : base + 8, :] = upper
        w_ref[base : base + 8, width:] = unit
        if base + 8 < width:
            u1, u2, u3 = split3(upper)
            v1, v2, v3 = split3(unit)
            left = jnp.concatenate([u1, u1, u2, u2, u1, u3], 0).astype(BF16)
            w1, w2, w3 = (jnp.concatenate([a, b], 1) for a, b in ((u1, v1), (u2, v2), (u3, v3)))
            right = jnp.concatenate([w1, w2, w1, w2, w3, w1], 0).astype(BF16)
            change = lax.dot_general(left, right, TN, preferred_element_type=F32)
            w_ref[base + 8 :, :] -= change[base + 8 :, :]


def factor_head(fill, head_ref, lh_ref, li_ref, w_ref, lt_ref):
    width = head_ref.shape[2]
    eye = jnp.where(eye_mask(width), 1.0, 0.0).astype(F32)
    for c in range(K):
        for r in range(K):
            at = slice(r * width, (r + 1) * width)
            if r < c:
                lh_ref[c, at, :] = jnp.zeros((width, width), F32)
                continue
            block = head_ref[c, r]
            lh_ref[c, at, :] = 0.5 * (block + block.T) if r == c else block

    def step(k, carry):
        w_ref[:, :width] = lh_ref[k, pl.ds(pl.multiple_of(k * width, width), width), :]
        w_ref[:, width:] = eye
        chol_inverse(w_ref, lt_ref)
        li_ref[k] = w_ref[:, width:]
        lh_ref[k, pl.ds(pl.multiple_of(k * width, width), width), :] = lt_ref[...].T
        for s in range(K - 1):

            @pl.when(k == s)
            def _(s=s):
                below = slice((s + 1) * width, K * width)
                solved = dot_nt(lh_ref[s, below, :], li_ref[s])
                lh_ref[s, below, :] = solved
                for j in range(s + 1, K):
                    part = solved[(j - s - 1) * width :]
                    change = dot_nt(part, part[:width])
                    for i in range(j, K):
                        at = slice(i * width, (i + 1) * width)
                        lh_ref[j, at, :] -= fill[i, j] * change[(i - j) * width : (i - j + 1) * width]

        return carry

    lax.fori_loop(0, K, step, 0)


def split2(a):
    hi = a.astype(BF16)
    return hi, (a - hi.astype(F32)).astype(BF16)


def hand_on(lh_ref, li_ref, uh_ref, ul_ref, ih_ref, il_ref, diag_ref):
    width = lh_ref.shape[2]

    def column(k, carry):
        diag_ref[k] = lh_ref[k, pl.ds(pl.multiple_of(k * width, width), width), :]
        ih_ref[k], il_ref[k] = split2(li_ref[k].T)

        def row(i, carry):
            at = pl.ds(pl.multiple_of(i * width, width), width)
            uh_ref[k, :, at], ul_ref[k, :, at] = split2(lh_ref[k, at, :].T)
            return carry

        return lax.fori_loop(k + 1, K, row, carry)

    lax.fori_loop(0, K, column, 0)


def dot3(a, b_hi, b_lo):
    a_hi, a_lo = split2(a)
    product = jnp.dot(a_hi, b_hi, preferred_element_type=F32)
    product += jnp.dot(a_lo, b_hi, preferred_element_type=F32)
    return product + jnp.dot(a_hi, b_lo, preferred_element_type=F32)


def solve_row(row, fill, a_ref, uh_ref, ul_ref, ih_ref, il_ref, diag_ref, o_ref):
    width = a_ref.shape[1]
    work = [a_ref[k] for k in range(K)]
    for k in range(K):
        solved = dot3(work[k], ih_ref[k], il_ref[k])
        solved = jnp.where(row > k, solved, jnp.where(row == k, diag_ref[k], 0.0))
        o_ref[:, k * width : (k + 1) * width] = solved
        if k + 1 < K:
            change = dot3(solved, uh_ref[k, :, (k + 1) * width :], ul_ref[k, :, (k + 1) * width :])
            for j in range(k + 1, K):
                work[j] = work[j] - fill[0, j] * change[:, (j - k - 1) * width : (j - k) * width]


def schur_kernel(pair, chunk, fill, keep, a_ref, rows_ref, cols_ref, o_ref, panels_ref, hi_ref, lo_ref, sem):
    g = pl.program_id(0)
    width = a_ref.shape[2]
    nrow = a_ref.shape[1] // width

    @pl.when(g == 0)
    def _():
        pltpu.make_async_copy(rows_ref, panels_ref, sem).start()

        def split(r, carry):
            at = pl.ds(pl.multiple_of(r * width, width), width)
            rows = rows_ref[at, :]
            hi = rows.astype(BF16)
            hi_ref[at, :] = hi
            lo_ref[at, :] = (rows - hi.astype(F32)).astype(BF16)
            return carry

        lax.fori_loop(0, nrow, split, 0)

    cols = cols_ref[...].reshape(pair * width, cols_ref.shape[2])
    col_hi = cols.astype(BF16)
    col_lo = (cols - col_hi.astype(F32)).astype(BF16)

    some = keep[nrow - 1, g * pair]
    for q in range(1, pair):
        some = some + keep[nrow - 1, g * pair + q]

    @pl.when(some > 0)
    def _():
        def step(m, carry):
            at = pl.ds(pl.multiple_of(m * chunk * width, chunk * width), chunk * width)
            hi = hi_ref[at, :]
            product = lax.dot_general(hi, col_hi, NT, preferred_element_type=F32)
            product += lax.dot_general(hi, col_lo, NT, preferred_element_type=F32)
            product += lax.dot_general(lo_ref[at, :], col_hi, NT, preferred_element_type=F32)
            for i in range(chunk):
                r = m * chunk + i
                here = pl.ds(pl.multiple_of(r * width, width), width)
                for q in range(pair):
                    part = product[i * width : (i + 1) * width, q * width : (q + 1) * width]
                    value = a_ref[q, here, :] - fill[r, g * pair + q] * part
                    o_ref[q, here, :] = jnp.where(keep[r, g * pair + q] > 0, value, 0.0)
            return carry

        lax.fori_loop(0, nrow // chunk, step, 0)

    @pl.when(some == 0)
    def _():
        o_ref[...] = jnp.zeros(o_ref.shape, F32)

    @pl.when(g == pl.num_programs(0) - 1)
    def _():
        pltpu.make_async_copy(rows_ref, panels_ref, sem).wait()


def trailing(fill, keep, matrix, rows_l, cols_l, pair=2, chunk=4):
    colslots, tall, width = matrix.shape
    depth = rows_l.shape[1]
    return pl.pallas_call(
        functools.partial(schur_kernel, pair, chunk),
        grid=(colslots // pair,),
        in_specs=[
            SMEM,
            SMEM,
            pl.BlockSpec((pair, tall, width), lambda g: (g, 0, 0)),
            pl.BlockSpec((tall, depth), lambda g: (0, 0), pipeline_mode=pl.Buffered(1)),
            pl.BlockSpec((pair, width, depth), lambda g: (g, 0, 0)),
        ],
        out_specs=[pl.BlockSpec((pair, tall, width), lambda g: (g, 0, 0)), pl.BlockSpec(memory_space=pl.ANY)],
        out_shape=[
            jax.ShapeDtypeStruct((colslots, tall, width), F32),
            jax.ShapeDtypeStruct((tall, depth), F32),
        ],
        scratch_shapes=[pltpu.VMEM((tall, depth), BF16), pltpu.VMEM((tall, depth), BF16), pltpu.SemaphoreType.DMA],
        compiler_params=params(),
        name="trailing",
    )(fill, keep, matrix, rows_l, cols_l)


RING = 4


def turn(value, by, size=RING):
    return lax.rem(value + (by + size), size)


class Sends:
    def __init__(self, ssem, rsem):
        self.ssem, self.rsem, self.all = ssem, rsem, []

        self.used = 0

    def plan(self, n, src, dst, patch, col):
        return pltpu.make_async_remote_copy(
            src_ref=src,
            dst_ref=dst,
            send_sem=self.ssem.at[n],
            recv_sem=self.rsem.at[n],
            device_id={"patch": patch, "col": col},
            device_id_type=pl.DeviceIdType.MESH,
        )

    def start(self, src, dst, patch, col):
        copy = self.plan(self.used, src, dst, patch, col)
        self.used += 1
        copy.start()
        self.all.append(copy)
        return copy

    def finish(self):
        for copy in self.all:
            copy.wait_send()


def meet(peers):
    barrier = pltpu.get_barrier_semaphore()
    for patch, col in peers:
        pl.semaphore_signal(
            barrier, inc=1, device_id={"patch": patch, "col": col}, device_id_type=pl.DeviceIdType.MESH
        )
    pl.semaphore_wait(barrier, len(peers))


def col_ring(sends, src, items_ref, patch, col):
    x, core = col // 2, lax.rem(col, 2)
    there = [turn(x, by) * 2 + core for by in range(RING)]
    other = x * 2 + (1 - core)
    half = items_ref.shape[1] // 2
    up = sends.start(src, items_ref.at[col], patch, there[1])
    down = sends.start(src, items_ref.at[col], patch, there[3])
    side = [sends.start(src, items_ref.at[col], patch, other)]
    yield
    up.wait_recv()
    from_down = items_ref.at[there[3]]
    onward = [sends.start(from_down.at[pl.ds(0, half)], from_down.at[pl.ds(0, half)], patch, there[1])]
    side.append(sends.start(from_down, from_down, patch, other))
    down.wait_recv()
    from_up = items_ref.at[there[1]]
    onward.append(sends.start(from_up.at[pl.ds(half, half)], from_up.at[pl.ds(half, half)], patch, there[3]))
    side.append(sends.start(from_up, from_up, patch, other))
    yield
    for copy in onward:
        copy.wait_recv()
    far = items_ref.at[there[2]]
    side.append(sends.start(far, far, patch, other))
    yield
    for copy in side:
        copy.wait_recv()
    yield


def patch_ring(sends, src, items_ref, patch, col, swap):
    y, z = patch // RING, lax.rem(patch, RING)

    def at(first, second):
        i, j = (first, second) if swap else (second, first)
        return turn(y, i) * RING + turn(z, j)

    size = items_ref.shape[1] // 2
    start = size if swap else 0
    whole = pl.ds(start, size)
    parts = (pl.ds(start, size // 2), pl.ds(start + size // 2, size // 2))

    def relay(item, rows, target):
        return sends.start(items_ref.at[item, rows], items_ref.at[item, rows], target, col)

    mine = src.at[whole]
    up = sends.start(mine, items_ref.at[patch, whole], at(1, 0), col)
    down = sends.start(mine, items_ref.at[patch, whole], at(3, 0), col)
    yield
    across = {0: [sends.start(mine, items_ref.at[patch, whole], at(0, by), col) for by in (1, 3)]}
    yield
    up.wait_recv()
    onward = [relay(at(3, 0), parts[0], at(1, 0))]
    across[3] = [relay(at(3, 0), whole, at(0, by)) for by in (1, 3)]
    yield
    down.wait_recv()
    onward.append(relay(at(1, 0), parts[1], at(3, 0)))
    across[1] = [relay(at(1, 0), whole, at(0, by)) for by in (1, 3)]
    yield
    for copy in onward:
        copy.wait_recv()
    across[2] = [relay(at(2, 0), whole, at(0, by)) for by in (1, 3)]
    last = []
    for i in (0, 3, 1, 2):
        yield
        across[i][0].wait_recv()
        last.append(relay(at(i, 3), parts[0], at(0, 1)))
        across[i][1].wait_recv()
        last.append(relay(at(i, 1), parts[1], at(0, 3)))
    yield
    for copy in last:
        copy.wait_recv()
    yield


def interleave(*steps):
    running = list(steps)
    while running:
        running = [one for one in running if next(one, "end") != "end"]


def spread_kernel(
    fill,
    panel_ref,
    uh_ref,
    ul_ref,
    ih_ref,
    il_ref,
    diag_ref,
    rows_ref,
    cols_ref,
    turned_ref,
    own_ref,
    ssem,
    rsem,
    lsem,
):
    patch, col = lax.axis_index("patch"), lax.axis_index("col")
    y, z = patch // RING, lax.rem(patch, RING)
    meet(
        [(patch, turn(col, by, K)) for by in range(1, K)]
        + [(turn(y, by) * RING + z, col) for by in (1, 3)]
        + [(y * RING + turn(z, by), col) for by in (1, 3)]
    )
    sends = Sends(ssem, rsem)
    local = pltpu.make_async_copy(panel_ref.at[col], turned_ref.at[col], lsem.at[0])
    local.start()
    first = [
        sends.start(panel_ref.at[turn(col, by, K)], turned_ref.at[col], patch, turn(col, by, K)) for by in range(1, K)
    ]
    local.wait()
    for copy in first:
        copy.wait_recv()
    solve_row(patch * K + col, fill, turned_ref, uh_ref, ul_ref, ih_ref, il_ref, diag_ref, own_ref)
    local = [
        pltpu.make_async_copy(own_ref, rows_ref.at[col], lsem.at[0]),
        pltpu.make_async_copy(own_ref, cols_ref.at[patch], lsem.at[1]),
    ]
    for copy in local:
        copy.start()
    interleave(
        patch_ring(sends, own_ref, cols_ref, patch, col, False),
        patch_ring(sends, own_ref, cols_ref, patch, col, True),
        col_ring(sends, own_ref, rows_ref, patch, col),
    )
    sends.finish()
    for copy in local:
        copy.wait()


def spread(fill, matrix, factor, npatch, ncol):
    width = matrix.shape[2]
    block = (width, width)
    wide = K * width
    copies = 48 + K - 1
    return pl.pallas_call(
        spread_kernel,
        grid=(1,),
        in_specs=[SMEM, pl.BlockSpec((K,) + block, lambda g: (0, 0, 0))] + [WHOLE] * 5,
        out_specs=[pl.BlockSpec(memory_space=pl.ANY)] * 2,
        out_shape=[
            jax.ShapeDtypeStruct((ncol, width, wide), F32),
            jax.ShapeDtypeStruct((npatch, width, wide), F32),
        ],
        scratch_shapes=[
            pltpu.VMEM((K,) + block, F32),
            pltpu.VMEM((width, wide), F32),
            pltpu.SemaphoreType.DMA((copies,)),
            pltpu.SemaphoreType.DMA((copies,)),
            pltpu.SemaphoreType.DMA((2,)),
        ],
        compiler_params=params(collective_id=1, has_side_effects=True),
        name="spread",
    )(fill, matrix, *factor)


def offsets():
    left = [o for o in itertools.product(range(RING), range(RING), range(RING), range(2)) if any(o)]
    random.Random(3).shuffle(left)

    def links(o):
        return [float(v in (2, want)) for v in o[:3] for want in (1, 3)]

    load, order = [0.0] * 6, []
    while left:
        best = min(left, key=lambda o: max(map(sum, zip(load, links(o)))) - min(map(sum, zip(load, links(o)))))
        left.remove(best)
        order.append(best)
        load = [sum(pair) for pair in zip(load, links(best))]
    return order


batches = (0, 0)


def head_cols(sends, head_ref, patch, col, rest):
    x, core = col // 2, lax.rem(col, 2)
    first = sends.used
    sends.used += 7 * RING

    def copy(by, j, chip, hand, to, across):
        ref = head_ref.at[chip * 2 + hand, pl.ds(2 * j, 2)]
        return sends.plan(first + ((3 + by) if across else (by - 1)) * RING + j, ref, ref, patch, to)

    def out(by, j):
        return copy(by, j, x, core, turn(x, by) * 2 + core, False)

    def side(by, j, hand):
        return copy(by, j, turn(x, RING - by), hand, x * 2 + 1 - core, True)

    def each(by, act):
        for j in range(RING):
            pl.when(j >= turn(x, RING - by))(functools.partial(act, j))

    for by in (1, 3, 2):
        each(0, lambda j: out(by, j).start())
    each(0, lambda j: side(0, j, core).start())
    rest()
    for by in (1, 3, 2):
        def pass_on(j, by=by):
            copy(by, j, turn(x, RING - by), core, turn(x, by) * 2 + core, False).wait_recv()
            side(by, j, core).start()

        each(by, pass_on)
    for by in range(RING):
        each(by, lambda j: side(by, j, 1 - core).wait_recv())

    def finish():
        for by in (1, 3, 2):
            each(0, lambda j: out(by, j).wait_send())
        for by in range(RING):
            each(by, lambda j: side(by, j, core).wait_send())

    return finish


def exchange_kernel(
    npatch,
    slots,
    turns,
    fill,
    x_ref,
    code_ref,
    reg_ref,
    all_ref,
    codes_ref,
    uh_ref,
    ul_ref,
    ih_ref,
    il_ref,
    diag_ref,
    lh_ref,
    li_ref,
    out_ref,
    mine_ref,
    tile_ref,
    row_ref,
    dense_ref,
    part_ref,
    piece_ref,
    head_ref,
    w_ref,
    lt_ref,
    ssem,
    rsem,
    bulk,
    lsem,
):
    patch, col = lax.axis_index("patch"), lax.axis_index("col")
    y, z, x, core = patch // RING, lax.rem(patch, RING), col // 2, lax.rem(col, 2)
    me = patch * K + col
    width = x_ref.shape[2]
    ndevice = npatch * K

    sign = 1 + 2 * core
    peers = []
    for dy, dz, dx, dc in offsets():
        to_patch = lax.rem(y + dy * sign, RING) * RING + lax.rem(z + dz * sign, RING)
        to_col = lax.rem(x + dx * sign, RING) * 2 + lax.rem(core + dc, 2)
        peers.append((to_patch, to_col))
    barrier = pltpu.get_barrier_semaphore()
    for to_patch, to_col in peers:
        pl.semaphore_signal(
            barrier, inc=1, device_id={"patch": to_patch, "col": to_col}, device_id_type=pl.DeviceIdType.MESH
        )

    def pack(d, carry):
        block = x_ref[jnp.maximum(slots[d], 0)]
        out_ref[d] = jnp.where(turns[d] > 0, block.T, block)
        return carry

    lax.fori_loop(0, K, pack, 0)
    row_ref[...] = jnp.broadcast_to(code_ref[...], (8, width))
    pl.semaphore_wait(barrier, len(peers))

    sends = Sends(ssem, rsem)

    def flow(count):
        for to_patch, to_col in peers[flow.done : flow.done + count]:
            pltpu.make_async_remote_copy(
                src_ref=out_ref.at[to_patch * K + to_col],
                dst_ref=all_ref.at[me],
                send_sem=bulk.at[0],
                recv_sem=bulk.at[1],
                device_id={"patch": to_patch, "col": to_col},
                device_id_type=pl.DeviceIdType.MESH,
            ).start()
        flow.done += count

    flow.done = 0

    local = [
        pltpu.make_async_copy(out_ref.at[col], mine_ref.at[col], lsem.at[0]),
        pltpu.make_async_copy(row_ref, tile_ref.at[col], lsem.at[1]),
    ]
    for copy in local:
        copy.start()
    first = []
    for by in range(1, K):
        to = turn(col, by, K)
        first.append(sends.start(row_ref, tile_ref.at[col], patch, to))
        first.append(sends.start(out_ref.at[to], mine_ref.at[col], patch, to))
    lax.fori_loop(K, ndevice, pack, 0)
    own = pltpu.make_async_copy(out_ref.at[me], all_ref.at[me], lsem.at[2])
    own.start()
    for copy in local:
        copy.wait()
    for copy in first:
        copy.wait_recv()
    reg = jnp.broadcast_to(reg_ref[...], (8, width))
    sub = lax.broadcasted_iota(jnp.int32, (8, width), 0)
    lane = lax.broadcasted_iota(jnp.int32, (8, width), 1)
    codes = []
    tile = jnp.zeros((8, width), F32)
    for c in range(K):
        row = tile_ref[c]
        tile = jnp.where(sub == c, row, tile)
        codes.append(jnp.broadcast_to(jnp.sum(jnp.where(lane == col, row, 0.0), 1, keepdims=True), (8, width)))
    for r in range(K):
        hits = [code == r for code in codes]
        shift = jnp.where((patch == 0) & (col == r), reg, 0.0)
        for q in range(npatch):
            total = jnp.where(lane == sub + q * 8, shift, 0.0)
            for c in range(K):
                total = total + jnp.where(hits[c], mine_ref[c, q * 8 : (q + 1) * 8, :], 0.0)
            dense_ref[q, r] = total
    here = pl.ds(pl.multiple_of(patch * 8, 8), 8)
    codes_ref[here, :] = tile
    second = []
    tables = []
    for by in range(1, npatch):
        to = turn(patch, by, npatch)
        second.append(sends.start(dense_ref.at[to], part_ref.at[by - 1], to, col))
    for by in range(1, npatch):
        tables.append(sends.start(codes_ref.at[here, :], codes_ref.at[here, :], turn(patch, by, npatch), col))
    flow(batches[0])
    total = dense_ref[patch]
    for by, copy in enumerate(second):
        copy.wait_recv()
        total = total + part_ref[by]
    piece_ref[...] = total
    local = pltpu.make_async_copy(piece_ref, head_ref.at[col, :, here, :], lsem.at[0])
    local.start()
    third = [
        sends.start(piece_ref, head_ref.at[col, :, here, :], turn(patch, by, npatch), col) for by in range(1, npatch)
    ]
    flow(batches[1])
    local.wait()
    for copy in third:
        copy.wait_recv()
    finish = head_cols(sends, head_ref, patch, col, lambda: flow(len(peers) - flow.done))

    factor_head(fill, head_ref, lh_ref, li_ref, w_ref, lt_ref)
    hand_on(lh_ref, li_ref, uh_ref, ul_ref, ih_ref, il_ref, diag_ref)

    finish()
    sends.finish()
    for copy in tables:
        copy.wait_recv()
    own.wait()
    every = pl.ds(0, ndevice - 1)
    whole = pltpu.make_async_remote_copy(
        src_ref=out_ref.at[every],
        dst_ref=all_ref.at[every],
        send_sem=bulk.at[0],
        recv_sem=bulk.at[1],
        device_id={"patch": peers[0][0], "col": peers[0][1]},
        device_id_type=pl.DeviceIdType.MESH,
    )
    whole.wait_send()
    whole.wait_recv()


def exchange(slots, turns, codes, fill, contributions, reg, npatch):
    width = contributions.shape[2]
    ndevice = npatch * K
    copies = 2 * (K - 1) + 3 * (npatch - 1) + 7 * RING
    rows = width // npatch
    block = (width, width)
    return pl.pallas_call(
        functools.partial(exchange_kernel, npatch),
        in_specs=[SMEM, SMEM, SMEM, WHOLE, WHOLE, WHOLE],
        out_specs=[pl.BlockSpec(memory_space=pl.ANY)] + [WHOLE] * 6,
        out_shape=[
            jax.ShapeDtypeStruct((ndevice,) + block, F32),
            jax.ShapeDtypeStruct((ndevice, ndevice), F32),
            jax.ShapeDtypeStruct((K, width, K * width), BF16),
            jax.ShapeDtypeStruct((K, width, K * width), BF16),
            jax.ShapeDtypeStruct((K,) + block, BF16),
            jax.ShapeDtypeStruct((K,) + block, BF16),
            jax.ShapeDtypeStruct((K,) + block, F32),
        ],
        scratch_shapes=[
            pltpu.VMEM((K, K * width, width), F32),
            pltpu.VMEM((K,) + block, F32),
            pltpu.VMEM((ndevice,) + block, F32),
            pltpu.VMEM((K,) + block, F32),
            pltpu.VMEM((K, 8, width), F32),
            pltpu.VMEM((8, width), F32),
            pltpu.VMEM((npatch, K, rows, width), F32),
            pltpu.VMEM((npatch - 1, K, rows, width), F32),
            pltpu.VMEM((K, rows, width), F32),
            pltpu.VMEM((K, K) + block, F32),
            pltpu.VMEM((width, 2 * width), F32),
            pltpu.VMEM(block, F32),
            pltpu.SemaphoreType.DMA((copies,)),
            pltpu.SemaphoreType.DMA((copies,)),
            pltpu.SemaphoreType.DMA((2,)),
            pltpu.SemaphoreType.DMA((3,)),
        ],
        compiler_params=params(collective_id=0, has_side_effects=True),
        name="exchange",
    )(slots, turns, fill, contributions, codes, reg)


def route(targets, counts, pivot, rowblk, ncol, ndevice):
    slots = targets.shape[0]
    blocks = jnp.arange(pivot.shape[0], dtype=jnp.int32)
    position = jnp.sum(jnp.where(targets[:, :, None] == blocks, pivot, 0), 2)
    pos_first, pos_second = position[:, 0], position[:, 1]
    upper_pos = jnp.maximum(pos_first, pos_second)
    lower_pos = jnp.minimum(pos_first, pos_second)
    number = jnp.arange(slots, dtype=jnp.int32)
    live = number < counts[0]
    owner = upper_pos // rowblk * ncol + lower_pos % ncol
    select = (owner[:, None] == jnp.arange(ndevice, dtype=jnp.int32)[None, :]) & live[:, None]
    turned = (pos_first < pos_second).astype(jnp.int32)
    code = lower_pos // ncol * rowblk + upper_pos % rowblk

    def pick(value):
        return jnp.max(jnp.where(select, value[:, None], -1), 0)

    return pick(number), pick(turned), pick(code).astype(F32)[None, :]


def body(contributions, targets, counts, pivot, fill_draw, regular):
    width = contributions.shape[1]
    npatch = lax.axis_size("patch")
    ncol = lax.axis_size("col")
    ndevice = npatch * ncol
    nblock = pivot.shape[0]
    rowblk = regular.shape[0] // width
    colslots = nblock // ncol
    patch_id = lax.axis_index("patch")
    col_id = lax.axis_index("col")

    slots, turns, codes = route(targets, counts, pivot, rowblk, ncol, ndevice)
    reg = lax.dynamic_slice_in_dim(regular, col_id * width, width, 0)[None, :]
    corner = fill_draw[:K, :K]
    corner = jnp.maximum(jnp.maximum(corner, corner.T), jnp.eye(K, dtype=jnp.int32)).astype(F32)
    got, table, *factor = exchange(slots, turns, codes, corner, contributions, reg, npatch)

    drawn = fill_draw.astype(F32)
    pattern = jnp.maximum(jnp.maximum(drawn, drawn.T), jnp.eye(nblock, dtype=F32))
    diag = (patch_id * rowblk + col_id).astype(jnp.int32)[None]
    codes = lax.dynamic_slice_in_dim(table, diag[0], 1, 1)[:, 0].astype(jnp.int32)
    matrix = place(codes, diag, got, reg)

    row_fill = lax.dynamic_slice(pattern, (diag[0], 0), (1, K))
    rows_l, cols_l = spread(row_fill, matrix, factor, npatch, ncol)
    rows_l = rows_l.reshape(rowblk * width, K * width)

    grow = patch_id * rowblk + jnp.arange(rowblk, dtype=jnp.int32)
    gcol = jnp.arange(colslots, dtype=jnp.int32) * ncol + col_id
    keep = ((grow[:, None] >= gcol[None, :]) & (gcol >= K)[None, :]).astype(jnp.int32)
    band = lax.dynamic_slice_in_dim(pattern, patch_id * rowblk, rowblk, 0).reshape(rowblk, colslots, ncol)
    local_fill = lax.dynamic_index_in_dim(band, col_id, 2, keepdims=False)
    schur, panels = trailing(local_fill, keep, matrix.reshape(colslots, rowblk * width, width), rows_l, cols_l)
    return (panels, schur.reshape(colslots, 1, rowblk * width, width))


def solution(mesh):
    in_specs = (
        P(("patch", "col"), None, None),
        P(("patch", "col"), None),
        P(("patch", "col")),
        P(),
        P(),
        P("patch"),
    )
    out_specs = (P("patch", None), P(None, "col", "patch", None))
    return jax.shard_map(body, mesh=mesh, in_specs=in_specs, out_specs=out_specs, check_vma=False)
```

```python
import functools
import itertools
import random

import jax
import jax.numpy as jnp
from jax import lax
from jax.experimental import pallas as pl
from jax.experimental.pallas import tpu as pltpu
from jax.sharding import PartitionSpec as P

K = 8
HIGH = lax.Precision.HIGHEST
F32 = jnp.float32
BF16 = jnp.bfloat16
VMEM_BYTES = 60 * 1024 * 1024
SMEM = pl.BlockSpec(memory_space=pltpu.SMEM)
WHOLE = pl.BlockSpec(memory_space=pltpu.VMEM)
ANY = pl.BlockSpec(memory_space=pl.ANY)
NT = (((1,), (1,)), ((), ()))
TN = (((0,), (0,)), ((), ()))


def params(**more):
    return pltpu.CompilerParams(vmem_limit_bytes=VMEM_BYTES, **more)


def dot_nt(a, b):
    return lax.dot_general(a, b, NT, precision=HIGH, preferred_element_type=F32)


def eye_mask(n):
    return lax.broadcasted_iota(jnp.int32, (n, n), 0) == lax.broadcasted_iota(jnp.int32, (n, n), 1)


def weight(drawn, i, j):
    return jnp.where(i == j, 1, jnp.maximum(drawn[i, j], drawn[j, i])).astype(F32)


def place_kernel(per, last, codes, diag, x_ref, reg_ref, o_ref):
    g = pl.program_id(0)
    width = x_ref.shape[2]

    @pl.when(g == 0)
    def _():
        def clear(q, carry):
            o_ref[q] = jnp.zeros((width, width), F32)
            return carry

        lax.fori_loop(0, o_ref.shape[0], clear, 0)

    def step(t, carry):
        code = codes[g * per + t]

        @pl.when(code >= 0)
        def _():
            o_ref[code] += x_ref[t]

        return carry

    lax.fori_loop(0, per, step, 0)

    @pl.when(g == last)
    def _():
        block = o_ref[diag[0]]
        o_ref[diag[0]] = 0.5 * (block + block.T) + jnp.where(eye_mask(width), reg_ref[...], 0.0)


def place(codes, diag, got, reg, per=16):
    ndevice, _, width = got.shape
    places = 128
    return pl.pallas_call(
        functools.partial(place_kernel, per, ndevice // per - 1),
        grid=(ndevice // per,),
        in_specs=[SMEM, SMEM, pl.BlockSpec((per, width, width), lambda g: (g, 0, 0)), pl.BlockSpec((1, width), lambda g: (0, 0))],
        out_specs=pl.BlockSpec((places, width, width), lambda g: (0, 0, 0), pipeline_mode=pl.Buffered(1)),
        out_shape=jax.ShapeDtypeStruct((places, width, width), F32),
        compiler_params=params(),
        name="place",
    )(codes, diag, got, reg)


def split3(a):
    one = a.astype(BF16).astype(F32)
    rest = a - one
    two = rest.astype(BF16).astype(F32)
    return one, two, rest - two


def chol_inverse(w_ref, lt_ref):
    width = w_ref.shape[0]
    sub = lax.broadcasted_iota(jnp.int32, (8, width), 0)
    lane = lax.broadcasted_iota(jnp.int32, (8, width), 1)
    for base in range(0, width, 8):
        both = w_ref[base : base + 8, :]
        rows = both[:, :width]
        unit = both[:, width:]
        cols = [jnp.broadcast_to(rows[:, base + j : base + j + 1], (8, width)) for j in range(8)]
        scale = jnp.zeros((8, width), F32)
        for j in range(8):
            root = lax.rsqrt(cols[j][j : j + 1, :])
            lower = cols[j] * root
            for i in range(j + 1, 8):
                cols[i] = cols[i] - lower * lower[i : i + 1, :]
            below = jnp.where(sub > j, lower, 0.0)
            rows = rows - below * (rows[j : j + 1, :] * root)
            unit = unit - below * (unit[j : j + 1, :] * root)
            scale = jnp.where(sub == j, root, scale)
        upper = jnp.where(lane >= sub + base, rows * scale, 0.0)
        unit = unit * scale
        lt_ref[base : base + 8, :] = upper
        w_ref[base : base + 8, width:] = unit
        if base + 8 < width:
            u1, u2, u3 = split3(upper)
            v1, v2, v3 = split3(unit)
            left = jnp.concatenate([u1, u1, u2, u2, u1, u3], 0).astype(BF16)
            w1, w2, w3 = (jnp.concatenate([a, b], 1) for a, b in ((u1, v1), (u2, v2), (u3, v3)))
            right = jnp.concatenate([w1, w2, w1, w2, w3, w1], 0).astype(BF16)
            change = lax.dot_general(left, right, TN, preferred_element_type=F32)
            w_ref[base + 8 :, :] -= change[base + 8 :, :]


def factor_head(fill, head_ref, lh_ref, li_ref, w_ref, lt_ref):
    width = head_ref.shape[2]
    eye = jnp.where(eye_mask(width), 1.0, 0.0).astype(F32)
    for c in range(K):
        for r in range(K):
            at = slice(r * width, (r + 1) * width)
            if r < c:
                lh_ref[c, at, :] = jnp.zeros((width, width), F32)
                continue
            block = head_ref[c, r]
            lh_ref[c, at, :] = 0.5 * (block + block.T) if r == c else block

    def step(k, carry):
        w_ref[:, :width] = lh_ref[k, pl.ds(pl.multiple_of(k * width, width), width), :]
        w_ref[:, width:] = eye
        chol_inverse(w_ref, lt_ref)
        li_ref[k] = w_ref[:, width:]
        lh_ref[k, pl.ds(pl.multiple_of(k * width, width), width), :] = lt_ref[...].T
        for s in range(K - 1):

            @pl.when(k == s)
            def _(s=s):
                below = slice((s + 1) * width, K * width)
                solved = dot_nt(lh_ref[s, below, :], li_ref[s])
                lh_ref[s, below, :] = solved
                for j in range(s + 1, K):
                    part = solved[(j - s - 1) * width :]
                    change = dot_nt(part, part[:width])
                    for i in range(j, K):
                        at = slice(i * width, (i + 1) * width)
                        lh_ref[j, at, :] -= weight(fill, i, j) * change[(i - j) * width : (i - j + 1) * width]

        return carry

    lax.fori_loop(0, K, step, 0)


def split2(a):
    hi = a.astype(BF16)
    return hi, (a - hi.astype(F32)).astype(BF16)


def hand_on(lh_ref, li_ref, uh_ref, ul_ref, ih_ref, il_ref, diag_ref):
    width = lh_ref.shape[2]

    def column(k, carry):
        diag_ref[k] = lh_ref[k, pl.ds(pl.multiple_of(k * width, width), width), :]
        ih_ref[k], il_ref[k] = split2(li_ref[k].T)

        def row(i, carry):
            at = pl.ds(pl.multiple_of(i * width, width), width)
            uh_ref[k, :, at], ul_ref[k, :, at] = split2(lh_ref[k, at, :].T)
            return carry

        return lax.fori_loop(k + 1, K, row, carry)

    lax.fori_loop(0, K, column, 0)


def dot3(a, b_hi, b_lo):
    a_hi, a_lo = split2(a)
    product = jnp.dot(a_hi, b_hi, preferred_element_type=F32)
    product += jnp.dot(a_lo, b_hi, preferred_element_type=F32)
    return product + jnp.dot(a_hi, b_lo, preferred_element_type=F32)


def solve_row(row, fill, a_ref, uh_ref, ul_ref, ih_ref, il_ref, diag_ref, o_ref):
    width = a_ref.shape[1]
    work = [a_ref[k] for k in range(K)]
    for k in range(K):
        solved = dot3(work[k], ih_ref[k], il_ref[k])
        solved = jnp.where(row > k, solved, jnp.where(row == k, diag_ref[k], 0.0))
        o_ref[:, k * width : (k + 1) * width] = solved
        if k + 1 < K:
            change = dot3(solved, uh_ref[k, :, (k + 1) * width :], ul_ref[k, :, (k + 1) * width :])
            for j in range(k + 1, K):
                work[j] = work[j] - weight(fill, row, j) * change[:, (j - k - 1) * width : (j - k) * width]


def schur_kernel(pair, chunk, fill, a_ref, rows_ref, cols_ref, o_ref, panels_ref, hi_ref, lo_ref, sem):
    g = pl.program_id(0)
    width = a_ref.shape[2]
    nrow = a_ref.shape[1] // width
    grow = lax.axis_index("patch") * nrow
    gcol = [(g * pair + q) * K + lax.axis_index("col") for q in range(pair)]

    @pl.when(g == 0)
    def _():
        pltpu.make_async_copy(rows_ref, panels_ref, sem).start()

        def split(r, carry):
            at = pl.ds(pl.multiple_of(r * width, width), width)
            rows = rows_ref[at, :]
            hi = rows.astype(BF16)
            hi_ref[at, :] = hi
            lo_ref[at, :] = (rows - hi.astype(F32)).astype(BF16)
            return carry

        lax.fori_loop(0, nrow, split, 0)

    cols = cols_ref[...].reshape(pair * width, cols_ref.shape[2])
    col_hi = cols.astype(BF16)
    col_lo = (cols - col_hi.astype(F32)).astype(BF16)

    some = (grow + nrow > gcol[0]) & (gcol[pair - 1] >= K)

    @pl.when(some)
    def _():
        def step(m, carry):
            at = pl.ds(pl.multiple_of(m * chunk * width, chunk * width), chunk * width)
            hi = hi_ref[at, :]
            product = lax.dot_general(hi, col_hi, NT, preferred_element_type=F32)
            product += lax.dot_general(hi, col_lo, NT, preferred_element_type=F32)
            product += lax.dot_general(lo_ref[at, :], col_hi, NT, preferred_element_type=F32)
            for i in range(chunk):
                r = m * chunk + i
                here = pl.ds(pl.multiple_of(r * width, width), width)
                for q in range(pair):
                    part = product[i * width : (i + 1) * width, q * width : (q + 1) * width]
                    value = a_ref[q, here, :] - weight(fill, grow + r, gcol[q]) * part
                    o_ref[q, here, :] = jnp.where((grow + r >= gcol[q]) & (gcol[q] >= K), value, 0.0)
            return carry

        lax.fori_loop(0, nrow // chunk, step, 0)

    @pl.when(jnp.logical_not(some))
    def _():
        o_ref[...] = jnp.zeros(o_ref.shape, F32)

    @pl.when(g == pl.num_programs(0) - 1)
    def _():
        pltpu.make_async_copy(rows_ref, panels_ref, sem).wait()


def trailing(fill, matrix, rows_l, cols_l, pair=2, chunk=4):
    colslots, tall, width = matrix.shape
    depth = rows_l.shape[1]
    return pl.pallas_call(
        functools.partial(schur_kernel, pair, chunk),
        grid=(colslots // pair,),
        in_specs=[
            SMEM,
            pl.BlockSpec((pair, tall, width), lambda g: (g, 0, 0)),
            pl.BlockSpec((tall, depth), lambda g: (0, 0), pipeline_mode=pl.Buffered(1)),
            pl.BlockSpec((pair, width, depth), lambda g: (g, 0, 0)),
        ],
        out_specs=[pl.BlockSpec((pair, tall, width), lambda g: (g, 0, 0)), pl.BlockSpec(memory_space=pl.ANY)],
        out_shape=[
            jax.ShapeDtypeStruct((colslots, tall, width), F32),
            jax.ShapeDtypeStruct((tall, depth), F32),
        ],
        scratch_shapes=[pltpu.VMEM((tall, depth), BF16), pltpu.VMEM((tall, depth), BF16), pltpu.SemaphoreType.DMA],
        compiler_params=params(),
        name="trailing",
    )(fill, matrix, rows_l, cols_l)


RING = 4


def turn(value, by, size=RING):
    return lax.rem(value + (by + size), size)


class Sends:
    def __init__(self, ssem, rsem):
        self.ssem, self.rsem, self.all = ssem, rsem, []

        self.used = 0

    def plan(self, n, src, dst, patch, col):
        return pltpu.make_async_remote_copy(
            src_ref=src,
            dst_ref=dst,
            send_sem=self.ssem.at[n],
            recv_sem=self.rsem.at[n],
            device_id={"patch": patch, "col": col},
            device_id_type=pl.DeviceIdType.MESH,
        )

    def start(self, src, dst, patch, col):
        copy = self.plan(self.used, src, dst, patch, col)
        self.used += 1
        copy.start()
        self.all.append(copy)
        return copy

    def finish(self):
        for copy in self.all:
            copy.wait_send()


def meet(peers):
    barrier = pltpu.get_barrier_semaphore()
    for patch, col in peers:
        pl.semaphore_signal(
            barrier, inc=1, device_id={"patch": patch, "col": col}, device_id_type=pl.DeviceIdType.MESH
        )
    pl.semaphore_wait(barrier, len(peers))


def col_ring(sends, src, items_ref, patch, col):
    x, core = col // 2, lax.rem(col, 2)
    there = [turn(x, by) * 2 + core for by in range(RING)]
    other = x * 2 + (1 - core)
    half = items_ref.shape[1] // 2
    up = sends.start(src, items_ref.at[col], patch, there[1])
    down = sends.start(src, items_ref.at[col], patch, there[3])
    side = [sends.start(src, items_ref.at[col], patch, other)]
    yield
    up.wait_recv()
    from_down = items_ref.at[there[3]]
    onward = [sends.start(from_down.at[pl.ds(0, half)], from_down.at[pl.ds(0, half)], patch, there[1])]
    side.append(sends.start(from_down, from_down, patch, other))
    down.wait_recv()
    from_up = items_ref.at[there[1]]
    onward.append(sends.start(from_up.at[pl.ds(half, half)], from_up.at[pl.ds(half, half)], patch, there[3]))
    side.append(sends.start(from_up, from_up, patch, other))
    yield
    for copy in onward:
        copy.wait_recv()
    far = items_ref.at[there[2]]
    side.append(sends.start(far, far, patch, other))
    yield
    for copy in side:
        copy.wait_recv()
    yield


def patch_ring(sends, src, items_ref, patch, col, swap):
    y, z = patch // RING, lax.rem(patch, RING)

    def at(first, second):
        i, j = (first, second) if swap else (second, first)
        return turn(y, i) * RING + turn(z, j)

    size = items_ref.shape[1] // 2
    start = size if swap else 0
    whole = pl.ds(start, size)
    parts = (pl.ds(start, size // 2), pl.ds(start + size // 2, size // 2))

    def relay(item, rows, target):
        return sends.start(items_ref.at[item, rows], items_ref.at[item, rows], target, col)

    mine = src.at[whole]
    up = sends.start(mine, items_ref.at[patch, whole], at(1, 0), col)
    down = sends.start(mine, items_ref.at[patch, whole], at(3, 0), col)
    yield
    across = {0: [sends.start(mine, items_ref.at[patch, whole], at(0, by), col) for by in (1, 3)]}
    yield
    up.wait_recv()
    onward = [relay(at(3, 0), parts[0], at(1, 0))]
    across[3] = [relay(at(3, 0), whole, at(0, by)) for by in (1, 3)]
    yield
    down.wait_recv()
    onward.append(relay(at(1, 0), parts[1], at(3, 0)))
    across[1] = [relay(at(1, 0), whole, at(0, by)) for by in (1, 3)]
    yield
    for copy in onward:
        copy.wait_recv()
    across[2] = [relay(at(2, 0), whole, at(0, by)) for by in (1, 3)]
    last = []
    for i in (0, 3, 1, 2):
        yield
        across[i][0].wait_recv()
        last.append(relay(at(i, 3), parts[0], at(0, 1)))
        across[i][1].wait_recv()
        last.append(relay(at(i, 1), parts[1], at(0, 3)))
    yield
    for copy in last:
        copy.wait_recv()
    yield


def interleave(*steps):
    running = list(steps)
    while running:
        running = [one for one in running if next(one, "end") != "end"]


def spread_kernel(
    fill,
    panel_ref,
    *refs,
):
    stored, (rows_ref, cols_ref), held, rest = refs[:5], refs[5:7], refs[7:12], refs[12:]
    turned_ref, own_ref, ssem, rsem, lsem = rest
    patch, col = lax.axis_index("patch"), lax.axis_index("col")
    y, z = patch // RING, lax.rem(patch, RING)
    loads = [pltpu.make_async_copy(a, b, lsem.at[2 + n]) for n, (a, b) in enumerate(zip(stored, held))]
    for copy in loads:
        copy.start()
    meet(
        [(patch, turn(col, by, K)) for by in range(1, K)]
        + [(turn(y, by) * RING + z, col) for by in (1, 3)]
        + [(y * RING + turn(z, by), col) for by in (1, 3)]
    )
    sends = Sends(ssem, rsem)
    local = pltpu.make_async_copy(panel_ref.at[col], turned_ref.at[col], lsem.at[0])
    local.start()
    first = [
        sends.start(panel_ref.at[turn(col, by, K)], turned_ref.at[col], patch, turn(col, by, K)) for by in range(1, K)
    ]
    local.wait()
    for copy in first:
        copy.wait_recv()
    for copy in loads:
        copy.wait()
    solve_row(patch * K + col, fill, turned_ref, *held, own_ref)
    local = [
        pltpu.make_async_copy(own_ref, rows_ref.at[col], lsem.at[0]),
        pltpu.make_async_copy(own_ref, cols_ref.at[patch], lsem.at[1]),
    ]
    for copy in local:
        copy.start()
    interleave(
        patch_ring(sends, own_ref, cols_ref, patch, col, False),
        patch_ring(sends, own_ref, cols_ref, patch, col, True),
        col_ring(sends, own_ref, rows_ref, patch, col),
    )
    sends.finish()
    for copy in local:
        copy.wait()


def spread(fill, matrix, factor, npatch, ncol):
    width = matrix.shape[2]
    block = (width, width)
    wide = K * width
    copies = 48 + K - 1
    return pl.pallas_call(
        spread_kernel,
        grid=(1,),
        in_specs=[SMEM, pl.BlockSpec((K,) + block, lambda g: (0, 0, 0))]
        + [pl.BlockSpec(memory_space=pl.ANY)] * 5,
        out_specs=[pl.BlockSpec(memory_space=pl.ANY)] * 2,
        out_shape=[
            jax.ShapeDtypeStruct((ncol, width, wide), F32),
            jax.ShapeDtypeStruct((npatch, width, wide), F32),
        ],
        scratch_shapes=[pltpu.VMEM(part.shape, part.dtype) for part in factor]
        + [
            pltpu.VMEM((K,) + block, F32),
            pltpu.VMEM((width, wide), F32),
            pltpu.SemaphoreType.DMA((copies,)),
            pltpu.SemaphoreType.DMA((copies,)),
            pltpu.SemaphoreType.DMA((7,)),
        ],
        compiler_params=params(collective_id=1, has_side_effects=True),
        name="spread",
    )(fill, matrix, *factor)


def offsets():
    left = [o for o in itertools.product(range(RING), range(RING), range(RING), range(2)) if any(o)]
    random.Random(3).shuffle(left)

    def links(o):
        return [float(v in (2, want)) for v in o[:3] for want in (1, 3)]

    load, order = [0.0] * 6, []
    while left:
        best = min(left, key=lambda o: max(map(sum, zip(load, links(o)))) - min(map(sum, zip(load, links(o)))))
        left.remove(best)
        order.append(best)
        load = [sum(pair) for pair in zip(load, links(best))]
    return order


batches = (0, 30)


def head_cols(sends, head_ref, patch, col, rest):
    x, core = col // 2, lax.rem(col, 2)
    first = sends.used
    sends.used += 7 * RING

    def copy(by, j, chip, hand, to, across):
        ref = head_ref.at[chip * 2 + hand, pl.ds(2 * j, 2)]
        return sends.plan(first + ((3 + by) if across else (by - 1)) * RING + j, ref, ref, patch, to)

    def out(by, j):
        return copy(by, j, x, core, turn(x, by) * 2 + core, False)

    def side(by, j, hand):
        return copy(by, j, turn(x, RING - by), hand, x * 2 + 1 - core, True)

    def each(by, act):
        for j in range(RING):
            pl.when(j >= turn(x, RING - by))(functools.partial(act, j))

    for by in (1, 3, 2):
        each(0, lambda j: out(by, j).start())
    each(0, lambda j: side(0, j, core).start())
    rest()
    for by in (1, 3, 2):
        def pass_on(j, by=by):
            copy(by, j, turn(x, RING - by), core, turn(x, by) * 2 + core, False).wait_recv()
            side(by, j, core).start()

        each(by, pass_on)
    for by in range(RING):
        each(by, lambda j: side(by, j, 1 - core).wait_recv())

    def finish():
        for by in (1, 3, 2):
            each(0, lambda j: out(by, j).wait_send())
        for by in range(RING):
            each(by, lambda j: side(by, j, core).wait_send())

    return finish


def exchange_kernel(
    npatch,
    slots,
    turns,
    fill,
    given_ref,
    code_ref,
    reg_ref,
    all_ref,
    codes_ref,
    *refs,
):
    stored, held, rest = refs[:5], refs[5:10], refs[10:]
    exchange_steps(
        npatch, slots, turns, fill, given_ref, code_ref, reg_ref, all_ref, codes_ref, stored, held, *rest
    )


def exchange_steps(
    npatch,
    slots,
    turns,
    fill,
    given_ref,
    code_ref,
    reg_ref,
    all_ref,
    codes_ref,
    stored,
    held,
    x_ref,
    lh_ref,
    li_ref,
    out_ref,
    mine_ref,
    tile_ref,
    row_ref,
    dense_ref,
    part_ref,
    piece_ref,
    head_ref,
    w_ref,
    lt_ref,
    ssem,
    rsem,
    bulk,
    lsem,
):
    patch, col = lax.axis_index("patch"), lax.axis_index("col")
    y, z, x, core = patch // RING, lax.rem(patch, RING), col // 2, lax.rem(col, 2)
    me = patch * K + col
    width = x_ref.shape[2]
    ndevice = npatch * K
    load = pltpu.make_async_copy(given_ref, x_ref, lsem.at[3])
    load.start()

    sign = 1 + 2 * core
    peers = []
    for dy, dz, dx, dc in offsets():
        to_patch = lax.rem(y + dy * sign, RING) * RING + lax.rem(z + dz * sign, RING)
        to_col = lax.rem(x + dx * sign, RING) * 2 + lax.rem(core + dc, 2)
        peers.append((to_patch, to_col))
    barrier = pltpu.get_barrier_semaphore()
    for to_patch, to_col in peers:
        pl.semaphore_signal(
            barrier, inc=1, device_id={"patch": to_patch, "col": to_col}, device_id_type=pl.DeviceIdType.MESH
        )

    def pack(d, carry):
        block = x_ref[jnp.maximum(slots[d], 0)]
        out_ref[d] = jnp.where(turns[d] > 0, block.T, block)
        return carry

    load.wait()
    lax.fori_loop(0, K, pack, 0)
    row_ref[...] = jnp.broadcast_to(code_ref[...], (8, width))
    pl.semaphore_wait(barrier, len(peers))

    sends = Sends(ssem, rsem)

    def flow(count):
        for to_patch, to_col in peers[flow.done : flow.done + count]:
            pltpu.make_async_remote_copy(
                src_ref=out_ref.at[to_patch * K + to_col],
                dst_ref=all_ref.at[me],
                send_sem=bulk.at[0],
                recv_sem=bulk.at[1],
                device_id={"patch": to_patch, "col": to_col},
                device_id_type=pl.DeviceIdType.MESH,
            ).start()
        flow.done += count

    flow.done = 0

    local = [
        pltpu.make_async_copy(out_ref.at[col], mine_ref.at[col], lsem.at[0]),
        pltpu.make_async_copy(row_ref, tile_ref.at[col], lsem.at[1]),
    ]
    for copy in local:
        copy.start()
    first = []
    for by in range(1, K):
        to = turn(col, by, K)
        first.append(sends.start(row_ref, tile_ref.at[col], patch, to))
        first.append(sends.start(out_ref.at[to], mine_ref.at[col], patch, to))
    lax.fori_loop(K, ndevice, pack, 0)
    own = pltpu.make_async_copy(out_ref.at[me], all_ref.at[me], lsem.at[2])
    own.start()
    for copy in local:
        copy.wait()
    for copy in first:
        copy.wait_recv()
    reg = jnp.broadcast_to(reg_ref[...], (8, width))
    sub = lax.broadcasted_iota(jnp.int32, (8, width), 0)
    lane = lax.broadcasted_iota(jnp.int32, (8, width), 1)
    codes = []
    tile = jnp.zeros((8, width), F32)
    for c in range(K):
        row = tile_ref[c]
        tile = jnp.where(sub == c, row, tile)
        codes.append(jnp.broadcast_to(jnp.sum(jnp.where(lane == col, row, 0.0), 1, keepdims=True), (8, width)))
    for r in range(K):
        hits = [code == r for code in codes]
        shift = jnp.where((patch == 0) & (col == r), reg, 0.0)
        for q in range(npatch):
            total = jnp.where(lane == sub + q * 8, shift, 0.0)
            for c in range(K):
                total = total + jnp.where(hits[c], mine_ref[c, q * 8 : (q + 1) * 8, :], 0.0)
            dense_ref[q, r] = total
    here = pl.ds(pl.multiple_of(patch * 8, 8), 8)
    codes_ref[here, :] = tile
    second = []
    tables = []
    for by in range(1, npatch):
        to = turn(patch, by, npatch)
        second.append(sends.start(dense_ref.at[to], part_ref.at[by - 1], to, col))
    for by in range(1, npatch):
        tables.append(sends.start(codes_ref.at[here, :], codes_ref.at[here, :], turn(patch, by, npatch), col))
    flow(batches[0])
    total = dense_ref[patch]
    for by, copy in enumerate(second):
        copy.wait_recv()
        total = total + part_ref[by]
    piece_ref[...] = total
    local = pltpu.make_async_copy(piece_ref, head_ref.at[col, :, here, :], lsem.at[0])
    local.start()
    third = [
        sends.start(piece_ref, head_ref.at[col, :, here, :], turn(patch, by, npatch), col) for by in range(1, npatch)
    ]
    flow(batches[1])
    local.wait()
    for copy in third:
        copy.wait_recv()
    finish = head_cols(sends, head_ref, patch, col, lambda: flow(len(peers) - flow.done))

    factor_head(fill, head_ref, lh_ref, li_ref, w_ref, lt_ref)
    hand_on(lh_ref, li_ref, *held)
    stores = [pltpu.make_async_copy(b, a, lsem.at[4 + n]) for n, (a, b) in enumerate(zip(stored, held))]
    for copy in stores:
        copy.start()

    finish()
    sends.finish()
    for copy in tables:
        copy.wait_recv()
    own.wait()
    for copy in stores:
        copy.wait()
    every = pl.ds(0, ndevice - 1)
    whole = pltpu.make_async_remote_copy(
        src_ref=out_ref.at[every],
        dst_ref=all_ref.at[every],
        send_sem=bulk.at[0],
        recv_sem=bulk.at[1],
        device_id={"patch": peers[0][0], "col": peers[0][1]},
        device_id_type=pl.DeviceIdType.MESH,
    )
    whole.wait_send()
    whole.wait_recv()


def exchange(slots, turns, codes, fill, contributions, reg, npatch):
    width = contributions.shape[2]
    ndevice = npatch * K
    copies = 2 * (K - 1) + 3 * (npatch - 1) + 7 * RING
    wide, one = (K, width, K * width), (K, width, width)
    factor = ((wide, BF16), (wide, BF16), (one, BF16), (one, BF16), (one, F32))
    rows = width // npatch
    block = (width, width)
    return pl.pallas_call(
        functools.partial(exchange_kernel, npatch),
        in_specs=[SMEM, SMEM, SMEM, ANY, WHOLE, WHOLE],
        out_specs=[ANY, WHOLE] + [ANY] * 5,
        out_shape=[
            jax.ShapeDtypeStruct((ndevice,) + block, F32),
            jax.ShapeDtypeStruct((ndevice, ndevice), F32),
            *(jax.ShapeDtypeStruct(shape, kind) for shape, kind in factor),
        ],
        scratch_shapes=[
            *(pltpu.VMEM(shape, kind) for shape, kind in factor),
            pltpu.VMEM(contributions.shape, F32),
            pltpu.VMEM((K, K * width, width), F32),
            pltpu.VMEM((K,) + block, F32),
            pltpu.VMEM((ndevice,) + block, F32),
            pltpu.VMEM((K,) + block, F32),
            pltpu.VMEM((K, 8, width), F32),
            pltpu.VMEM((8, width), F32),
            pltpu.VMEM((npatch, K, rows, width), F32),
            pltpu.VMEM((npatch - 1, K, rows, width), F32),
            pltpu.VMEM((K, rows, width), F32),
            pltpu.VMEM((K, K) + block, F32),
            pltpu.VMEM((width, 2 * width), F32),
            pltpu.VMEM(block, F32),
            pltpu.SemaphoreType.DMA((copies,)),
            pltpu.SemaphoreType.DMA((copies,)),
            pltpu.SemaphoreType.DMA((2,)),
            pltpu.SemaphoreType.DMA((9,)),
        ],
        compiler_params=params(collective_id=0, has_side_effects=True),
        name="exchange",
    )(slots, turns, fill, contributions, codes, reg)


def route(targets, counts, pivot, rowblk, ncol, ndevice):
    slots = targets.shape[0]
    blocks = jnp.arange(pivot.shape[0], dtype=jnp.int32)
    position = jnp.sum(jnp.where(targets[:, :, None] == blocks, pivot, 0), 2)
    pos_first, pos_second = position[:, 0], position[:, 1]
    upper_pos = jnp.maximum(pos_first, pos_second)
    lower_pos = jnp.minimum(pos_first, pos_second)
    number = jnp.arange(slots, dtype=jnp.int32)
    live = number < counts[0]
    owner = upper_pos // rowblk * ncol + lower_pos % ncol
    select = (owner[:, None] == jnp.arange(ndevice, dtype=jnp.int32)[None, :]) & live[:, None]
    turned = (pos_first < pos_second).astype(jnp.int32)
    code = lower_pos // ncol * rowblk + upper_pos % rowblk

    def pick(value):
        return jnp.max(jnp.where(select, value[:, None], -1), 0)

    return pick(number), pick(turned), pick(code).astype(F32)[None, :]


def body(contributions, targets, counts, pivot, fill_draw, regular):
    width = contributions.shape[1]
    npatch = lax.axis_size("patch")
    ncol = lax.axis_size("col")
    ndevice = npatch * ncol
    nblock = pivot.shape[0]
    rowblk = regular.shape[0] // width
    colslots = nblock // ncol
    patch_id = lax.axis_index("patch")
    col_id = lax.axis_index("col")

    slots, turns, codes = route(targets, counts, pivot, rowblk, ncol, ndevice)
    reg = lax.dynamic_slice_in_dim(regular, col_id * width, width, 0)[None, :]
    got, table, *factor = exchange(slots, turns, codes, fill_draw, contributions, reg, npatch)

    diag = (patch_id * rowblk + col_id).astype(jnp.int32)[None]
    codes = lax.dynamic_slice_in_dim(table, diag[0], 1, 1)[:, 0].astype(jnp.int32)
    matrix = place(codes, diag, got, reg)

    rows_l, cols_l = spread(fill_draw, matrix, factor, npatch, ncol)
    rows_l = rows_l.reshape(rowblk * width, K * width)

    schur, panels = trailing(fill_draw, matrix.reshape(colslots, rowblk * width, width), rows_l, cols_l)
    return (panels, schur.reshape(colslots, 1, rowblk * width, width))


def solution(mesh):
    in_specs = (
        P(("patch", "col"), None, None),
        P(("patch", "col"), None),
        P(("patch", "col")),
        P(),
        P(),
        P("patch"),
    )
    out_specs = (P("patch", None), P(None, "col", "patch", None))
    return jax.shard_map(body, mesh=mesh, in_specs=in_specs, out_specs=out_specs, check_vma=False)
```

```python
import functools
import itertools
import random

import jax
import jax.numpy as jnp
from jax import lax
from jax.experimental import pallas as pl
from jax.experimental.pallas import tpu as pltpu
from jax.sharding import PartitionSpec as P

K = 8
HIGH = lax.Precision.HIGHEST
F32 = jnp.float32
BF16 = jnp.bfloat16
MIB = 1024 * 1024
SMEM = pl.BlockSpec(memory_space=pltpu.SMEM)
WHOLE = pl.BlockSpec(memory_space=pltpu.VMEM)
ANY = pl.BlockSpec(memory_space=pl.ANY)
NT = (((1,), (1,)), ((), ()))
TN = (((0,), (0,)), ((), ()))


def params(size, **more):
    return pltpu.CompilerParams(vmem_limit_bytes=size * MIB, **more)


def dot_nt(a, b):
    return lax.dot_general(a, b, NT, precision=HIGH, preferred_element_type=F32)


def eye_mask(n):
    return lax.broadcasted_iota(jnp.int32, (n, n), 0) == lax.broadcasted_iota(jnp.int32, (n, n), 1)


def weight(drawn, i, j):
    return jnp.where(i == j, 1, jnp.maximum(drawn[i, j], drawn[j, i])).astype(F32)


def place_kernel(per, last, codes, diag, x_ref, reg_ref, o_ref):
    g = pl.program_id(0)
    width = x_ref.shape[2]

    @pl.when(g == 0)
    def _():
        def clear(q, carry):
            o_ref[q] = jnp.zeros((width, width), F32)
            return carry

        lax.fori_loop(0, o_ref.shape[0], clear, 0)

    def step(t, carry):
        code = codes[0, g * per + t]

        @pl.when(code >= 0)
        def _():
            o_ref[code] += x_ref[t]

        return carry

    lax.fori_loop(0, per, step, 0)

    @pl.when(g == last)
    def _():
        block = o_ref[diag[0]]
        o_ref[diag[0]] = 0.5 * (block + block.T) + jnp.where(eye_mask(width), reg_ref[...], 0.0)


def place(codes, diag, got, reg, per=16):
    ndevice, _, width = got.shape
    places = 128
    return pl.pallas_call(
        functools.partial(place_kernel, per, ndevice // per - 1),
        grid=(ndevice // per,),
        in_specs=[SMEM, SMEM, pl.BlockSpec((per, width, width), lambda g: (g, 0, 0)), pl.BlockSpec((1, width), lambda g: (0, 0))],
        out_specs=pl.BlockSpec((places, width, width), lambda g: (0, 0, 0), pipeline_mode=pl.Buffered(1)),
        out_shape=jax.ShapeDtypeStruct((places, width, width), F32),
        compiler_params=params(43),
        name="place",
    )(codes, diag, got, reg)


def split3(a):
    one = a.astype(BF16).astype(F32)
    rest = a - one
    two = rest.astype(BF16).astype(F32)
    return one, two, rest - two


def chol_inverse(w_ref, lt_ref):
    width = w_ref.shape[0]
    sub = lax.broadcasted_iota(jnp.int32, (8, width), 0)
    lane = lax.broadcasted_iota(jnp.int32, (8, width), 1)
    for base in range(0, width, 8):
        both = w_ref[base : base + 8, :]
        rows = both[:, :width]
        unit = both[:, width:]
        cols = [jnp.broadcast_to(rows[:, base + j : base + j + 1], (8, width)) for j in range(8)]
        scale = jnp.zeros((8, width), F32)
        for j in range(8):
            root = lax.rsqrt(cols[j][j : j + 1, :])
            lower = cols[j] * root
            for i in range(j + 1, 8):
                cols[i] = cols[i] - lower * lower[i : i + 1, :]
            below = jnp.where(sub > j, lower, 0.0)
            rows = rows - below * (rows[j : j + 1, :] * root)
            unit = unit - below * (unit[j : j + 1, :] * root)
            scale = jnp.where(sub == j, root, scale)
        upper = jnp.where(lane >= sub + base, rows * scale, 0.0)
        unit = unit * scale
        lt_ref[base : base + 8, :] = upper
        w_ref[base : base + 8, width:] = unit
        if base + 8 < width:
            u1, u2, u3 = split3(upper)
            v1, v2, v3 = split3(unit)
            left = jnp.concatenate([u1, u1, u2, u2, u1, u3], 0).astype(BF16)
            w1, w2, w3 = (jnp.concatenate([a, b], 1) for a, b in ((u1, v1), (u2, v2), (u3, v3)))
            right = jnp.concatenate([w1, w2, w1, w2, w3, w1], 0).astype(BF16)
            change = lax.dot_general(left, right, TN, preferred_element_type=F32)
            w_ref[base + 8 :, :] -= change[base + 8 :, :]


def factor_head(fill, head_ref, lh_ref, li_ref, w_ref, lt_ref):
    width = head_ref.shape[2]
    eye = jnp.where(eye_mask(width), 1.0, 0.0).astype(F32)
    for c in range(K):
        for r in range(K):
            at = slice(r * width, (r + 1) * width)
            if r < c:
                lh_ref[c, at, :] = jnp.zeros((width, width), F32)
                continue
            block = head_ref[c, r]
            lh_ref[c, at, :] = 0.5 * (block + block.T) if r == c else block

    def step(k, carry):
        w_ref[:, :width] = lh_ref[k, pl.ds(pl.multiple_of(k * width, width), width), :]
        w_ref[:, width:] = eye
        chol_inverse(w_ref, lt_ref)
        li_ref[k] = w_ref[:, width:]
        lh_ref[k, pl.ds(pl.multiple_of(k * width, width), width), :] = lt_ref[...].T
        for s in range(K - 1):

            @pl.when(k == s)
            def _(s=s):
                below = slice((s + 1) * width, K * width)
                solved = dot_nt(lh_ref[s, below, :], li_ref[s])
                lh_ref[s, below, :] = solved
                for j in range(s + 1, K):
                    part = solved[(j - s - 1) * width :]
                    change = dot_nt(part, part[:width])
                    for i in range(j, K):
                        at = slice(i * width, (i + 1) * width)
                        lh_ref[j, at, :] -= weight(fill, i, j) * change[(i - j) * width : (i - j + 1) * width]

        return carry

    lax.fori_loop(0, K, step, 0)


def split2(a):
    hi = a.astype(BF16)
    return hi, (a - hi.astype(F32)).astype(BF16)


def hand_on(lh_ref, li_ref, uh_ref, ul_ref, ih_ref, il_ref, diag_ref):
    width = lh_ref.shape[2]

    def column(k, carry):
        diag_ref[k] = lh_ref[k, pl.ds(pl.multiple_of(k * width, width), width), :]
        ih_ref[k], il_ref[k] = split2(li_ref[k].T)

        def row(i, carry):
            at = pl.ds(pl.multiple_of(i * width, width), width)
            uh_ref[k, :, at], ul_ref[k, :, at] = split2(lh_ref[k, at, :].T)
            return carry

        return lax.fori_loop(k + 1, K, row, carry)

    lax.fori_loop(0, K, column, 0)


def dot3(a, b_hi, b_lo):
    a_hi, a_lo = split2(a)
    product = jnp.dot(a_hi, b_hi, preferred_element_type=F32)
    product += jnp.dot(a_lo, b_hi, preferred_element_type=F32)
    return product + jnp.dot(a_hi, b_lo, preferred_element_type=F32)


def solve_row(row, fill, a_ref, uh_ref, ul_ref, ih_ref, il_ref, diag_ref, o_ref):
    width = a_ref.shape[1]
    work = [a_ref[k] for k in range(K)]
    for k in range(K):
        solved = dot3(work[k], ih_ref[k], il_ref[k])
        solved = jnp.where(row > k, solved, jnp.where(row == k, diag_ref[k], 0.0))
        o_ref[:, k * width : (k + 1) * width] = solved
        if k + 1 < K:
            change = dot3(solved, uh_ref[k, :, (k + 1) * width :], ul_ref[k, :, (k + 1) * width :])
            for j in range(k + 1, K):
                work[j] = work[j] - weight(fill, row, j) * change[:, (j - k - 1) * width : (j - k) * width]


def schur_kernel(pair, chunk, fill, a_ref, rows_ref, cols_ref, o_ref, panels_ref, hi_ref, lo_ref, sem):
    g = pl.program_id(0)
    width = a_ref.shape[2]
    nrow = a_ref.shape[1] // width
    grow = lax.axis_index("patch") * nrow
    gcol = [(g * pair + q) * K + lax.axis_index("col") for q in range(pair)]

    @pl.when(g == 0)
    def _():
        pltpu.make_async_copy(rows_ref, panels_ref, sem).start()

        def split(r, carry):
            at = pl.ds(pl.multiple_of(r * width, width), width)
            rows = rows_ref[at, :]
            hi = rows.astype(BF16)
            hi_ref[at, :] = hi
            lo_ref[at, :] = (rows - hi.astype(F32)).astype(BF16)
            return carry

        lax.fori_loop(0, nrow, split, 0)

    cols = cols_ref[...].reshape(pair * width, cols_ref.shape[2])
    col_hi = cols.astype(BF16)
    col_lo = (cols - col_hi.astype(F32)).astype(BF16)

    some = (grow + nrow > gcol[0]) & (gcol[pair - 1] >= K)

    @pl.when(some)
    def _():
        def step(m, carry):
            at = pl.ds(pl.multiple_of(m * chunk * width, chunk * width), chunk * width)
            hi = hi_ref[at, :]
            product = lax.dot_general(hi, col_hi, NT, preferred_element_type=F32)
            product += lax.dot_general(hi, col_lo, NT, preferred_element_type=F32)
            product += lax.dot_general(lo_ref[at, :], col_hi, NT, preferred_element_type=F32)
            for i in range(chunk):
                r = m * chunk + i
                here = pl.ds(pl.multiple_of(r * width, width), width)
                for q in range(pair):
                    part = product[i * width : (i + 1) * width, q * width : (q + 1) * width]
                    value = a_ref[q, here, :] - weight(fill, grow + r, gcol[q]) * part
                    o_ref[q, here, :] = jnp.where((grow + r >= gcol[q]) & (gcol[q] >= K), value, 0.0)
            return carry

        lax.fori_loop(0, nrow // chunk, step, 0)

    @pl.when(jnp.logical_not(some))
    def _():
        o_ref[...] = jnp.zeros(o_ref.shape, F32)

    @pl.when(g == pl.num_programs(0) - 1)
    def _():
        pltpu.make_async_copy(rows_ref, panels_ref, sem).wait()


def trailing(fill, matrix, rows_l, cols_l, pair=2, chunk=4):
    colslots, tall, width = matrix.shape
    depth = rows_l.shape[1]
    return pl.pallas_call(
        functools.partial(schur_kernel, pair, chunk),
        grid=(colslots // pair,),
        in_specs=[
            SMEM,
            pl.BlockSpec((pair, tall, width), lambda g: (g, 0, 0)),
            pl.BlockSpec((tall, depth), lambda g: (0, 0), pipeline_mode=pl.Buffered(1)),
            pl.BlockSpec((pair, width, depth), lambda g: (g, 0, 0)),
        ],
        out_specs=[pl.BlockSpec((pair, tall, width), lambda g: (g, 0, 0)), pl.BlockSpec(memory_space=pl.ANY)],
        out_shape=[
            jax.ShapeDtypeStruct((colslots, tall, width), F32),
            jax.ShapeDtypeStruct((tall, depth), F32),
        ],
        scratch_shapes=[pltpu.VMEM((tall, depth), BF16), pltpu.VMEM((tall, depth), BF16), pltpu.SemaphoreType.DMA],
        compiler_params=params(22),
        name="trailing",
    )(fill, matrix, rows_l, cols_l)


RING = 4


def turn(value, by, size=RING):
    return lax.rem(value + (by + size), size)


class Sends:
    def __init__(self, ssem, rsem):
        self.ssem, self.rsem, self.all = ssem, rsem, []

        self.used = 0

    def plan(self, n, src, dst, patch, col):
        return pltpu.make_async_remote_copy(
            src_ref=src,
            dst_ref=dst,
            send_sem=self.ssem.at[n],
            recv_sem=self.rsem.at[n],
            device_id={"patch": patch, "col": col},
            device_id_type=pl.DeviceIdType.MESH,
        )

    def start(self, src, dst, patch, col):
        copy = self.plan(self.used, src, dst, patch, col)
        self.used += 1
        copy.start()
        self.all.append(copy)
        return copy

    def finish(self):
        for copy in self.all:
            copy.wait_send()


def meet(peers):
    barrier = pltpu.get_barrier_semaphore()
    for patch, col in peers:
        pl.semaphore_signal(
            barrier, inc=1, device_id={"patch": patch, "col": col}, device_id_type=pl.DeviceIdType.MESH
        )
    pl.semaphore_wait(barrier, len(peers))


def col_ring(sends, src, items_ref, patch, col):
    x, core = col // 2, lax.rem(col, 2)
    there = [turn(x, by) * 2 + core for by in range(RING)]
    other = x * 2 + (1 - core)
    half = items_ref.shape[1] // 2
    up = sends.start(src, items_ref.at[col], patch, there[1])
    down = sends.start(src, items_ref.at[col], patch, there[3])
    side = [sends.start(src, items_ref.at[col], patch, other)]
    yield
    up.wait_recv()
    from_down = items_ref.at[there[3]]
    onward = [sends.start(from_down.at[pl.ds(0, half)], from_down.at[pl.ds(0, half)], patch, there[1])]
    side.append(sends.start(from_down, from_down, patch, other))
    down.wait_recv()
    from_up = items_ref.at[there[1]]
    onward.append(sends.start(from_up.at[pl.ds(half, half)], from_up.at[pl.ds(half, half)], patch, there[3]))
    side.append(sends.start(from_up, from_up, patch, other))
    yield
    for copy in onward:
        copy.wait_recv()
    far = items_ref.at[there[2]]
    side.append(sends.start(far, far, patch, other))
    yield
    for copy in side:
        copy.wait_recv()
    yield


def patch_ring(sends, src, items_ref, patch, col, swap):
    y, z = patch // RING, lax.rem(patch, RING)

    def at(first, second):
        i, j = (first, second) if swap else (second, first)
        return turn(y, i) * RING + turn(z, j)

    size = items_ref.shape[1] // 2
    start = size if swap else 0
    whole = pl.ds(start, size)
    parts = (pl.ds(start, size // 2), pl.ds(start + size // 2, size // 2))

    def relay(item, rows, target):
        return sends.start(items_ref.at[item, rows], items_ref.at[item, rows], target, col)

    mine = src.at[whole]
    up = sends.start(mine, items_ref.at[patch, whole], at(1, 0), col)
    down = sends.start(mine, items_ref.at[patch, whole], at(3, 0), col)
    yield
    across = {0: [sends.start(mine, items_ref.at[patch, whole], at(0, by), col) for by in (1, 3)]}
    yield
    up.wait_recv()
    onward = [relay(at(3, 0), parts[0], at(1, 0))]
    across[3] = [relay(at(3, 0), whole, at(0, by)) for by in (1, 3)]
    yield
    down.wait_recv()
    onward.append(relay(at(1, 0), parts[1], at(3, 0)))
    across[1] = [relay(at(1, 0), whole, at(0, by)) for by in (1, 3)]
    yield
    for copy in onward:
        copy.wait_recv()
    across[2] = [relay(at(2, 0), whole, at(0, by)) for by in (1, 3)]
    last = []
    for i in (0, 3, 1, 2):
        yield
        across[i][0].wait_recv()
        last.append(relay(at(i, 3), parts[0], at(0, 1)))
        across[i][1].wait_recv()
        last.append(relay(at(i, 1), parts[1], at(0, 3)))
    yield
    for copy in last:
        copy.wait_recv()
    yield


def interleave(*steps):
    running = list(steps)
    while running:
        running = [one for one in running if next(one, "end") != "end"]


def spread_kernel(
    fill,
    panel_ref,
    *refs,
):
    stored, (rows_ref, cols_ref), held, rest = refs[:5], refs[5:7], refs[7:12], refs[12:]
    turned_ref, own_ref, ssem, rsem, lsem = rest
    patch, col = lax.axis_index("patch"), lax.axis_index("col")
    y, z = patch // RING, lax.rem(patch, RING)
    loads = [pltpu.make_async_copy(a, b, lsem.at[2 + n]) for n, (a, b) in enumerate(zip(stored, held))]
    for copy in loads:
        copy.start()
    meet(
        [(patch, turn(col, by, K)) for by in range(1, K)]
        + [(turn(y, by) * RING + z, col) for by in (1, 3)]
        + [(y * RING + turn(z, by), col) for by in (1, 3)]
    )
    sends = Sends(ssem, rsem)
    local = pltpu.make_async_copy(panel_ref.at[col], turned_ref.at[col], lsem.at[0])
    local.start()
    first = [
        sends.start(panel_ref.at[turn(col, by, K)], turned_ref.at[col], patch, turn(col, by, K)) for by in range(1, K)
    ]
    local.wait()
    for copy in first:
        copy.wait_recv()
    for copy in loads:
        copy.wait()
    solve_row(patch * K + col, fill, turned_ref, *held, own_ref)
    local = [
        pltpu.make_async_copy(own_ref, rows_ref.at[col], lsem.at[0]),
        pltpu.make_async_copy(own_ref, cols_ref.at[patch], lsem.at[1]),
    ]
    for copy in local:
        copy.start()
    interleave(
        patch_ring(sends, own_ref, cols_ref, patch, col, False),
        patch_ring(sends, own_ref, cols_ref, patch, col, True),
        col_ring(sends, own_ref, rows_ref, patch, col),
    )
    sends.finish()
    for copy in local:
        copy.wait()


def spread(fill, matrix, factor, npatch, ncol):
    width = matrix.shape[2]
    block = (width, width)
    wide = K * width
    copies = 48 + K - 1
    return pl.pallas_call(
        spread_kernel,
        grid=(1,),
        in_specs=[SMEM, pl.BlockSpec((K,) + block, lambda g: (0, 0, 0))]
        + [pl.BlockSpec(memory_space=pl.ANY)] * 5,
        out_specs=[pl.BlockSpec(memory_space=pl.ANY)] * 2,
        out_shape=[
            jax.ShapeDtypeStruct((ncol, width, wide), F32),
            jax.ShapeDtypeStruct((npatch, width, wide), F32),
        ],
        scratch_shapes=[pltpu.VMEM(part.shape, part.dtype) for part in factor]
        + [
            pltpu.VMEM((K,) + block, F32),
            pltpu.VMEM((width, wide), F32),
            pltpu.SemaphoreType.DMA((copies,)),
            pltpu.SemaphoreType.DMA((copies,)),
            pltpu.SemaphoreType.DMA((7,)),
        ],
        compiler_params=params(10, collective_id=1, has_side_effects=True),
        name="spread",
    )(fill, matrix, *factor)


def offsets():
    left = [o for o in itertools.product(range(RING), range(RING), range(RING), range(2)) if any(o)]
    random.Random(3).shuffle(left)

    def links(o):
        return [float(v in (2, want)) for v in o[:3] for want in (1, 3)]

    load, order = [0.0] * 6, []
    while left:
        best = min(left, key=lambda o: max(map(sum, zip(load, links(o)))) - min(map(sum, zip(load, links(o)))))
        left.remove(best)
        order.append(best)
        load = [sum(pair) for pair in zip(load, links(best))]
    return order


batches = (0, 30)


def head_cols(sends, head_ref, patch, col, rest):
    x, core = col // 2, lax.rem(col, 2)
    first = sends.used
    sends.used += 7 * RING

    def copy(by, j, chip, hand, to, across):
        ref = head_ref.at[chip * 2 + hand, pl.ds(2 * j, 2)]
        return sends.plan(first + ((3 + by) if across else (by - 1)) * RING + j, ref, ref, patch, to)

    def out(by, j):
        return copy(by, j, x, core, turn(x, by) * 2 + core, False)

    def side(by, j, hand):
        return copy(by, j, turn(x, RING - by), hand, x * 2 + 1 - core, True)

    def each(by, act):
        for j in range(RING):
            pl.when(j >= turn(x, RING - by))(functools.partial(act, j))

    for by in (1, 3, 2):
        each(0, lambda j: out(by, j).start())
    each(0, lambda j: side(0, j, core).start())
    rest()
    for by in (1, 3, 2):
        def pass_on(j, by=by):
            copy(by, j, turn(x, RING - by), core, turn(x, by) * 2 + core, False).wait_recv()
            side(by, j, core).start()

        each(by, pass_on)
    for by in range(RING):
        each(by, lambda j: side(by, j, 1 - core).wait_recv())

    def finish():
        for by in (1, 3, 2):
            each(0, lambda j: out(by, j).wait_send())
        for by in range(RING):
            each(by, lambda j: side(by, j, core).wait_send())

    return finish


def exchange_kernel(
    npatch,
    slots,
    turns,
    fill,
    given_ref,
    code_ref,
    reg_ref,
    all_ref,
    mine_codes_ref,
    *refs,
):
    stored, held, rest = refs[:5], refs[5:10], refs[10:]
    exchange_steps(
        npatch, slots, turns, fill, given_ref, code_ref, reg_ref, all_ref, mine_codes_ref, stored, held, *rest
    )


def exchange_steps(
    npatch,
    slots,
    turns,
    fill,
    given_ref,
    code_ref,
    reg_ref,
    all_ref,
    mine_codes_ref,
    stored,
    held,
    codes_ref,
    x_ref,
    lh_ref,
    li_ref,
    out_ref,
    mine_ref,
    tile_ref,
    row_ref,
    dense_ref,
    part_ref,
    piece_ref,
    head_ref,
    w_ref,
    lt_ref,
    ssem,
    rsem,
    bulk,
    lsem,
):
    patch, col = lax.axis_index("patch"), lax.axis_index("col")
    y, z, x, core = patch // RING, lax.rem(patch, RING), col // 2, lax.rem(col, 2)
    me = patch * K + col
    width = x_ref.shape[2]
    ndevice = npatch * K
    load = pltpu.make_async_copy(given_ref, x_ref, lsem.at[3])
    load.start()

    sign = 1 + 2 * core
    peers = []
    for dy, dz, dx, dc in offsets():
        to_patch = lax.rem(y + dy * sign, RING) * RING + lax.rem(z + dz * sign, RING)
        to_col = lax.rem(x + dx * sign, RING) * 2 + lax.rem(core + dc, 2)
        peers.append((to_patch, to_col))
    barrier = pltpu.get_barrier_semaphore()
    for to_patch, to_col in peers:
        pl.semaphore_signal(
            barrier, inc=1, device_id={"patch": to_patch, "col": to_col}, device_id_type=pl.DeviceIdType.MESH
        )

    def pack(d, carry):
        block = x_ref[jnp.maximum(slots[d], 0)]
        out_ref[d] = jnp.where(turns[d] > 0, block.T, block)
        return carry

    load.wait()
    lax.fori_loop(0, K, pack, 0)
    row_ref[...] = jnp.broadcast_to(code_ref[...], (8, width))
    pl.semaphore_wait(barrier, len(peers))

    sends = Sends(ssem, rsem)

    def flow(count):
        for to_patch, to_col in peers[flow.done : flow.done + count]:
            pltpu.make_async_remote_copy(
                src_ref=out_ref.at[to_patch * K + to_col],
                dst_ref=all_ref.at[me],
                send_sem=bulk.at[0],
                recv_sem=bulk.at[1],
                device_id={"patch": to_patch, "col": to_col},
                device_id_type=pl.DeviceIdType.MESH,
            ).start()
        flow.done += count

    flow.done = 0

    local = [
        pltpu.make_async_copy(out_ref.at[col], mine_ref.at[col], lsem.at[0]),
        pltpu.make_async_copy(row_ref, tile_ref.at[col], lsem.at[1]),
    ]
    for copy in local:
        copy.start()
    first = []
    for by in range(1, K):
        to = turn(col, by, K)
        first.append(sends.start(row_ref, tile_ref.at[col], patch, to))
        first.append(sends.start(out_ref.at[to], mine_ref.at[col], patch, to))
    lax.fori_loop(K, ndevice, pack, 0)
    own = pltpu.make_async_copy(out_ref.at[me], all_ref.at[me], lsem.at[2])
    own.start()
    for copy in local:
        copy.wait()
    for copy in first:
        copy.wait_recv()
    reg = jnp.broadcast_to(reg_ref[...], (8, width))
    sub = lax.broadcasted_iota(jnp.int32, (8, width), 0)
    lane = lax.broadcasted_iota(jnp.int32, (8, width), 1)
    codes = []
    tile = jnp.zeros((8, width), F32)
    for c in range(K):
        row = tile_ref[c]
        tile = jnp.where(sub == c, row, tile)
        codes.append(jnp.broadcast_to(jnp.sum(jnp.where(lane == col, row, 0.0), 1, keepdims=True), (8, width)))
    for r in range(K):
        hits = [code == r for code in codes]
        shift = jnp.where((patch == 0) & (col == r), reg, 0.0)
        for q in range(npatch):
            total = jnp.where(lane == sub + q * 8, shift, 0.0)
            for c in range(K):
                total = total + jnp.where(hits[c], mine_ref[c, q * 8 : (q + 1) * 8, :], 0.0)
            dense_ref[q, r] = total
    here = pl.ds(pl.multiple_of(patch * 8, 8), 8)
    codes_ref[here, :] = tile
    second = []
    tables = []
    for by in range(1, npatch):
        to = turn(patch, by, npatch)
        second.append(sends.start(dense_ref.at[to], part_ref.at[by - 1], to, col))
    for by in range(1, npatch):
        tables.append(sends.start(codes_ref.at[here, :], codes_ref.at[here, :], turn(patch, by, npatch), col))
    flow(batches[0])
    total = dense_ref[patch]
    for by, copy in enumerate(second):
        copy.wait_recv()
        total = total + part_ref[by]
    piece_ref[...] = total
    local = pltpu.make_async_copy(piece_ref, head_ref.at[col, :, here, :], lsem.at[0])
    local.start()
    third = [
        sends.start(piece_ref, head_ref.at[col, :, here, :], turn(patch, by, npatch), col) for by in range(1, npatch)
    ]
    flow(batches[1])
    local.wait()
    for copy in third:
        copy.wait_recv()
    finish = head_cols(sends, head_ref, patch, col, lambda: flow(len(peers) - flow.done))

    factor_head(fill, head_ref, lh_ref, li_ref, w_ref, lt_ref)
    hand_on(lh_ref, li_ref, *held)
    stores = [pltpu.make_async_copy(b, a, lsem.at[4 + n]) for n, (a, b) in enumerate(zip(stored, held))]
    for copy in stores:
        copy.start()

    finish()
    sends.finish()
    for copy in tables:
        copy.wait_recv()
    lt_ref[...] = codes_ref[...].T
    mine_codes_ref[...] = lt_ref[pl.ds(me, 1), :].astype(jnp.int32)
    own.wait()
    for copy in stores:
        copy.wait()
    every = pl.ds(0, ndevice - 1)
    whole = pltpu.make_async_remote_copy(
        src_ref=out_ref.at[every],
        dst_ref=all_ref.at[every],
        send_sem=bulk.at[0],
        recv_sem=bulk.at[1],
        device_id={"patch": peers[0][0], "col": peers[0][1]},
        device_id_type=pl.DeviceIdType.MESH,
    )
    whole.wait_send()
    whole.wait_recv()


def exchange(slots, turns, codes, fill, contributions, reg, npatch):
    width = contributions.shape[2]
    ndevice = npatch * K
    copies = 2 * (K - 1) + 3 * (npatch - 1) + 7 * RING
    wide, one = (K, width, K * width), (K, width, width)
    factor = ((wide, BF16), (wide, BF16), (one, BF16), (one, BF16), (one, F32))
    rows = width // npatch
    block = (width, width)
    return pl.pallas_call(
        functools.partial(exchange_kernel, npatch),
        in_specs=[SMEM, SMEM, SMEM, ANY, WHOLE, WHOLE],
        out_specs=[ANY, WHOLE] + [ANY] * 5,
        out_shape=[
            jax.ShapeDtypeStruct((ndevice,) + block, F32),
            jax.ShapeDtypeStruct((1, ndevice), jnp.int32),
            *(jax.ShapeDtypeStruct(shape, kind) for shape, kind in factor),
        ],
        scratch_shapes=[
            *(pltpu.VMEM(shape, kind) for shape, kind in factor),
            pltpu.VMEM((ndevice, ndevice), F32),
            pltpu.VMEM(contributions.shape, F32),
            pltpu.VMEM((K, K * width, width), F32),
            pltpu.VMEM((K,) + block, F32),
            pltpu.VMEM((ndevice,) + block, F32),
            pltpu.VMEM((K,) + block, F32),
            pltpu.VMEM((K, 8, width), F32),
            pltpu.VMEM((8, width), F32),
            pltpu.VMEM((npatch, K, rows, width), F32),
            pltpu.VMEM((npatch - 1, K, rows, width), F32),
            pltpu.VMEM((K, rows, width), F32),
            pltpu.VMEM((K, K) + block, F32),
            pltpu.VMEM((width, 2 * width), F32),
            pltpu.VMEM(block, F32),
            pltpu.SemaphoreType.DMA((copies,)),
            pltpu.SemaphoreType.DMA((copies,)),
            pltpu.SemaphoreType.DMA((2,)),
            pltpu.SemaphoreType.DMA((9,)),
        ],
        compiler_params=params(38, collective_id=0, has_side_effects=True),
        name="exchange",
    )(slots, turns, fill, contributions, codes, reg)


def route(targets, counts, pivot, rowblk, ncol, ndevice):
    slots = targets.shape[0]
    blocks = jnp.arange(pivot.shape[0], dtype=jnp.int32)
    position = jnp.sum(jnp.where(targets[:, :, None] == blocks, pivot, 0), 2)
    pos_first, pos_second = position[:, 0], position[:, 1]
    upper_pos = jnp.maximum(pos_first, pos_second)
    lower_pos = jnp.minimum(pos_first, pos_second)
    number = jnp.arange(slots, dtype=jnp.int32)
    live = number < counts[0]
    owner = upper_pos // rowblk * ncol + lower_pos % ncol
    select = (owner[:, None] == jnp.arange(ndevice, dtype=jnp.int32)[None, :]) & live[:, None]
    turned = (pos_first < pos_second).astype(jnp.int32)
    code = lower_pos // ncol * rowblk + upper_pos % rowblk

    def pick(value):
        return jnp.max(jnp.where(select, value[:, None], -1), 0)

    return pick(number), pick(turned), pick(code).astype(F32)[None, :]


def body(contributions, targets, counts, pivot, fill_draw, regular):
    width = contributions.shape[1]
    npatch = lax.axis_size("patch")
    ncol = lax.axis_size("col")
    ndevice = npatch * ncol
    nblock = pivot.shape[0]
    rowblk = regular.shape[0] // width
    colslots = nblock // ncol
    patch_id = lax.axis_index("patch")
    col_id = lax.axis_index("col")

    slots, turns, codes = route(targets, counts, pivot, rowblk, ncol, ndevice)
    reg = lax.dynamic_slice_in_dim(regular, col_id * width, width, 0)[None, :]
    got, places, *factor = exchange(slots, turns, codes, fill_draw, contributions, reg, npatch)

    diag = (patch_id * rowblk + col_id).astype(jnp.int32)[None]
    matrix = place(places, diag, got, reg)

    rows_l, cols_l = spread(fill_draw, matrix, factor, npatch, ncol)
    rows_l = rows_l.reshape(rowblk * width, K * width)

    schur, panels = trailing(fill_draw, matrix.reshape(colslots, rowblk * width, width), rows_l, cols_l)
    return (panels, schur.reshape(colslots, 1, rowblk * width, width))


def solution(mesh):
    in_specs = (
        P(("patch", "col"), None, None),
        P(("patch", "col"), None),
        P(("patch", "col")),
        P(),
        P(),
        P("patch"),
    )
    out_specs = (P("patch", None), P(None, "col", "patch", None))
    return jax.shard_map(body, mesh=mesh, in_specs=in_specs, out_specs=out_specs, check_vma=False)
```

```python
import functools
import itertools
import random

import jax
import jax.numpy as jnp
from jax import lax
from jax.experimental import pallas as pl
from jax.experimental.pallas import tpu as pltpu
from jax.sharding import PartitionSpec as P

K = 8
HIGH = lax.Precision.HIGHEST
F32 = jnp.float32
BF16 = jnp.bfloat16
MIB = 1024 * 1024
SMEM = pl.BlockSpec(memory_space=pltpu.SMEM)
WHOLE = pl.BlockSpec(memory_space=pltpu.VMEM)
ANY = pl.BlockSpec(memory_space=pl.ANY)
HBM = pl.BlockSpec(memory_space=pltpu.HBM)
NT = (((1,), (1,)), ((), ()))
TN = (((0,), (0,)), ((), ()))


def params(size, **more):
    return pltpu.CompilerParams(vmem_limit_bytes=size * MIB, **more)


def dot_nt(a, b):
    return lax.dot_general(a, b, NT, precision=HIGH, preferred_element_type=F32)


def eye_mask(n):
    return lax.broadcasted_iota(jnp.int32, (n, n), 0) == lax.broadcasted_iota(jnp.int32, (n, n), 1)


def weight(drawn, i, j):
    return jnp.where(i == j, 1, jnp.maximum(drawn[i, j], drawn[j, i])).astype(F32)


def place_kernel(per, last, codes, diag, x_ref, reg_ref, o_ref):
    g = pl.program_id(0)
    width = x_ref.shape[2]

    @pl.when(g == 0)
    def _():
        def clear(q, carry):
            o_ref[q] = jnp.zeros((width, width), F32)
            return carry

        lax.fori_loop(0, o_ref.shape[0], clear, 0)

    def step(t, carry):
        code = codes[0, g * per + t]

        @pl.when(code >= 0)
        def _():
            o_ref[code] += x_ref[t]

        return carry

    lax.fori_loop(0, per, step, 0)

    @pl.when(g == last)
    def _():
        block = o_ref[diag[0]]
        o_ref[diag[0]] = 0.5 * (block + block.T) + jnp.where(eye_mask(width), reg_ref[...], 0.0)


def place(codes, diag, got, reg, per=16):
    ndevice, _, width = got.shape
    places = 128
    return pl.pallas_call(
        functools.partial(place_kernel, per, ndevice // per - 1),
        grid=(ndevice // per,),
        in_specs=[SMEM, SMEM, pl.BlockSpec((per, width, width), lambda g: (g, 0, 0)), pl.BlockSpec((1, width), lambda g: (0, 0))],
        out_specs=pl.BlockSpec((places, width, width), lambda g: (0, 0, 0), pipeline_mode=pl.Buffered(1)),
        out_shape=jax.ShapeDtypeStruct((places, width, width), F32),
        compiler_params=params(43),
        name="place",
    )(codes, diag, got, reg)


def split3(a):
    one = a.astype(BF16).astype(F32)
    rest = a - one
    two = rest.astype(BF16).astype(F32)
    return one, two, rest - two


def chol_inverse(w_ref, lt_ref):
    width = w_ref.shape[0]
    sub = lax.broadcasted_iota(jnp.int32, (8, width), 0)
    lane = lax.broadcasted_iota(jnp.int32, (8, width), 1)
    for base in range(0, width, 8):
        both = w_ref[base : base + 8, :]
        rows = both[:, :width]
        unit = both[:, width:]
        cols = [jnp.broadcast_to(rows[:, base + j : base + j + 1], (8, width)) for j in range(8)]
        scale = jnp.zeros((8, width), F32)
        for j in range(8):
            root = lax.rsqrt(cols[j][j : j + 1, :])
            lower = cols[j] * root
            for i in range(j + 1, 8):
                cols[i] = cols[i] - lower * lower[i : i + 1, :]
            below = jnp.where(sub > j, lower, 0.0)
            rows = rows - below * (rows[j : j + 1, :] * root)
            unit = unit - below * (unit[j : j + 1, :] * root)
            scale = jnp.where(sub == j, root, scale)
        upper = jnp.where(lane >= sub + base, rows * scale, 0.0)
        unit = unit * scale
        lt_ref[base : base + 8, :] = upper
        w_ref[base : base + 8, width:] = unit
        if base + 8 < width:
            u1, u2, u3 = split3(upper)
            v1, v2, v3 = split3(unit)
            left = jnp.concatenate([u1, u1, u2, u2, u1, u3], 0).astype(BF16)
            w1, w2, w3 = (jnp.concatenate([a, b], 1) for a, b in ((u1, v1), (u2, v2), (u3, v3)))
            right = jnp.concatenate([w1, w2, w1, w2, w3, w1], 0).astype(BF16)
            change = lax.dot_general(left, right, TN, preferred_element_type=F32)
            w_ref[base + 8 :, :] -= change[base + 8 :, :]


def factor_head(fill, head_ref, lh_ref, li_ref, w_ref, lt_ref):
    width = head_ref.shape[2]
    eye = jnp.where(eye_mask(width), 1.0, 0.0).astype(F32)
    for c in range(K):
        for r in range(K):
            at = slice(r * width, (r + 1) * width)
            if r < c:
                lh_ref[c, at, :] = jnp.zeros((width, width), F32)
                continue
            block = head_ref[c, r]
            lh_ref[c, at, :] = 0.5 * (block + block.T) if r == c else block

    def step(k, carry):
        w_ref[:, :width] = lh_ref[k, pl.ds(pl.multiple_of(k * width, width), width), :]
        w_ref[:, width:] = eye
        chol_inverse(w_ref, lt_ref)
        li_ref[k] = w_ref[:, width:]
        lh_ref[k, pl.ds(pl.multiple_of(k * width, width), width), :] = lt_ref[...].T
        for s in range(K - 1):

            @pl.when(k == s)
            def _(s=s):
                below = slice((s + 1) * width, K * width)
                solved = dot_nt(lh_ref[s, below, :], li_ref[s])
                lh_ref[s, below, :] = solved
                for j in range(s + 1, K):
                    part = solved[(j - s - 1) * width :]
                    change = dot_nt(part, part[:width])
                    for i in range(j, K):
                        at = slice(i * width, (i + 1) * width)
                        lh_ref[j, at, :] -= weight(fill, i, j) * change[(i - j) * width : (i - j + 1) * width]

        return carry

    lax.fori_loop(0, K, step, 0)


def split2(a):
    hi = a.astype(BF16)
    return hi, (a - hi.astype(F32)).astype(BF16)


def hand_on(lh_ref, li_ref, uh_ref, ul_ref, ih_ref, il_ref, diag_ref):
    width = lh_ref.shape[2]

    def column(k, carry):
        diag_ref[k] = lh_ref[k, pl.ds(pl.multiple_of(k * width, width), width), :]
        ih_ref[k], il_ref[k] = split2(li_ref[k].T)

        def row(i, carry):
            at = pl.ds(pl.multiple_of(i * width, width), width)
            uh_ref[k, :, at], ul_ref[k, :, at] = split2(lh_ref[k, at, :].T)
            return carry

        return lax.fori_loop(k + 1, K, row, carry)

    lax.fori_loop(0, K, column, 0)


def dot3(a, b_hi, b_lo):
    a_hi, a_lo = split2(a)
    product = jnp.dot(a_hi, b_hi, preferred_element_type=F32)
    product += jnp.dot(a_lo, b_hi, preferred_element_type=F32)
    return product + jnp.dot(a_hi, b_lo, preferred_element_type=F32)


def solve_row(row, fill, a_ref, uh_ref, ul_ref, ih_ref, il_ref, diag_ref, o_ref):
    width = a_ref.shape[1]
    work = [a_ref[k] for k in range(K)]
    for k in range(K):
        solved = dot3(work[k], ih_ref[k], il_ref[k])
        solved = jnp.where(row > k, solved, jnp.where(row == k, diag_ref[k], 0.0))
        o_ref[:, k * width : (k + 1) * width] = solved
        if k + 1 < K:
            change = dot3(solved, uh_ref[k, :, (k + 1) * width :], ul_ref[k, :, (k + 1) * width :])
            for j in range(k + 1, K):
                work[j] = work[j] - weight(fill, row, j) * change[:, (j - k - 1) * width : (j - k) * width]


def schur_kernel(pair, chunk, fill, a_ref, rows_ref, cols_ref, o_ref, panels_ref, hi_ref, lo_ref, sem):
    g = pl.program_id(0)
    width = a_ref.shape[2]
    nrow = a_ref.shape[1] // width
    grow = lax.axis_index("patch") * nrow
    gcol = [(g * pair + q) * K + lax.axis_index("col") for q in range(pair)]

    @pl.when(g == 0)
    def _():
        pltpu.make_async_copy(rows_ref, panels_ref, sem).start()

        def split(r, carry):
            at = pl.ds(pl.multiple_of(r * width, width), width)
            rows = rows_ref[at, :]
            hi = rows.astype(BF16)
            hi_ref[at, :] = hi
            lo_ref[at, :] = (rows - hi.astype(F32)).astype(BF16)
            return carry

        lax.fori_loop(0, nrow, split, 0)

    cols = cols_ref[...].reshape(pair * width, cols_ref.shape[2])
    col_hi = cols.astype(BF16)
    col_lo = (cols - col_hi.astype(F32)).astype(BF16)

    some = (grow + nrow > gcol[0]) & (gcol[pair - 1] >= K)

    @pl.when(some)
    def _():
        def step(m, carry):
            at = pl.ds(pl.multiple_of(m * chunk * width, chunk * width), chunk * width)
            hi = hi_ref[at, :]
            product = lax.dot_general(hi, col_hi, NT, preferred_element_type=F32)
            product += lax.dot_general(hi, col_lo, NT, preferred_element_type=F32)
            product += lax.dot_general(lo_ref[at, :], col_hi, NT, preferred_element_type=F32)
            for i in range(chunk):
                r = m * chunk + i
                here = pl.ds(pl.multiple_of(r * width, width), width)
                for q in range(pair):
                    part = product[i * width : (i + 1) * width, q * width : (q + 1) * width]
                    value = a_ref[q, here, :] - weight(fill, grow + r, gcol[q]) * part
                    o_ref[q, here, :] = jnp.where((grow + r >= gcol[q]) & (gcol[q] >= K), value, 0.0)
            return carry

        lax.fori_loop(0, nrow // chunk, step, 0)

    @pl.when(jnp.logical_not(some))
    def _():
        o_ref[...] = jnp.zeros(o_ref.shape, F32)

    @pl.when(g == pl.num_programs(0) - 1)
    def _():
        pltpu.make_async_copy(rows_ref, panels_ref, sem).wait()


def trailing(fill, matrix, rows_l, cols_l, pair=2, chunk=4):
    colslots, tall, width = matrix.shape
    depth = rows_l.shape[1]
    return pl.pallas_call(
        functools.partial(schur_kernel, pair, chunk),
        grid=(colslots // pair,),
        in_specs=[
            SMEM,
            pl.BlockSpec((pair, tall, width), lambda g: (g, 0, 0)),
            pl.BlockSpec((tall, depth), lambda g: (0, 0), pipeline_mode=pl.Buffered(1)),
            pl.BlockSpec((pair, width, depth), lambda g: (g, 0, 0)),
        ],
        out_specs=[pl.BlockSpec((pair, tall, width), lambda g: (g, 0, 0)), pl.BlockSpec(memory_space=pl.ANY)],
        out_shape=[
            jax.ShapeDtypeStruct((colslots, tall, width), F32),
            jax.ShapeDtypeStruct((tall, depth), F32),
        ],
        scratch_shapes=[pltpu.VMEM((tall, depth), BF16), pltpu.VMEM((tall, depth), BF16), pltpu.SemaphoreType.DMA],
        compiler_params=params(22),
        name="trailing",
    )(fill, matrix, rows_l, cols_l)


RING = 4


def turn(value, by, size=RING):
    return lax.rem(value + (by + size), size)


class Sends:
    def __init__(self, ssem, rsem):
        self.ssem, self.rsem, self.all = ssem, rsem, []

        self.used = 0

    def plan(self, n, src, dst, patch, col):
        return pltpu.make_async_remote_copy(
            src_ref=src,
            dst_ref=dst,
            send_sem=self.ssem.at[n],
            recv_sem=self.rsem.at[n],
            device_id={"patch": patch, "col": col},
            device_id_type=pl.DeviceIdType.MESH,
        )

    def start(self, src, dst, patch, col):
        copy = self.plan(self.used, src, dst, patch, col)
        self.used += 1
        copy.start()
        self.all.append(copy)
        return copy

    def finish(self):
        for copy in self.all:
            copy.wait_send()


def meet(peers):
    barrier = pltpu.get_barrier_semaphore()
    for patch, col in peers:
        pl.semaphore_signal(
            barrier, inc=1, device_id={"patch": patch, "col": col}, device_id_type=pl.DeviceIdType.MESH
        )
    pl.semaphore_wait(barrier, len(peers))


def col_ring(sends, src, items_ref, patch, col):
    x, core = col // 2, lax.rem(col, 2)
    there = [turn(x, by) * 2 + core for by in range(RING)]
    other = x * 2 + (1 - core)
    half = items_ref.shape[1] // 2
    up = sends.start(src, items_ref.at[col], patch, there[1])
    down = sends.start(src, items_ref.at[col], patch, there[3])
    side = [sends.start(src, items_ref.at[col], patch, other)]
    yield
    up.wait_recv()
    from_down = items_ref.at[there[3]]
    onward = [sends.start(from_down.at[pl.ds(0, half)], from_down.at[pl.ds(0, half)], patch, there[1])]
    side.append(sends.start(from_down, from_down, patch, other))
    down.wait_recv()
    from_up = items_ref.at[there[1]]
    onward.append(sends.start(from_up.at[pl.ds(half, half)], from_up.at[pl.ds(half, half)], patch, there[3]))
    side.append(sends.start(from_up, from_up, patch, other))
    yield
    for copy in onward:
        copy.wait_recv()
    far = items_ref.at[there[2]]
    side.append(sends.start(far, far, patch, other))
    yield
    for copy in side:
        copy.wait_recv()
    yield


def patch_ring(sends, src, items_ref, patch, col, swap):
    y, z = patch // RING, lax.rem(patch, RING)

    def at(first, second):
        i, j = (first, second) if swap else (second, first)
        return turn(y, i) * RING + turn(z, j)

    size = items_ref.shape[1] // 2
    start = size if swap else 0
    whole = pl.ds(start, size)
    parts = (pl.ds(start, size // 2), pl.ds(start + size // 2, size // 2))

    def relay(item, rows, target):
        return sends.start(items_ref.at[item, rows], items_ref.at[item, rows], target, col)

    mine = src.at[whole]
    up = sends.start(mine, items_ref.at[patch, whole], at(1, 0), col)
    down = sends.start(mine, items_ref.at[patch, whole], at(3, 0), col)
    yield
    across = {0: [sends.start(mine, items_ref.at[patch, whole], at(0, by), col) for by in (1, 3)]}
    yield
    up.wait_recv()
    onward = [relay(at(3, 0), parts[0], at(1, 0))]
    across[3] = [relay(at(3, 0), whole, at(0, by)) for by in (1, 3)]
    yield
    down.wait_recv()
    onward.append(relay(at(1, 0), parts[1], at(3, 0)))
    across[1] = [relay(at(1, 0), whole, at(0, by)) for by in (1, 3)]
    yield
    for copy in onward:
        copy.wait_recv()
    across[2] = [relay(at(2, 0), whole, at(0, by)) for by in (1, 3)]
    last = []
    for i in (0, 3, 1, 2):
        yield
        across[i][0].wait_recv()
        last.append(relay(at(i, 3), parts[0], at(0, 1)))
        across[i][1].wait_recv()
        last.append(relay(at(i, 1), parts[1], at(0, 3)))
    yield
    for copy in last:
        copy.wait_recv()
    yield


def interleave(*steps):
    running = list(steps)
    while running:
        running = [one for one in running if next(one, "end") != "end"]


def spread_kernel(
    drawn_ref,
    panel_ref,
    *refs,
):
    stored, (rows_ref, cols_ref), held, rest = refs[:5], refs[5:7], refs[7:12], refs[12:]
    turned_ref, own_ref, fill, ssem, rsem, lsem = rest
    patch, col = lax.axis_index("patch"), lax.axis_index("col")
    y, z = patch // RING, lax.rem(patch, RING)
    loads = [pltpu.make_async_copy(a, b, lsem.at[2 + n]) for n, (a, b) in enumerate(zip(stored, held))]
    loads.append(pltpu.make_async_copy(drawn_ref, fill, lsem.at[7]))
    for copy in loads:
        copy.start()
    meet(
        [(patch, turn(col, by, K)) for by in range(1, K)]
        + [(turn(y, by) * RING + z, col) for by in (1, 3)]
        + [(y * RING + turn(z, by), col) for by in (1, 3)]
    )
    sends = Sends(ssem, rsem)
    local = pltpu.make_async_copy(panel_ref.at[col], turned_ref.at[col], lsem.at[0])
    local.start()
    first = [
        sends.start(panel_ref.at[turn(col, by, K)], turned_ref.at[col], patch, turn(col, by, K)) for by in range(1, K)
    ]
    local.wait()
    for copy in first:
        copy.wait_recv()
    for copy in loads:
        copy.wait()
    solve_row(patch * K + col, fill, turned_ref, *held, own_ref)
    local = [
        pltpu.make_async_copy(own_ref, rows_ref.at[col], lsem.at[0]),
        pltpu.make_async_copy(own_ref, cols_ref.at[patch], lsem.at[1]),
    ]
    for copy in local:
        copy.start()
    interleave(
        patch_ring(sends, own_ref, cols_ref, patch, col, False),
        patch_ring(sends, own_ref, cols_ref, patch, col, True),
        col_ring(sends, own_ref, rows_ref, patch, col),
    )
    sends.finish()
    for copy in local:
        copy.wait()


def spread(fill, matrix, factor, npatch, ncol):
    width = matrix.shape[2]
    block = (width, width)
    wide = K * width
    copies = 48 + K - 1
    return pl.pallas_call(
        spread_kernel,
        grid=(1,),
        in_specs=[HBM, pl.BlockSpec((K,) + block, lambda g: (0, 0, 0))]
        + [pl.BlockSpec(memory_space=pl.ANY)] * 5,
        out_specs=[pl.BlockSpec(memory_space=pl.ANY)] * 2,
        out_shape=[
            jax.ShapeDtypeStruct((ncol, width, wide), F32),
            jax.ShapeDtypeStruct((npatch, width, wide), F32),
        ],
        scratch_shapes=[pltpu.VMEM(part.shape, part.dtype) for part in factor]
        + [
            pltpu.VMEM((K,) + block, F32),
            pltpu.VMEM((width, wide), F32),
            pltpu.SMEM(fill.shape, jnp.int32),
            pltpu.SemaphoreType.DMA((copies,)),
            pltpu.SemaphoreType.DMA((copies,)),
            pltpu.SemaphoreType.DMA((8,)),
        ],
        compiler_params=params(10, collective_id=1, has_side_effects=True),
        name="spread",
    )(fill, matrix, *factor)


def offsets():
    left = [o for o in itertools.product(range(RING), range(RING), range(RING), range(2)) if any(o)]
    random.Random(3).shuffle(left)

    def links(o):
        return [float(v in (2, want)) for v in o[:3] for want in (1, 3)]

    def hops(o):
        return sum(min(v, RING - v) for v in o[:2])

    order = []
    for group in ([o for o in left if hops(o) <= 1], [o for o in left if hops(o) > 1]):
        load = [0.0] * 6
        while group:
            best = min(group, key=lambda o: max(map(sum, zip(load, links(o)))) - min(map(sum, zip(load, links(o)))))
            group.remove(best)
            order.append(best)
            load = [sum(pair) for pair in zip(load, links(best))]
    return order


batches = (30, 20)


def head_cols(sends, head_ref, patch, col, rest):
    x, core = col // 2, lax.rem(col, 2)
    first = sends.used
    sends.used += 7 * RING

    def copy(by, j, chip, hand, to, across):
        ref = head_ref.at[chip * 2 + hand, pl.ds(2 * j, 2)]
        return sends.plan(first + ((3 + by) if across else (by - 1)) * RING + j, ref, ref, patch, to)

    def out(by, j):
        return copy(by, j, x, core, turn(x, by) * 2 + core, False)

    def side(by, j, hand):
        return copy(by, j, turn(x, RING - by), hand, x * 2 + 1 - core, True)

    def each(by, act):
        for j in range(RING):
            pl.when(j >= turn(x, RING - by))(functools.partial(act, j))

    for by in (1, 3, 2):
        each(0, lambda j: out(by, j).start())
    each(0, lambda j: side(0, j, core).start())
    rest()
    for by in (1, 3, 2):
        def pass_on(j, by=by):
            copy(by, j, turn(x, RING - by), core, turn(x, by) * 2 + core, False).wait_recv()
            side(by, j, core).start()

        each(by, pass_on)
    for by in range(RING):
        each(by, lambda j: side(by, j, 1 - core).wait_recv())

    def finish():
        for by in (1, 3, 2):
            each(0, lambda j: out(by, j).wait_send())
        for by in range(RING):
            each(by, lambda j: side(by, j, core).wait_send())

    return finish


def exchange_kernel(
    npatch,
    slots,
    turns,
    fill,
    given_ref,
    code_ref,
    reg_ref,
    all_ref,
    mine_codes_ref,
    *refs,
):
    stored, held, rest = refs[:5], refs[5:10], refs[10:]
    exchange_steps(
        npatch, slots, turns, fill, given_ref, code_ref, reg_ref, all_ref, mine_codes_ref, stored, held, *rest
    )


def exchange_steps(
    npatch,
    slots,
    turns,
    drawn_ref,
    given_ref,
    code_ref,
    reg_ref,
    all_ref,
    mine_codes_ref,
    stored,
    held,
    codes_ref,
    fill,
    x_ref,
    lh_ref,
    li_ref,
    out_ref,
    mine_ref,
    tile_ref,
    row_ref,
    dense_ref,
    part_ref,
    piece_ref,
    head_ref,
    w_ref,
    lt_ref,
    ssem,
    rsem,
    bulk,
    lsem,
):
    patch, col = lax.axis_index("patch"), lax.axis_index("col")
    y, z, x, core = patch // RING, lax.rem(patch, RING), col // 2, lax.rem(col, 2)
    me = patch * K + col
    width = x_ref.shape[2]
    ndevice = npatch * K
    load = pltpu.make_async_copy(given_ref, x_ref, lsem.at[3])
    load.start()
    draw = pltpu.make_async_copy(drawn_ref, fill, lsem.at[9])
    draw.start()

    sign = 1 + 2 * core
    peers = []
    for dy, dz, dx, dc in offsets():
        to_patch = lax.rem(y + dy * sign, RING) * RING + lax.rem(z + dz * sign, RING)
        to_col = lax.rem(x + dx * sign, RING) * 2 + lax.rem(core + dc, 2)
        peers.append((to_patch, to_col))
    barrier = pltpu.get_barrier_semaphore()
    for to_patch, to_col in peers:
        pl.semaphore_signal(
            barrier, inc=1, device_id={"patch": to_patch, "col": to_col}, device_id_type=pl.DeviceIdType.MESH
        )

    def pack(d, carry):
        block = x_ref[jnp.maximum(slots[d], 0)]
        out_ref[d] = jnp.where(turns[d] > 0, block.T, block)
        return carry

    load.wait()
    lax.fori_loop(0, K, pack, 0)
    row_ref[...] = jnp.broadcast_to(code_ref[...], (8, width))
    pl.semaphore_wait(barrier, len(peers))

    sends = Sends(ssem, rsem)

    def flow(count):
        for to_patch, to_col in peers[flow.done : flow.done + count]:
            pltpu.make_async_remote_copy(
                src_ref=out_ref.at[to_patch * K + to_col],
                dst_ref=all_ref.at[me],
                send_sem=bulk.at[0],
                recv_sem=bulk.at[1],
                device_id={"patch": to_patch, "col": to_col},
                device_id_type=pl.DeviceIdType.MESH,
            ).start()
        flow.done += count

    flow.done = 0

    local = [
        pltpu.make_async_copy(out_ref.at[col], mine_ref.at[col], lsem.at[0]),
        pltpu.make_async_copy(row_ref, tile_ref.at[col], lsem.at[1]),
    ]
    for copy in local:
        copy.start()
    first = []
    for by in range(1, K):
        to = turn(col, by, K)
        first.append(sends.start(row_ref, tile_ref.at[col], patch, to))
        first.append(sends.start(out_ref.at[to], mine_ref.at[col], patch, to))
    lax.fori_loop(K, ndevice, pack, 0)
    own = pltpu.make_async_copy(out_ref.at[me], all_ref.at[me], lsem.at[2])
    own.start()
    for copy in local:
        copy.wait()
    for copy in first:
        copy.wait_recv()
    reg = jnp.broadcast_to(reg_ref[...], (8, width))
    sub = lax.broadcasted_iota(jnp.int32, (8, width), 0)
    lane = lax.broadcasted_iota(jnp.int32, (8, width), 1)
    codes = []
    tile = jnp.zeros((8, width), F32)
    for c in range(K):
        row = tile_ref[c]
        tile = jnp.where(sub == c, row, tile)
        codes.append(jnp.broadcast_to(jnp.sum(jnp.where(lane == col, row, 0.0), 1, keepdims=True), (8, width)))
    for r in range(K):
        hits = [code == r for code in codes]
        shift = jnp.where((patch == 0) & (col == r), reg, 0.0)
        for q in range(npatch):
            total = jnp.where(lane == sub + q * 8, shift, 0.0)
            for c in range(K):
                total = total + jnp.where(hits[c], mine_ref[c, q * 8 : (q + 1) * 8, :], 0.0)
            dense_ref[q, r] = total
    here = pl.ds(pl.multiple_of(patch * 8, 8), 8)
    codes_ref[here, :] = tile
    second = []
    tables = []
    for by in range(1, npatch):
        to = turn(patch, by, npatch)
        second.append(sends.start(dense_ref.at[to], part_ref.at[by - 1], to, col))
    for by in range(1, npatch):
        tables.append(sends.start(codes_ref.at[here, :], codes_ref.at[here, :], turn(patch, by, npatch), col))
    flow(batches[0])
    total = dense_ref[patch]
    for by, copy in enumerate(second):
        copy.wait_recv()
        total = total + part_ref[by]
    piece_ref[...] = total
    local = pltpu.make_async_copy(piece_ref, head_ref.at[col, :, here, :], lsem.at[0])
    local.start()
    third = [
        sends.start(piece_ref, head_ref.at[col, :, here, :], turn(patch, by, npatch), col) for by in range(1, npatch)
    ]
    flow(batches[1])
    local.wait()
    for copy in third:
        copy.wait_recv()
    finish = head_cols(sends, head_ref, patch, col, lambda: flow(len(peers) - flow.done))

    draw.wait()
    factor_head(fill, head_ref, lh_ref, li_ref, w_ref, lt_ref)
    hand_on(lh_ref, li_ref, *held)
    stores = [pltpu.make_async_copy(b, a, lsem.at[4 + n]) for n, (a, b) in enumerate(zip(stored, held))]
    for copy in stores:
        copy.start()

    finish()
    sends.finish()
    for copy in tables:
        copy.wait_recv()
    lt_ref[...] = codes_ref[...].T
    mine_codes_ref[...] = lt_ref[pl.ds(me, 1), :].astype(jnp.int32)
    own.wait()
    for copy in stores:
        copy.wait()
    every = pl.ds(0, ndevice - 1)
    whole = pltpu.make_async_remote_copy(
        src_ref=out_ref.at[every],
        dst_ref=all_ref.at[every],
        send_sem=bulk.at[0],
        recv_sem=bulk.at[1],
        device_id={"patch": peers[0][0], "col": peers[0][1]},
        device_id_type=pl.DeviceIdType.MESH,
    )
    whole.wait_send()
    whole.wait_recv()


def exchange(slots, turns, codes, fill, contributions, reg, npatch):
    width = contributions.shape[2]
    ndevice = npatch * K
    copies = 2 * (K - 1) + 3 * (npatch - 1) + 7 * RING
    wide, one = (K, width, K * width), (K, width, width)
    factor = ((wide, BF16), (wide, BF16), (one, BF16), (one, BF16), (one, F32))
    rows = width // npatch
    block = (width, width)
    return pl.pallas_call(
        functools.partial(exchange_kernel, npatch),
        in_specs=[SMEM, SMEM, HBM, HBM, WHOLE, WHOLE],
        out_specs=[ANY, WHOLE] + [ANY] * 5,
        out_shape=[
            jax.ShapeDtypeStruct((ndevice,) + block, F32),
            jax.ShapeDtypeStruct((1, ndevice), jnp.int32),
            *(jax.ShapeDtypeStruct(shape, kind) for shape, kind in factor),
        ],
        scratch_shapes=[
            *(pltpu.VMEM(shape, kind) for shape, kind in factor),
            pltpu.VMEM((ndevice, ndevice), F32),
            pltpu.SMEM(fill.shape, jnp.int32),
            pltpu.VMEM(contributions.shape, F32),
            pltpu.VMEM((K, K * width, width), F32),
            pltpu.VMEM((K,) + block, F32),
            pltpu.VMEM((ndevice,) + block, F32),
            pltpu.VMEM((K,) + block, F32),
            pltpu.VMEM((K, 8, width), F32),
            pltpu.VMEM((8, width), F32),
            pltpu.VMEM((npatch, K, rows, width), F32),
            pltpu.VMEM((npatch - 1, K, rows, width), F32),
            pltpu.VMEM((K, rows, width), F32),
            pltpu.VMEM((K, K) + block, F32),
            pltpu.VMEM((width, 2 * width), F32),
            pltpu.VMEM(block, F32),
            pltpu.SemaphoreType.DMA((copies,)),
            pltpu.SemaphoreType.DMA((copies,)),
            pltpu.SemaphoreType.DMA((2,)),
            pltpu.SemaphoreType.DMA((10,)),
        ],
        compiler_params=params(46, collective_id=0, has_side_effects=True),
        name="exchange",
    )(slots, turns, fill, contributions, codes, reg)


def route(targets, counts, pivot, rowblk, ncol, ndevice):
    slots = targets.shape[0]
    blocks = jnp.arange(pivot.shape[0], dtype=jnp.int32)
    position = jnp.sum(jnp.where(targets[:, :, None] == blocks, pivot, 0), 2)
    pos_first, pos_second = position[:, 0], position[:, 1]
    upper_pos = jnp.maximum(pos_first, pos_second)
    lower_pos = jnp.minimum(pos_first, pos_second)
    number = jnp.arange(slots, dtype=jnp.int32)
    live = number < counts[0]
    owner = upper_pos // rowblk * ncol + lower_pos % ncol
    select = (owner[:, None] == jnp.arange(ndevice, dtype=jnp.int32)[None, :]) & live[:, None]
    turned = (pos_first < pos_second).astype(jnp.int32)
    code = lower_pos // ncol * rowblk + upper_pos % rowblk

    def pick(value):
        return jnp.max(jnp.where(select, value[:, None], -1), 0)

    return pick(number), pick(turned), pick(code).astype(F32)[None, :]


def body(contributions, targets, counts, pivot, fill_draw, regular):
    width = contributions.shape[1]
    npatch = lax.axis_size("patch")
    ncol = lax.axis_size("col")
    ndevice = npatch * ncol
    nblock = pivot.shape[0]
    rowblk = regular.shape[0] // width
    colslots = nblock // ncol
    patch_id = lax.axis_index("patch")
    col_id = lax.axis_index("col")

    still = pltpu.with_memory_space_constraint(fill_draw, pltpu.HBM)
    slots, turns, codes = route(targets, counts, pivot, rowblk, ncol, ndevice)
    reg = lax.dynamic_slice_in_dim(regular, col_id * width, width, 0)[None, :]
    got, places, *factor = exchange(slots, turns, codes, still, contributions, reg, npatch)

    diag = (patch_id * rowblk + col_id).astype(jnp.int32)[None]
    matrix = place(places, diag, got, reg)

    rows_l, cols_l = spread(still, matrix, factor, npatch, ncol)
    rows_l = rows_l.reshape(rowblk * width, K * width)

    schur, panels = trailing(fill_draw, matrix.reshape(colslots, rowblk * width, width), rows_l, cols_l)
    return (panels, schur.reshape(colslots, 1, rowblk * width, width))


def solution(mesh):
    in_specs = (
        P(("patch", "col"), None, None),
        P(("patch", "col"), None),
        P(("patch", "col")),
        P(),
        P(),
        P("patch"),
    )
    out_specs = (P("patch", None), P(None, "col", "patch", None))
    return jax.shard_map(body, mesh=mesh, in_specs=in_specs, out_specs=out_specs, check_vma=False)
```

```python
import functools
import itertools
import random

import jax
import jax.numpy as jnp
from jax import lax
from jax.experimental import pallas as pl
from jax.experimental.pallas import tpu as pltpu
from jax.sharding import PartitionSpec as P

K = 8
HIGH = lax.Precision.HIGHEST
F32 = jnp.float32
BF16 = jnp.bfloat16
MIB = 1024 * 1024
SMEM = pl.BlockSpec(memory_space=pltpu.SMEM)
WHOLE = pl.BlockSpec(memory_space=pltpu.VMEM)
ANY = pl.BlockSpec(memory_space=pl.ANY)
HBM = pl.BlockSpec(memory_space=pltpu.HBM)
NT = (((1,), (1,)), ((), ()))
TN = (((0,), (0,)), ((), ()))


def params(size, **more):
    return pltpu.CompilerParams(vmem_limit_bytes=size * MIB, **more)


def dot_nt(a, b):
    return lax.dot_general(a, b, NT, precision=HIGH, preferred_element_type=F32)


def eye_mask(n):
    return lax.broadcasted_iota(jnp.int32, (n, n), 0) == lax.broadcasted_iota(jnp.int32, (n, n), 1)


def weight(drawn, i, j):
    return jnp.where(i == j, 1, jnp.maximum(drawn[i, j], drawn[j, i])).astype(F32)


def place_kernel(per, last, codes, diag, x_ref, reg_ref, o_ref):
    g = pl.program_id(0)
    width = x_ref.shape[2]

    @pl.when(g == 0)
    def _():
        def clear(q, carry):
            o_ref[q] = jnp.zeros((width, width), F32)
            return carry

        lax.fori_loop(0, o_ref.shape[0], clear, 0)

    def step(t, carry):
        code = codes[0, g * per + t]

        @pl.when(code >= 0)
        def _():
            o_ref[code] += x_ref[t]

        return carry

    lax.fori_loop(0, per, step, 0)

    @pl.when(g == last)
    def _():
        block = o_ref[diag[0]]
        o_ref[diag[0]] = 0.5 * (block + block.T) + jnp.where(eye_mask(width), reg_ref[...], 0.0)


def place(codes, diag, got, reg, per=16):
    ndevice, _, width = got.shape
    places = 128
    return pl.pallas_call(
        functools.partial(place_kernel, per, ndevice // per - 1),
        grid=(ndevice // per,),
        in_specs=[SMEM, SMEM, pl.BlockSpec((per, width, width), lambda g: (g, 0, 0)), pl.BlockSpec((1, width), lambda g: (0, 0))],
        out_specs=pl.BlockSpec((places, width, width), lambda g: (0, 0, 0), pipeline_mode=pl.Buffered(1)),
        out_shape=jax.ShapeDtypeStruct((places, width, width), F32),
        compiler_params=params(43),
        name="place",
    )(codes, diag, got, reg)


def split3(a):
    one = a.astype(BF16).astype(F32)
    rest = a - one
    two = rest.astype(BF16).astype(F32)
    return one, two, rest - two


def chol_inverse(w_ref, lt_ref):
    width = w_ref.shape[0]
    sub = lax.broadcasted_iota(jnp.int32, (8, width), 0)
    lane = lax.broadcasted_iota(jnp.int32, (8, width), 1)
    for base in range(0, width, 8):
        both = w_ref[base : base + 8, :]
        rows = both[:, :width]
        unit = both[:, width:]
        cols = [jnp.broadcast_to(rows[:, base + j : base + j + 1], (8, width)) for j in range(8)]
        scale = jnp.zeros((8, width), F32)
        for j in range(8):
            root = lax.rsqrt(cols[j][j : j + 1, :])
            lower = cols[j] * root
            for i in range(j + 1, 8):
                cols[i] = cols[i] - lower * lower[i : i + 1, :]
            below = jnp.where(sub > j, lower, 0.0)
            rows = rows - below * (rows[j : j + 1, :] * root)
            unit = unit - below * (unit[j : j + 1, :] * root)
            scale = jnp.where(sub == j, root, scale)
        upper = jnp.where(lane >= sub + base, rows * scale, 0.0)
        unit = unit * scale
        lt_ref[base : base + 8, :] = upper
        w_ref[base : base + 8, width:] = unit
        if base + 8 < width:
            u1, u2, u3 = split3(upper)
            v1, v2, v3 = split3(unit)
            left = jnp.concatenate([u1, u1, u2, u2, u1, u3], 0).astype(BF16)
            w1, w2, w3 = (jnp.concatenate([a, b], 1) for a, b in ((u1, v1), (u2, v2), (u3, v3)))
            right = jnp.concatenate([w1, w2, w1, w2, w3, w1], 0).astype(BF16)
            change = lax.dot_general(left, right, TN, preferred_element_type=F32)
            w_ref[base + 8 :, :] -= change[base + 8 :, :]


def factor_head(fill, head_ref, lh_ref, li_ref, w_ref, lt_ref):
    width = head_ref.shape[2]
    eye = jnp.where(eye_mask(width), 1.0, 0.0).astype(F32)
    for c in range(K):
        for r in range(K):
            at = slice(r * width, (r + 1) * width)
            if r < c:
                lh_ref[c, at, :] = jnp.zeros((width, width), F32)
                continue
            block = head_ref[c, r]
            lh_ref[c, at, :] = 0.5 * (block + block.T) if r == c else block

    def step(k, carry):
        w_ref[:, :width] = lh_ref[k, pl.ds(pl.multiple_of(k * width, width), width), :]
        w_ref[:, width:] = eye
        chol_inverse(w_ref, lt_ref)
        li_ref[k] = w_ref[:, width:]
        lh_ref[k, pl.ds(pl.multiple_of(k * width, width), width), :] = lt_ref[...].T
        for s in range(K - 1):

            @pl.when(k == s)
            def _(s=s):
                below = slice((s + 1) * width, K * width)
                solved = dot_nt(lh_ref[s, below, :], li_ref[s])
                lh_ref[s, below, :] = solved
                for j in range(s + 1, K):
                    part = solved[(j - s - 1) * width :]
                    change = dot_nt(part, part[:width])
                    for i in range(j, K):
                        at = slice(i * width, (i + 1) * width)
                        lh_ref[j, at, :] -= weight(fill, i, j) * change[(i - j) * width : (i - j + 1) * width]

        return carry

    lax.fori_loop(0, K, step, 0)


def split2(a):
    hi = a.astype(BF16)
    return hi, (a - hi.astype(F32)).astype(BF16)


def hand_on(lh_ref, li_ref, uh_ref, ul_ref, ih_ref, il_ref, diag_ref):
    width = lh_ref.shape[2]

    def column(k, carry):
        diag_ref[k] = lh_ref[k, pl.ds(pl.multiple_of(k * width, width), width), :]
        ih_ref[k], il_ref[k] = split2(li_ref[k].T)

        def row(i, carry):
            at = pl.ds(pl.multiple_of(i * width, width), width)
            uh_ref[k, :, at], ul_ref[k, :, at] = split2(lh_ref[k, at, :].T)
            return carry

        return lax.fori_loop(k + 1, K, row, carry)

    lax.fori_loop(0, K, column, 0)


def dot3(a, b_hi, b_lo):
    a_hi, a_lo = split2(a)
    product = jnp.dot(a_hi, b_hi, preferred_element_type=F32)
    product += jnp.dot(a_lo, b_hi, preferred_element_type=F32)
    return product + jnp.dot(a_hi, b_lo, preferred_element_type=F32)


def solve_row(row, fill, a_ref, uh_ref, ul_ref, ih_ref, il_ref, diag_ref, o_ref):
    width = a_ref.shape[1]
    work = [a_ref[k] for k in range(K)]
    for k in range(K):
        solved = dot3(work[k], ih_ref[k], il_ref[k])
        solved = jnp.where(row > k, solved, jnp.where(row == k, diag_ref[k], 0.0))
        o_ref[:, k * width : (k + 1) * width] = solved
        if k + 1 < K:
            change = dot3(solved, uh_ref[k, :, (k + 1) * width :], ul_ref[k, :, (k + 1) * width :])
            for j in range(k + 1, K):
                work[j] = work[j] - weight(fill, row, j) * change[:, (j - k - 1) * width : (j - k) * width]


def schur_kernel(pair, chunk, fill, a_ref, rows_ref, cols_ref, o_ref, panels_ref, hi_ref, lo_ref, sem):
    g = pl.program_id(0)
    width = a_ref.shape[2]
    nrow = a_ref.shape[1] // width
    grow = lax.axis_index("patch") * nrow
    gcol = [(g * pair + q) * K + lax.axis_index("col") for q in range(pair)]

    @pl.when(g == 0)
    def _():
        pltpu.make_async_copy(rows_ref, panels_ref, sem).start()

        def split(r, carry):
            at = pl.ds(pl.multiple_of(r * width, width), width)
            rows = rows_ref[at, :]
            hi = rows.astype(BF16)
            hi_ref[at, :] = hi
            lo_ref[at, :] = (rows - hi.astype(F32)).astype(BF16)
            return carry

        lax.fori_loop(0, nrow, split, 0)

    cols = cols_ref[...].reshape(pair * width, cols_ref.shape[2])
    col_hi = cols.astype(BF16)
    col_lo = (cols - col_hi.astype(F32)).astype(BF16)

    some = (grow + nrow > gcol[0]) & (gcol[pair - 1] >= K)

    @pl.when(some)
    def _():
        def step(m, carry):
            at = pl.ds(pl.multiple_of(m * chunk * width, chunk * width), chunk * width)
            hi = hi_ref[at, :]
            product = lax.dot_general(hi, col_hi, NT, preferred_element_type=F32)
            product += lax.dot_general(hi, col_lo, NT, preferred_element_type=F32)
            product += lax.dot_general(lo_ref[at, :], col_hi, NT, preferred_element_type=F32)
            for i in range(chunk):
                r = m * chunk + i
                here = pl.ds(pl.multiple_of(r * width, width), width)
                for q in range(pair):
                    part = product[i * width : (i + 1) * width, q * width : (q + 1) * width]
                    value = a_ref[q, here, :] - weight(fill, grow + r, gcol[q]) * part
                    o_ref[q, here, :] = jnp.where((grow + r >= gcol[q]) & (gcol[q] >= K), value, 0.0)
            return carry

        lax.fori_loop(0, nrow // chunk, step, 0)

    @pl.when(jnp.logical_not(some))
    def _():
        o_ref[...] = jnp.zeros(o_ref.shape, F32)

    @pl.when(g == pl.num_programs(0) - 1)
    def _():
        pltpu.make_async_copy(rows_ref, panels_ref, sem).wait()


def trailing(fill, matrix, rows_l, cols_l, pair=2, chunk=8):
    colslots, tall, width = matrix.shape
    depth = rows_l.shape[1]
    return pl.pallas_call(
        functools.partial(schur_kernel, pair, chunk),
        grid=(colslots // pair,),
        in_specs=[
            SMEM,
            pl.BlockSpec((pair, tall, width), lambda g: (g, 0, 0)),
            pl.BlockSpec((tall, depth), lambda g: (0, 0), pipeline_mode=pl.Buffered(1)),
            pl.BlockSpec((pair, width, depth), lambda g: (g, 0, 0)),
        ],
        out_specs=[pl.BlockSpec((pair, tall, width), lambda g: (g, 0, 0)), pl.BlockSpec(memory_space=pl.ANY)],
        out_shape=[
            jax.ShapeDtypeStruct((colslots, tall, width), F32),
            jax.ShapeDtypeStruct((tall, depth), F32),
        ],
        scratch_shapes=[pltpu.VMEM((tall, depth), BF16), pltpu.VMEM((tall, depth), BF16), pltpu.SemaphoreType.DMA],
        compiler_params=params(22),
        name="trailing",
    )(fill, matrix, rows_l, cols_l)


RING = 4


def turn(value, by, size=RING):
    return lax.rem(value + (by + size), size)


class Sends:
    def __init__(self, ssem, rsem):
        self.ssem, self.rsem, self.all = ssem, rsem, []

        self.used = 0

    def plan(self, n, src, dst, patch, col):
        return pltpu.make_async_remote_copy(
            src_ref=src,
            dst_ref=dst,
            send_sem=self.ssem.at[n],
            recv_sem=self.rsem.at[n],
            device_id={"patch": patch, "col": col},
            device_id_type=pl.DeviceIdType.MESH,
        )

    def start(self, src, dst, patch, col):
        copy = self.plan(self.used, src, dst, patch, col)
        self.used += 1
        copy.start()
        self.all.append(copy)
        return copy

    def finish(self):
        for copy in self.all:
            copy.wait_send()


def meet(peers):
    barrier = pltpu.get_barrier_semaphore()
    for patch, col in peers:
        pl.semaphore_signal(
            barrier, inc=1, device_id={"patch": patch, "col": col}, device_id_type=pl.DeviceIdType.MESH
        )
    pl.semaphore_wait(barrier, len(peers))


def col_ring(sends, src, items_ref, patch, col):
    x, core = col // 2, lax.rem(col, 2)
    there = [turn(x, by) * 2 + core for by in range(RING)]
    other = x * 2 + (1 - core)
    half = items_ref.shape[1] // 2
    up = sends.start(src, items_ref.at[col], patch, there[1])
    down = sends.start(src, items_ref.at[col], patch, there[3])
    side = [sends.start(src, items_ref.at[col], patch, other)]
    yield
    up.wait_recv()
    from_down = items_ref.at[there[3]]
    onward = [sends.start(from_down.at[pl.ds(0, half)], from_down.at[pl.ds(0, half)], patch, there[1])]
    side.append(sends.start(from_down, from_down, patch, other))
    down.wait_recv()
    from_up = items_ref.at[there[1]]
    onward.append(sends.start(from_up.at[pl.ds(half, half)], from_up.at[pl.ds(half, half)], patch, there[3]))
    side.append(sends.start(from_up, from_up, patch, other))
    yield
    for copy in onward:
        copy.wait_recv()
    far = items_ref.at[there[2]]
    side.append(sends.start(far, far, patch, other))
    yield
    for copy in side:
        copy.wait_recv()
    yield


def patch_ring(sends, src, items_ref, patch, col, swap):
    y, z = patch // RING, lax.rem(patch, RING)

    def at(first, second):
        i, j = (first, second) if swap else (second, first)
        return turn(y, i) * RING + turn(z, j)

    size = items_ref.shape[1] // 2
    start = size if swap else 0
    whole = pl.ds(start, size)
    parts = (pl.ds(start, size // 2), pl.ds(start + size // 2, size // 2))

    def relay(item, rows, target):
        return sends.start(items_ref.at[item, rows], items_ref.at[item, rows], target, col)

    mine = src.at[whole]
    up = sends.start(mine, items_ref.at[patch, whole], at(1, 0), col)
    down = sends.start(mine, items_ref.at[patch, whole], at(3, 0), col)
    yield
    across = {0: [sends.start(mine, items_ref.at[patch, whole], at(0, by), col) for by in (1, 3)]}
    yield
    up.wait_recv()
    onward = [relay(at(3, 0), parts[0], at(1, 0))]
    across[3] = [relay(at(3, 0), whole, at(0, by)) for by in (1, 3)]
    yield
    down.wait_recv()
    onward.append(relay(at(1, 0), parts[1], at(3, 0)))
    across[1] = [relay(at(1, 0), whole, at(0, by)) for by in (1, 3)]
    yield
    for copy in onward:
        copy.wait_recv()
    across[2] = [relay(at(2, 0), whole, at(0, by)) for by in (1, 3)]
    last = []
    for i in (0, 3, 1, 2):
        yield
        across[i][0].wait_recv()
        last.append(relay(at(i, 3), parts[0], at(0, 1)))
        across[i][1].wait_recv()
        last.append(relay(at(i, 1), parts[1], at(0, 3)))
    yield
    for copy in last:
        copy.wait_recv()
    yield


def interleave(*steps):
    running = list(steps)
    while running:
        running = [one for one in running if next(one, "end") != "end"]


def spread_kernel(
    drawn_ref,
    panel_ref,
    *refs,
):
    stored, (rows_ref, cols_ref), held, rest = refs[:5], refs[5:7], refs[7:12], refs[12:]
    turned_ref, own_ref, fill, ssem, rsem, lsem = rest
    patch, col = lax.axis_index("patch"), lax.axis_index("col")
    y, z = patch // RING, lax.rem(patch, RING)
    loads = [pltpu.make_async_copy(a, b, lsem.at[2 + n]) for n, (a, b) in enumerate(zip(stored, held))]
    loads.append(pltpu.make_async_copy(drawn_ref, fill, lsem.at[7]))
    for copy in loads:
        copy.start()
    meet(
        [(patch, turn(col, by, K)) for by in range(1, K)]
        + [(turn(y, by) * RING + z, col) for by in (1, 3)]
        + [(y * RING + turn(z, by), col) for by in (1, 3)]
    )
    sends = Sends(ssem, rsem)
    local = pltpu.make_async_copy(panel_ref.at[col], turned_ref.at[col], lsem.at[0])
    local.start()
    first = [
        sends.start(panel_ref.at[turn(col, by, K)], turned_ref.at[col], patch, turn(col, by, K)) for by in range(1, K)
    ]
    local.wait()
    for copy in first:
        copy.wait_recv()
    for copy in loads:
        copy.wait()
    solve_row(patch * K + col, fill, turned_ref, *held, own_ref)
    local = [
        pltpu.make_async_copy(own_ref, rows_ref.at[col], lsem.at[0]),
        pltpu.make_async_copy(own_ref, cols_ref.at[patch], lsem.at[1]),
    ]
    for copy in local:
        copy.start()
    interleave(
        patch_ring(sends, own_ref, cols_ref, patch, col, False),
        patch_ring(sends, own_ref, cols_ref, patch, col, True),
        col_ring(sends, own_ref, rows_ref, patch, col),
    )
    sends.finish()
    for copy in local:
        copy.wait()


def spread(fill, matrix, factor, npatch, ncol):
    width = matrix.shape[2]
    block = (width, width)
    wide = K * width
    copies = 48 + K - 1
    return pl.pallas_call(
        spread_kernel,
        grid=(1,),
        in_specs=[HBM, pl.BlockSpec((K,) + block, lambda g: (0, 0, 0))]
        + [pl.BlockSpec(memory_space=pl.ANY)] * 5,
        out_specs=[pl.BlockSpec(memory_space=pl.ANY)] * 2,
        out_shape=[
            jax.ShapeDtypeStruct((ncol, width, wide), F32),
            jax.ShapeDtypeStruct((npatch, width, wide), F32),
        ],
        scratch_shapes=[pltpu.VMEM(part.shape, part.dtype) for part in factor]
        + [
            pltpu.VMEM((K,) + block, F32),
            pltpu.VMEM((width, wide), F32),
            pltpu.SMEM(fill.shape, jnp.int32),
            pltpu.SemaphoreType.DMA((copies,)),
            pltpu.SemaphoreType.DMA((copies,)),
            pltpu.SemaphoreType.DMA((8,)),
        ],
        compiler_params=params(10, collective_id=1, has_side_effects=True),
        name="spread",
    )(fill, matrix, *factor)


def offsets():
    left = [o for o in itertools.product(range(RING), range(RING), range(RING), range(2)) if any(o)]
    random.Random(3).shuffle(left)

    def links(o):
        return [float(v in (2, want)) for v in o[:3] for want in (1, 3)]

    def hops(o):
        return sum(min(v, RING - v) for v in o[:2])

    order = []
    for group in ([o for o in left if hops(o) <= 1], [o for o in left if hops(o) > 1]):
        load = [0.0] * 6
        while group:
            best = min(group, key=lambda o: max(map(sum, zip(load, links(o)))) - min(map(sum, zip(load, links(o)))))
            group.remove(best)
            order.append(best)
            load = [sum(pair) for pair in zip(load, links(best))]
    return order


batches = (30, 20)


def head_cols(sends, head_ref, patch, col, rest):
    x, core = col // 2, lax.rem(col, 2)
    first = sends.used
    sends.used += 7 * RING

    def copy(by, j, chip, hand, to, across):
        ref = head_ref.at[chip * 2 + hand, pl.ds(2 * j, 2)]
        return sends.plan(first + ((3 + by) if across else (by - 1)) * RING + j, ref, ref, patch, to)

    def out(by, j):
        return copy(by, j, x, core, turn(x, by) * 2 + core, False)

    def side(by, j, hand):
        return copy(by, j, turn(x, RING - by), hand, x * 2 + 1 - core, True)

    def each(by, act):
        for j in range(RING):
            pl.when(j >= turn(x, RING - by))(functools.partial(act, j))

    for by in (1, 3, 2):
        each(0, lambda j: out(by, j).start())
    each(0, lambda j: side(0, j, core).start())
    rest()
    for by in (1, 3, 2):
        def pass_on(j, by=by):
            copy(by, j, turn(x, RING - by), core, turn(x, by) * 2 + core, False).wait_recv()
            side(by, j, core).start()

        each(by, pass_on)
    for by in range(RING):
        each(by, lambda j: side(by, j, 1 - core).wait_recv())

    def finish():
        for by in (1, 3, 2):
            each(0, lambda j: out(by, j).wait_send())
        for by in range(RING):
            each(by, lambda j: side(by, j, core).wait_send())

    return finish


def exchange_kernel(
    npatch,
    slots,
    turns,
    fill,
    given_ref,
    code_ref,
    reg_ref,
    all_ref,
    mine_codes_ref,
    *refs,
):
    stored, held, rest = refs[:5], refs[5:10], refs[10:]
    exchange_steps(
        npatch, slots, turns, fill, given_ref, code_ref, reg_ref, all_ref, mine_codes_ref, stored, held, *rest
    )


def exchange_steps(
    npatch,
    slots,
    turns,
    drawn_ref,
    given_ref,
    code_ref,
    reg_ref,
    all_ref,
    mine_codes_ref,
    stored,
    held,
    codes_ref,
    fill,
    x_ref,
    lh_ref,
    li_ref,
    out_ref,
    mine_ref,
    tile_ref,
    row_ref,
    dense_ref,
    part_ref,
    piece_ref,
    head_ref,
    w_ref,
    lt_ref,
    ssem,
    rsem,
    bulk,
    lsem,
):
    patch, col = lax.axis_index("patch"), lax.axis_index("col")
    y, z, x, core = patch // RING, lax.rem(patch, RING), col // 2, lax.rem(col, 2)
    me = patch * K + col
    width = x_ref.shape[2]
    ndevice = npatch * K
    load = pltpu.make_async_copy(given_ref, x_ref, lsem.at[3])
    load.start()
    draw = pltpu.make_async_copy(drawn_ref, fill, lsem.at[9])
    draw.start()

    sign = 1 + 2 * core
    peers = []
    for dy, dz, dx, dc in offsets():
        to_patch = lax.rem(y + dy * sign, RING) * RING + lax.rem(z + dz * sign, RING)
        to_col = lax.rem(x + dx * sign, RING) * 2 + lax.rem(core + dc, 2)
        peers.append((to_patch, to_col))
    barrier = pltpu.get_barrier_semaphore()
    for to_patch, to_col in peers:
        pl.semaphore_signal(
            barrier, inc=1, device_id={"patch": to_patch, "col": to_col}, device_id_type=pl.DeviceIdType.MESH
        )

    def pack(d, carry):
        block = x_ref[jnp.maximum(slots[d], 0)]
        out_ref[d] = jnp.where(turns[d] > 0, block.T, block)
        return carry

    load.wait()
    lax.fori_loop(0, K, pack, 0)
    row_ref[...] = jnp.broadcast_to(code_ref[...], (8, width))
    pl.semaphore_wait(barrier, len(peers))

    sends = Sends(ssem, rsem)

    def flow(count):
        for to_patch, to_col in peers[flow.done : flow.done + count]:
            pltpu.make_async_remote_copy(
                src_ref=out_ref.at[to_patch * K + to_col],
                dst_ref=all_ref.at[me],
                send_sem=bulk.at[0],
                recv_sem=bulk.at[1],
                device_id={"patch": to_patch, "col": to_col},
                device_id_type=pl.DeviceIdType.MESH,
            ).start()
        flow.done += count

    flow.done = 0

    local = [
        pltpu.make_async_copy(out_ref.at[col], mine_ref.at[col], lsem.at[0]),
        pltpu.make_async_copy(row_ref, tile_ref.at[col], lsem.at[1]),
    ]
    for copy in local:
        copy.start()
    first = []
    for by in range(1, K):
        to = turn(col, by, K)
        first.append(sends.start(row_ref, tile_ref.at[col], patch, to))
        first.append(sends.start(out_ref.at[to], mine_ref.at[col], patch, to))
    lax.fori_loop(K, ndevice, pack, 0)
    own = pltpu.make_async_copy(out_ref.at[me], all_ref.at[me], lsem.at[2])
    own.start()
    for copy in local:
        copy.wait()
    for copy in first:
        copy.wait_recv()
    reg = jnp.broadcast_to(reg_ref[...], (8, width))
    sub = lax.broadcasted_iota(jnp.int32, (8, width), 0)
    lane = lax.broadcasted_iota(jnp.int32, (8, width), 1)
    codes = []
    tile = jnp.zeros((8, width), F32)
    for c in range(K):
        row = tile_ref[c]
        tile = jnp.where(sub == c, row, tile)
        codes.append(jnp.broadcast_to(jnp.sum(jnp.where(lane == col, row, 0.0), 1, keepdims=True), (8, width)))
    for r in range(K):
        hits = [code == r for code in codes]
        shift = jnp.where((patch == 0) & (col == r), reg, 0.0)
        for q in range(npatch):
            total = jnp.where(lane == sub + q * 8, shift, 0.0)
            for c in range(K):
                total = total + jnp.where(hits[c], mine_ref[c, q * 8 : (q + 1) * 8, :], 0.0)
            dense_ref[q, r] = total
    here = pl.ds(pl.multiple_of(patch * 8, 8), 8)
    codes_ref[here, :] = tile
    second = []
    tables = []
    for by in range(1, npatch):
        to = turn(patch, by, npatch)
        second.append(sends.start(dense_ref.at[to], part_ref.at[by - 1], to, col))
    for by in range(1, npatch):
        tables.append(sends.start(codes_ref.at[here, :], codes_ref.at[here, :], turn(patch, by, npatch), col))
    flow(batches[0])
    total = dense_ref[patch]
    for by, copy in enumerate(second):
        copy.wait_recv()
        total = total + part_ref[by]
    piece_ref[...] = total
    local = pltpu.make_async_copy(piece_ref, head_ref.at[col, :, here, :], lsem.at[0])
    local.start()
    third = [
        sends.start(piece_ref, head_ref.at[col, :, here, :], turn(patch, by, npatch), col) for by in range(1, npatch)
    ]
    flow(batches[1])
    local.wait()
    for copy in third:
        copy.wait_recv()
    finish = head_cols(sends, head_ref, patch, col, lambda: flow(len(peers) - flow.done))

    draw.wait()
    factor_head(fill, head_ref, lh_ref, li_ref, w_ref, lt_ref)
    hand_on(lh_ref, li_ref, *held)
    stores = [pltpu.make_async_copy(b, a, lsem.at[4 + n]) for n, (a, b) in enumerate(zip(stored, held))]
    for copy in stores:
        copy.start()

    finish()
    sends.finish()
    for copy in tables:
        copy.wait_recv()
    lt_ref[...] = codes_ref[...].T
    mine_codes_ref[...] = lt_ref[pl.ds(me, 1), :].astype(jnp.int32)
    own.wait()
    for copy in stores:
        copy.wait()
    every = pl.ds(0, ndevice - 1)
    whole = pltpu.make_async_remote_copy(
        src_ref=out_ref.at[every],
        dst_ref=all_ref.at[every],
        send_sem=bulk.at[0],
        recv_sem=bulk.at[1],
        device_id={"patch": peers[0][0], "col": peers[0][1]},
        device_id_type=pl.DeviceIdType.MESH,
    )
    whole.wait_send()
    whole.wait_recv()


def exchange(slots, turns, codes, fill, contributions, reg, npatch):
    width = contributions.shape[2]
    ndevice = npatch * K
    copies = 2 * (K - 1) + 3 * (npatch - 1) + 7 * RING
    wide, one = (K, width, K * width), (K, width, width)
    factor = ((wide, BF16), (wide, BF16), (one, BF16), (one, BF16), (one, F32))
    rows = width // npatch
    block = (width, width)
    return pl.pallas_call(
        functools.partial(exchange_kernel, npatch),
        in_specs=[SMEM, SMEM, HBM, HBM, WHOLE, WHOLE],
        out_specs=[ANY, WHOLE] + [ANY] * 5,
        out_shape=[
            jax.ShapeDtypeStruct((ndevice,) + block, F32),
            jax.ShapeDtypeStruct((1, ndevice), jnp.int32),
            *(jax.ShapeDtypeStruct(shape, kind) for shape, kind in factor),
        ],
        scratch_shapes=[
            *(pltpu.VMEM(shape, kind) for shape, kind in factor),
            pltpu.VMEM((ndevice, ndevice), F32),
            pltpu.SMEM(fill.shape, jnp.int32),
            pltpu.VMEM(contributions.shape, F32),
            pltpu.VMEM((K, K * width, width), F32),
            pltpu.VMEM((K,) + block, F32),
            pltpu.VMEM((ndevice,) + block, F32),
            pltpu.VMEM((K,) + block, F32),
            pltpu.VMEM((K, 8, width), F32),
            pltpu.VMEM((8, width), F32),
            pltpu.VMEM((npatch, K, rows, width), F32),
            pltpu.VMEM((npatch - 1, K, rows, width), F32),
            pltpu.VMEM((K, rows, width), F32),
            pltpu.VMEM((K, K) + block, F32),
            pltpu.VMEM((width, 2 * width), F32),
            pltpu.VMEM(block, F32),
            pltpu.SemaphoreType.DMA((copies,)),
            pltpu.SemaphoreType.DMA((copies,)),
            pltpu.SemaphoreType.DMA((2,)),
            pltpu.SemaphoreType.DMA((10,)),
        ],
        compiler_params=params(46, collective_id=0, has_side_effects=True),
        name="exchange",
    )(slots, turns, fill, contributions, codes, reg)


def route(targets, counts, pivot, rowblk, ncol, ndevice):
    slots = targets.shape[0]
    blocks = jnp.arange(pivot.shape[0], dtype=jnp.int32)
    position = jnp.sum(jnp.where(targets[:, :, None] == blocks, pivot, 0), 2)
    pos_first, pos_second = position[:, 0], position[:, 1]
    upper_pos = jnp.maximum(pos_first, pos_second)
    lower_pos = jnp.minimum(pos_first, pos_second)
    number = jnp.arange(slots, dtype=jnp.int32)
    live = number < counts[0]
    owner = upper_pos // rowblk * ncol + lower_pos % ncol
    select = (owner[:, None] == jnp.arange(ndevice, dtype=jnp.int32)[None, :]) & live[:, None]
    turned = (pos_first < pos_second).astype(jnp.int32)
    code = lower_pos // ncol * rowblk + upper_pos % rowblk

    def pick(value):
        return jnp.max(jnp.where(select, value[:, None], -1), 0)

    return pick(number), pick(turned), pick(code).astype(F32)[None, :]


def body(contributions, targets, counts, pivot, fill_draw, regular):
    width = contributions.shape[1]
    npatch = lax.axis_size("patch")
    ncol = lax.axis_size("col")
    ndevice = npatch * ncol
    nblock = pivot.shape[0]
    rowblk = regular.shape[0] // width
    colslots = nblock // ncol
    patch_id = lax.axis_index("patch")
    col_id = lax.axis_index("col")

    still = pltpu.with_memory_space_constraint(fill_draw, pltpu.HBM)
    slots, turns, codes = route(targets, counts, pivot, rowblk, ncol, ndevice)
    reg = lax.dynamic_slice_in_dim(regular, col_id * width, width, 0)[None, :]
    got, places, *factor = exchange(slots, turns, codes, still, contributions, reg, npatch)

    diag = (patch_id * rowblk + col_id).astype(jnp.int32)[None]
    matrix = place(places, diag, got, reg)

    rows_l, cols_l = spread(still, matrix, factor, npatch, ncol)
    rows_l = rows_l.reshape(rowblk * width, K * width)

    schur, panels = trailing(fill_draw, matrix.reshape(colslots, rowblk * width, width), rows_l, cols_l)
    return (panels, schur.reshape(colslots, 1, rowblk * width, width))


def solution(mesh):
    in_specs = (
        P(("patch", "col"), None, None),
        P(("patch", "col"), None),
        P(("patch", "col")),
        P(),
        P(),
        P("patch"),
    )
    out_specs = (P("patch", None), P(None, "col", "patch", None))
    return jax.shard_map(body, mesh=mesh, in_specs=in_specs, out_specs=out_specs, check_vma=False)
```
